32 devices in a mesh: shard: 8 (over z, y), seq: 4 (over x, core).
Axes of the slice: x: 2, y: 2, z: 4, core: 2. Of those that a mesh axis runs over, the one named last changes fastest.
Arguments:
- tokens: bfloat16 [16384, 768], P(('shard', 'seq')), may hold values from -6 to 6
- segment_ids: int32 [8, 2048], P('shard'), may hold values from 0 to 15, never falling along the last dimension, each value on 1 to 1024 neighbouring positions
- qkv_weight: bfloat16 [768, 2304], P('shard'), may hold values from -0.21875 to 0.21875
- out_weight: bfloat16 [768, 768], P('shard'), may hold values from -1.25 to 1.25
- up_weight: bfloat16 [768, 3072], P('shard'), may hold values from -0.21875 to 0.21875
- down_weight: bfloat16 [3072, 768], P('shard'), may hold values from -0.109375 to 0.109375
- first_gain: bfloat16 [768], P('shard'), may hold values from 0.5 to 1.5
- first_bias: bfloat16 [768], P('shard'), may hold values from -3 to 3
- second_gain: bfloat16 [768], P('shard'), may hold values from 0.5 to 1.5
- second_bias: bfloat16 [768], P('shard'), may hold values from -3 to 3
- out_grad: bfloat16 [16384, 768], P(('shard', 'seq')), may hold values from -6 to 6
Outputs:
- layer_output: bfloat16 [16384, 768], P(('shard', 'seq'))
- input_grad: float32 [16384, 768], P(('shard', 'seq'))
- qkv_grad: float32 [768, 2304], P('shard')
- mixer_grad: float32 [768, 768], P('shard')
- widen_grad: float32 [768, 3072], P('shard')
- narrow_grad: float32 [3072, 768], P('shard')
- first_gain_grad: float32 [768], P('shard')
- first_bias_grad: float32 [768], P('shard')
- second_gain_grad: float32 [768], P('shard')
- second_bias_grad: float32 [768], P('shard')
The draws below stay inside these ranges and needn't reach their ends.
Inputs may be any that keep to these rules, and one draw needn't show every extreme that they name: `segment_ids`: in each row the ids never decrease; every document holds 1 to 1024 tokens and one holds exactly 1024.
All inputs are finite; a program needn't handle non-finite values.
Results may differ from the reference program's by a relative error of at most 0.02.
Values may be sent and summed in bfloat16 or wider, within the bound.
No kernel may reach another device: no remote copies, remote signals or barrier semaphores. Data moves between devices by JAX's collectives and lax.ppermute only.
A program may use at most 128 MiB of HBM per device.

```python
import math
from functools import partial
import jax
import jax.numpy as jnp
import numpy as np
from jax import lax

D = 768
FF = 3072
HEADS = 12
HEAD_DIM = 64
SEGS = 16
LEN = 2048
SEQS = 8
TOKENS = 16384


def levels(rng, dims, shards, low, high):
    gain = 1.0
    for position, blocks in shards:
        heights = jax.random.uniform(jax.random.fold_in(jax.random.fold_in(rng, 6), position), (blocks,), jnp.float32, low / len(shards), high / len(shards))
        gain = gain * jnp.repeat(jnp.exp(heights), dims[position] // blocks).reshape((-1,) + (1,) * (len(dims) - 1 - position))
    return gain


def profile(amount, total, reach, slope):
    loads = [(1 << 20) // math.isqrt(standing ** slope) + 1 for standing in range(2, amount + 1)]
    rest, holding = total - reach - (amount - 1), [1] * (amount - 1)
    while rest > 0:
        candidates = [i for i in range(amount - 1) if holding[i] < reach]
        whole, left = sum([loads[i] for i in candidates]), rest
        for i in candidates:
            more = min(reach - holding[i], max(1, left * loads[i] // whole), rest)
            holding[i] = holding[i] + more
            rest = rest - more
    return np.array([reach] + holding)


def uneven(key, count, total, most, slope):
    if count == 2:
        one = jax.random.randint(key, (), max(1, total - most), min(most, total - 1) + 1)
        return jnp.stack([one, total - one])
    tallies = jnp.asarray(profile(count, total, most, slope), jnp.int32)
    couples = (count - 1) // 2
    source_of, receiver = tallies[1:1 + 2 * couples:2], tallies[2:2 + 2 * couples:2]
    slack = jnp.minimum(source_of - 1, most - receiver)
    shifted = jax.random.randint(jax.random.fold_in(key, 1), (couples,), 0, 1 << 20) % (slack + 1)
    tallies = tallies.at[1:1 + 2 * couples:2].set(source_of - shifted).at[2:2 + 2 * couples:2].set(receiver + shifted)
    return tallies[jax.random.permutation(jax.random.fold_in(key, 2), count)]


def bell_draw(stream_key, shape, spread, limit, pieces=(), held_as=jnp.bfloat16):
    level = levels(stream_key, shape, pieces, -0.22, 0.18) if pieces else 1.0
    entries = jax.random.normal(stream_key, shape, jnp.float32) * spread * level
    return jnp.minimum(jnp.maximum(entries, -limit), limit).astype(held_as)


def setup_inputs(seed: int = 0) -> dict:
    streams_of = jax.random.split(jax.random.key(seed), 12)
    return {
        "tokens": bell_draw(streams_of[0], (TOKENS, D), 1.0, 6.0, ((0, 32),)),
        "segment_ids": jax.vmap(lambda own: jnp.searchsorted(jnp.cumsum(uneven(own, SEGS, LEN, LEN // 2, 3)), jnp.arange(LEN), side="right"))(jax.random.split(streams_of[1], SEQS)).reshape((SEQS, LEN)).astype(jnp.int32),
        "qkv_weight": bell_draw(streams_of[2], (D, 3 * D), D ** -0.5, 0.21875, ((0, 8),)),
        "out_weight": bell_draw(streams_of[3], (D, D), (D // 32) ** -0.5, 1.25, ((0, 8),)),
        "up_weight": bell_draw(streams_of[4], (D, FF), D ** -0.5, 0.21875, ((0, 8),)),
        "down_weight": bell_draw(streams_of[5], (FF, D), FF ** -0.5, 0.109375, ((0, 8),)),
        "first_gain": jnp.clip(1.0 + 0.1 * jax.random.normal(streams_of[6], (D,), jnp.float32), 0.5, 1.5).astype(jnp.bfloat16),
        "first_bias": bell_draw(streams_of[7], (D,), 0.5, 3.0, ((0, 8),)),
        "second_gain": jnp.clip(1.0 + 0.1 * jax.random.normal(streams_of[8], (D,), jnp.float32), 0.5, 1.5).astype(jnp.bfloat16),
        "second_bias": bell_draw(streams_of[9], (D,), 0.5, 3.0, ((0, 8),)),
        "out_grad": bell_draw(streams_of[10], (TOKENS, D), 1.0, 6.0, ((0, 32),)),
    }


@jax.custom_vjp
def low(v):
    return lax.optimization_barrier(v.astype(jnp.bfloat16)).astype(jnp.float32)

@jax.custom_vjp
def low_back(v):
    return v

def low_keep(v):
    return (low(v), None)

def low_pass(kept, grad):
    return (grad,)

def back_keep(v):
    return (v, None)

def back_low(kept, grad):
    return (low(grad),)
low.defvjp(low_keep, low_pass)
low_back.defvjp(back_keep, back_low)
EPSILON = 1e-12
MASKED = -1000000000.0

def product(left_mat, right_mat):
    return jnp.dot(left_mat, right_mat, precision=lax.Precision.HIGHEST, preferred_element_type=jnp.float32)

def layer_norm(hidden, gain_vec, shift_vec):
    row_mean = lax.optimization_barrier(jnp.mean(hidden, -1, keepdims=True))
    centred = hidden - row_mean
    variance = lax.optimization_barrier(jnp.mean(centred * centred, -1, keepdims=True))
    return centred * lax.rsqrt(variance + EPSILON) * gain_vec + shift_vec

def head_attend(inputs, same_doc):
    query, key_rows, value_rows = inputs
    scores = low_back(product(query, key_rows.T) * HEAD_DIM ** (-0.5))
    attend = jax.nn.softmax(jnp.where(same_doc, scores, MASKED), axis=-1)
    return product(low(attend), value_rows)

def seq_attend(inputs):
    queries, key_heads, value_heads, doc_ids = inputs
    same_doc = doc_ids[:, None] == doc_ids[None, :]
    per_head = jax.checkpoint(partial(head_attend, same_doc=same_doc))
    return lax.map(per_head, (queries, key_heads, value_heads))

def heads_of(matrix):
    return matrix.reshape(SEQS, LEN, HEADS, HEAD_DIM).transpose(0, 2, 1, 3)

def reference(tokens, segment_ids, qkv_weight, out_weight, up_weight, down_weight, first_gain, first_bias, second_gain, second_bias, out_grad):

    def forward(tokens_f, merged_w, mixer_w, widen_w, narrow_w, gain_one, bias_one, gain_two, bias_two):
        merged = low_back(low(product(tokens_f, merged_w)))
        context = lax.map(jax.checkpoint(seq_attend), (heads_of(merged[:, :D]), heads_of(merged[:, D:2 * D]), heads_of(merged[:, 2 * D:]), segment_ids))
        context = low_back(low(context.transpose(0, 2, 1, 3).reshape(TOKENS, D)))
        first_norm = layer_norm(tokens_f + low_back(product(context, mixer_w)), gain_one, bias_one)
        pre_act = low_back(product(low(first_norm), widen_w))
        act_low = low(jax.nn.gelu(pre_act, approximate=True))
        return layer_norm(first_norm + low_back(product(act_low, narrow_w)), gain_two, bias_two)
    primals = (tokens.astype(jnp.float32), qkv_weight.astype(jnp.float32), out_weight.astype(jnp.float32), up_weight.astype(jnp.float32), down_weight.astype(jnp.float32), first_gain.astype(jnp.float32), first_bias.astype(jnp.float32), second_gain.astype(jnp.float32), second_bias.astype(jnp.float32))
    result, pullback = jax.vjp(forward, *primals)
    gradients = pullback(out_grad.astype(jnp.float32))
    return (result.astype(jnp.bfloat16), gradients[0], gradients[1], gradients[2], gradients[3], gradients[4], gradients[5], gradients[6], gradients[7], gradients[8])
```

```python
from functools import partial

import jax
import jax.numpy as jnp
from jax import lax
from jax.experimental import pallas as pl
from jax.experimental.pallas import tpu as pltpu
from jax.sharding import PartitionSpec as P

HEADS = 12
HEAD_DIM = 64
GROUPS = 16
EPSILON = 1e-12
FAR = -(2.0**30)
SCALE = HEAD_DIM**-0.5
BQ = 256
BK = 256
BF = jnp.bfloat16
F32 = jnp.float32


def dot(a, b, ca, cb):
    return lax.dot_general(a, b, (((ca,), (cb,)), ((), ())), preferred_element_type=F32)


def doc_rows(ids_ref, same, other):
    ids = ids_ref[...]
    rows = lax.broadcasted_iota(jnp.int32, (GROUPS, ids.shape[1]), 0)
    return jnp.where(rows == ids, same, other).astype(BF)


def fill_tokens(info, own, recv, ids_ref, nq, q_t, k_nat, v_t, k_t, v_nat):
    half = own.shape[1]
    total = 2 * half
    place = info[2 * nq]
    q_t[HEAD_DIM : HEAD_DIM + GROUPS, :] = doc_rows(ids_ref, 0.0, FAR)
    q_t[HEAD_DIM + GROUPS :, :] = jnp.zeros((128 - HEAD_DIM - GROUPS, total), BF)
    for side, ref in ((place, own), (1 - place, recv)):
        at = pl.multiple_of(side * half, half)
        q_t[:HEAD_DIM, pl.ds(at, half)] = ref[:HEAD_DIM, :] * SCALE
        keys = ref[HEAD_DIM : 2 * HEAD_DIM, :]
        values = ref[2 * HEAD_DIM :, :]
        if k_t is not None:
            k_t[:, pl.ds(at, half)] = keys
        if v_t is not None:
            v_t[:, pl.ds(at, half)] = values
        k_nat[pl.ds(at, half), :HEAD_DIM] = keys.T
        if v_nat is not None:
            v_nat[pl.ds(at, half), :] = jnp.concatenate(
                [values, jnp.zeros((128 - HEAD_DIM, half), BF)], 0
            ).T
    docs = jnp.concatenate(
        [doc_rows(ids_ref, 1.0, 0.0), jnp.zeros((128 - HEAD_DIM - GROUPS, total), BF)], 0
    )
    k_nat[:, HEAD_DIM:] = docs.T


def attend_kernel(nq, info, own, recv, ids_ref, ctx_own, ctx_send, ctx_full, lse, q_t, k_nat, v_t):
    half = own.shape[1]
    fill_tokens(info, own, recv, ids_ref, nq, q_t, k_nat, v_t, None, None)

    def query_block(i, carry):
        at = pl.multiple_of(i * BQ, BQ)
        query = q_t[:, pl.ds(at, BQ)]

        def key_block(k, state):
            top, total, acc = state
            kat = pl.multiple_of(k * BK, BK)
            scores = jnp.dot(k_nat[pl.ds(kat, BK), :], query, preferred_element_type=F32)
            new_top = jnp.maximum(top, jnp.max(scores, 0, keepdims=True))
            powers = jnp.exp(scores - new_top)
            fade = jnp.exp(top - new_top)
            total = total * fade + jnp.sum(powers, 0, keepdims=True)
            acc = acc * fade + jnp.dot(
                v_t[:, pl.ds(kat, BK)], powers.astype(BF), preferred_element_type=F32
            )
            return new_top, total, acc

        top, total, acc = lax.fori_loop(
            info[i],
            info[nq + i],
            key_block,
            (
                jnp.full((1, BQ), -3e38, F32),
                jnp.zeros((1, BQ), F32),
                jnp.zeros((HEAD_DIM, BQ), F32),
            ),
        )
        ctx_full[:, pl.ds(at, BQ)] = acc / total
        lse[:, pl.ds(at, BQ)] = top + jnp.log(total)
        return carry

    lax.fori_loop(0, nq, query_block, 0)
    place = info[2 * nq]
    ctx_own[...] = ctx_full[:, pl.ds(pl.multiple_of(place * half, half), half)].astype(BF)
    ctx_send[...] = ctx_full[:, pl.ds(pl.multiple_of((1 - place) * half, half), half)].astype(BF)


def attend(info, own, recv, ids):
    half = own.shape[1]
    total = 2 * half
    nq = total // BQ
    vm = pl.BlockSpec(memory_space=pltpu.VMEM)
    return pl.pallas_call(
        partial(attend_kernel, nq),
        out_shape=(
            jax.ShapeDtypeStruct((HEAD_DIM, half), BF),
            jax.ShapeDtypeStruct((HEAD_DIM, half), BF),
            jax.ShapeDtypeStruct((HEAD_DIM, total), F32),
            jax.ShapeDtypeStruct((1, total), F32),
        ),
        in_specs=[pl.BlockSpec(memory_space=pltpu.SMEM), vm, vm, vm],
        out_specs=(vm, vm, vm, vm),
        scratch_shapes=[
            pltpu.VMEM((128, total), BF),
            pltpu.VMEM((total, 128), BF),
            pltpu.VMEM((HEAD_DIM, total), BF),
        ],
        cost_estimate=pl.CostEstimate(
            flops=4 * total * total * HEAD_DIM, bytes_accessed=8 * 192 * total, transcendentals=total * total // 3
        ),
        name="attend",
    )(info, own, recv, ids)


def attend_back_kernel(
    nq, info, own, recv, g_own, g_recv, ids_ref, ctx_full, lse, out_own, out_send,
    q_t, k_nat, k_t, v_nat, g_t, qg_nat, acc, dq_t,
):
    half = own.shape[1]
    place = info[2 * nq]
    fill_tokens(info, own, recv, ids_ref, nq, q_t, k_nat, None, k_t, v_nat)
    g_t[HEAD_DIM:, :] = jnp.zeros((128 - HEAD_DIM, 2 * half), BF)
    for side, ref, grad in ((place, own, g_own), (1 - place, recv, g_recv)):
        at = pl.multiple_of(side * half, half)
        g_t[:HEAD_DIM, pl.ds(at, half)] = grad[...]
        qg_nat[pl.ds(at, half), :] = jnp.concatenate([ref[:HEAD_DIM, :] * SCALE, grad[...]], 0).T
    acc[...] = jnp.zeros_like(acc)

    def query_block(i, carry):
        at = pl.multiple_of(i * BQ, BQ)
        query = q_t[:, pl.ds(at, BQ)]
        grad = g_t[:, pl.ds(at, BQ)]
        row_term = jnp.sum(
            ctx_full[:, pl.ds(at, BQ)] * grad[:HEAD_DIM].astype(F32), 0, keepdims=True
        )
        log_total = lse[:, pl.ds(at, BQ)]
        natural = qg_nat[pl.ds(at, BQ), :]
        left = lax.broadcasted_iota(jnp.int32, (BK, 128), 1) < HEAD_DIM

        def key_block(k, dq):
            kat = pl.multiple_of(k * BK, BK)
            scores = jnp.dot(k_nat[pl.ds(kat, BK), :], query, preferred_element_type=F32)
            chance = jnp.exp(scores - log_total)
            grad_chance = jnp.dot(v_nat[pl.ds(kat, BK), :], grad, preferred_element_type=F32)
            grad_scores = (chance * (grad_chance - row_term)).astype(BF)
            dq = dq + jnp.dot(k_t[:, pl.ds(kat, BK)], grad_scores, preferred_element_type=F32)
            acc[pl.ds(kat, BK), :] += jnp.where(
                left,
                jnp.dot(grad_scores, natural, preferred_element_type=F32),
                jnp.dot(chance.astype(BF), natural, preferred_element_type=F32),
            )
            return dq

        dq_t[:, pl.ds(at, BQ)] = (
            lax.fori_loop(info[i], info[nq + i], key_block, jnp.zeros((HEAD_DIM, BQ), F32)) * SCALE
        )
        return carry

    lax.fori_loop(0, nq, query_block, 0)
    for side, out in ((place, out_own), (1 - place, out_send)):
        at = pl.multiple_of(side * half, half)
        out[:HEAD_DIM, :] = dq_t[:, pl.ds(at, half)].astype(BF)
        out[HEAD_DIM:, :] = acc[pl.ds(at, half), :].T.astype(BF)


def attend_back(info, own, recv, g_own, g_recv, ids, ctx_full, lse):
    half = own.shape[1]
    total = 2 * half
    nq = total // BQ
    vm = pl.BlockSpec(memory_space=pltpu.VMEM)
    return pl.pallas_call(
        partial(attend_back_kernel, nq),
        out_shape=(
            jax.ShapeDtypeStruct((3 * HEAD_DIM, half), BF),
            jax.ShapeDtypeStruct((3 * HEAD_DIM, half), BF),
        ),
        in_specs=[pl.BlockSpec(memory_space=pltpu.SMEM)] + [vm] * 7,
        out_specs=(vm, vm),
        scratch_shapes=[
            pltpu.VMEM((128, total), BF),
            pltpu.VMEM((total, 128), BF),
            pltpu.VMEM((HEAD_DIM, total), BF),
            pltpu.VMEM((total, 128), BF),
            pltpu.VMEM((128, total), BF),
            pltpu.VMEM((total, 128), BF),
            pltpu.VMEM((total, 128), F32),
            pltpu.VMEM((HEAD_DIM, total), F32),
        ],
        cost_estimate=pl.CostEstimate(
            flops=10 * total * total * HEAD_DIM, bytes_accessed=12 * 192 * total, transcendentals=total * total // 3
        ),
        name="attend_back",
    )(info, own, recv, g_own, g_recv, ids, ctx_full, lse)


def norm_rows(hidden, gain_vec, shift_vec):
    row_mean = jnp.mean(hidden, -1, keepdims=True)
    centred = hidden - row_mean
    variance = jnp.mean(centred * centred, -1, keepdims=True)
    inverse = lax.rsqrt(variance + EPSILON)
    normed = centred * inverse
    return (normed * gain_vec + shift_vec, normed, inverse)


def norm_back(grad_y, normed, inverse, gain_vec):
    grad_n = grad_y * gain_vec
    bracket = (
        grad_n
        - jnp.mean(grad_n, -1, keepdims=True)
        - normed * jnp.mean(grad_n * normed, -1, keepdims=True)
    )
    return (inverse * bracket, jnp.sum(grad_y * normed, 0), jnp.sum(grad_y, 0))


def gelu_both(u):
    root = 0.7978845608028654
    t = jnp.tanh(root * (u + 0.044715 * (u * u * u)))
    act = 0.5 * u * (1.0 + t)
    slope = 0.5 * (1.0 + t) + 0.5 * u * (1.0 - t * t) * (root * (1.0 + 3 * 0.044715 * (u * u)))
    return act, slope


def shards(
    n_shard,
    tokens,
    segment_ids,
    qkv_weight,
    out_weight,
    up_weight,
    down_weight,
    first_gain,
    first_bias,
    second_gain,
    second_bias,
    out_grad,
):
    rows, width = tokens.shape
    shard = lax.axis_index("shard")
    seq = lax.axis_index("seq")
    xb, cb = seq // 2, seq % 2
    bits = [1 << b for b in range(n_shard.bit_length() - 1)]
    top = bits[-1]
    owner = (shard // top) % 2 == cb

    def swap(value, mask):
        return lax.ppermute(value, "shard", [(i, i ^ mask) for i in range(n_shard)])

    def swap_core(value):
        return lax.ppermute(value, "seq", [(i, i ^ 1) for i in range(4)])

    def swap_x(value):
        return lax.ppermute(value, "seq", [(i, i ^ 2) for i in range(4)])

    def to_core(value, to_owner):
        pairs = []
        for sh in range(n_shard):
            for se in range(4):
                if (sh // top == se % 2) != to_owner:
                    pairs.append((sh * 4 + se, (sh ^ top) * 4 + se))
        return lax.ppermute(value, ("shard", "seq"), pairs)

    def ordered(flag, own, other, axis):
        return jnp.where(
            flag == 0, jnp.stack([own, other], axis), jnp.stack([other, own], axis)
        )

    def gather(block, over):
        value = block[None]
        for bit in over:
            value = ordered((shard // bit) % 2, value, swap(value, bit), 1)
            value = value.reshape((-1,) + block.shape)
        return value.reshape((-1,) + block.shape[1:])

    def gather_half(block):
        there = to_core(block, False)
        return gather(jnp.where(owner, block, there), bits[-2::-1])

    def reduce(partial_sum, over, blocks):
        value = partial_sum.reshape((blocks, -1) + partial_sum.shape[1:])
        for bit in over:
            pairs = value.reshape((value.shape[0] // 2, 2) + value.shape[1:])
            flag = (shard // bit) % 2
            mine = jnp.where(flag == 0, pairs[:, 0], pairs[:, 1])
            theirs = jnp.where(flag == 0, pairs[:, 1], pairs[:, 0])
            value = (mine.astype(F32) + swap(theirs, bit).astype(F32)).astype(BF)
        return value[0]

    def add_x(value):
        return (value.astype(F32) + swap_x(value).astype(F32)).astype(BF)

    def reduce_cols(partial_sum):
        return add_x(reduce(partial_sum, bits, n_shard))

    def reduce_half(partial_sum):
        value = reduce(partial_sum, bits[:-1], n_shard // 2)
        there = to_core(value, True)
        value = add_x((value.astype(F32) + there.astype(F32)).astype(BF))
        return jnp.where(owner, value, swap_core(value))

    def pick(value, flag, axis):
        return jnp.where(flag == 0, lax.index_in_dim(value, 0, axis, False), lax.index_in_dim(value, 1, axis, False))

    def chip_rows(value):
        both = ordered(cb, value, swap_core(value), 0)
        return both.reshape((2 * rows,) + value.shape[1:])

    def core_sum(partial_sum):
        halves = partial_sum.reshape(2, rows, -1)
        return pick(halves, cb, 0) + swap_core(pick(halves, 1 - cb, 0).astype(BF)).astype(F32)

    half_width = width // 2
    chip_tokens = chip_rows(tokens)
    sections = lax.dynamic_slice_in_dim(
        qkv_weight.reshape(-1, 3, width), cb * half_width, half_width, 2
    )
    qkv_parts = [
        gather(sections[:, :, j * 128 : (j + 1) * 128].reshape(-1, 384), bits[::-1]) for j in range(3)
    ]
    vectors = jnp.stack([first_gain, first_bias, second_gain, second_bias])
    vectors = jnp.concatenate([vectors, vectors, vectors, vectors], 0)
    vectors = gather(vectors[None], bits[::-1])[:, :4].transpose(1, 0, 2).reshape(4, width).astype(F32)
    gain_one, bias_one, gain_two, bias_two = vectors[0], vectors[1], vectors[2], vectors[3]
    mixer = gather_half(out_weight)
    ff_half = up_weight.shape[1] // 2
    widen = gather(lax.dynamic_slice_in_dim(up_weight, cb * ff_half, ff_half, 1), bits[::-1])
    narrow = gather_half(down_weight)

    ids = segment_ids[0]
    length = ids.shape[0]
    nq = length // BQ
    first = ids.reshape(nq, BQ)[:, 0]
    last = ids.reshape(nq, BQ)[:, -1]
    begin = jnp.sum((ids[None] < first[:, None]).astype(jnp.int32), 1) // BK
    end = (jnp.sum((ids[None] <= last[:, None]).astype(jnp.int32), 1) + BK - 1) // BK
    info = jnp.concatenate([begin, end, xb[None].astype(jnp.int32)])
    ids_row = ids[None]
    saved = []
    context = []
    for j in range(3):
        merged = dot(qkv_parts[j], chip_tokens, 0, 1).astype(BF).reshape(3, 2, HEAD_DIM, 2 * rows)
        own = pick(merged, xb, 1).reshape(3 * HEAD_DIM, 2 * rows)
        recv = swap_x(pick(merged, 1 - xb, 1).reshape(3 * HEAD_DIM, 2 * rows))
        ctx_own, ctx_send, ctx_full, lse = attend(info, own, recv, ids_row)
        context.append(ordered(xb, ctx_own, swap_x(ctx_send), 0))
        saved.append((own, recv, ctx_full, lse))
    context = jnp.stack(context).reshape(half_width, 2 * rows)

    attn_out = core_sum(dot(context, mixer, 0, 0))
    first_norm, normed_one, inverse_one = norm_rows(
        tokens.astype(F32) + attn_out, gain_one, bias_one
    )
    first_low = chip_rows(first_norm.astype(BF))
    act, slope = gelu_both(dot(first_low, widen, 1, 0))
    act_low = act.astype(BF)
    slope_low = slope.astype(BF)
    mlp_out = core_sum(dot(act_low, narrow, 1, 0))
    result, normed_two, inverse_two = norm_rows(first_norm + mlp_out, gain_two, bias_two)

    grad_two, late_gain, late_shift = norm_back(
        out_grad.astype(F32), normed_two, inverse_two, gain_two
    )
    grad_mlp = chip_rows(grad_two.astype(BF))
    grad_pre = (dot(grad_mlp, narrow, 1, 1) * slope_low.astype(F32)).astype(BF)
    grad_first = grad_two + core_sum(dot(grad_pre, widen, 1, 1))
    grad_one, early_gain, early_shift = norm_back(grad_first, normed_one, inverse_one, gain_one)
    grad_attn = chip_rows(grad_one.astype(BF))
    grad_context = dot(mixer, grad_attn, 1, 1).astype(BF).reshape(3, 2, HEAD_DIM, 2 * rows)
    g_own = pick(grad_context, xb, 1)
    g_recv = swap_x(pick(grad_context, 1 - xb, 1))

    narrow_grad = reduce_half(dot(act_low, grad_mlp, 0, 0).astype(BF))
    widen_grad = reduce_cols(dot(first_low, grad_pre, 0, 0).astype(BF))
    mixer_grad = reduce_half(dot(context, grad_attn, 1, 0).astype(BF))

    sums = jnp.stack([early_gain, early_shift, late_gain, late_shift])
    sums = sums + swap_core(sums)
    sums = sums.reshape(4, n_shard, -1).transpose(1, 0, 2)
    sums = jnp.concatenate([sums, jnp.zeros_like(sums), jnp.zeros_like(sums), jnp.zeros_like(sums)], 1).astype(BF)
    sums = add_x(reduce(sums.reshape(n_shard * 16, -1), bits, n_shard)).astype(F32)

    grads = []
    qkv_grads = []
    for j in range(3):
        own, recv, ctx_full, lse = saved[j]
        d_own, d_send = attend_back(
            info, own, recv, g_own[j], g_recv[j], ids_row, ctx_full, lse
        )
        d_recv = swap_x(d_send)
        both = ordered(
            xb, d_own.reshape(3, HEAD_DIM, -1), d_recv.reshape(3, HEAD_DIM, -1), 1
        ).reshape(384, 2 * rows)
        grads.append(both)
        qkv_grads.append(reduce_cols(dot(chip_tokens, both, 0, 1).astype(BF)))
    back = sum(dot(grads[j], qkv_parts[j], 0, 1) for j in range(3))
    input_grad = grad_one + core_sum(back)

    mine = jnp.concatenate([g.reshape(-1, 3, 128) for g in qkv_grads], 2)
    qkv_grad = ordered(cb, mine, swap_core(mine), 2).reshape(mine.shape[0], 3 * width)
    widen_grad = ordered(cb, widen_grad, swap_core(widen_grad), 1).reshape(-1, 2 * ff_half)
    return (
        result.astype(BF),
        input_grad,
        qkv_grad.astype(F32),
        mixer_grad.astype(F32),
        widen_grad.astype(F32),
        narrow_grad.astype(F32),
        sums[0],
        sums[1],
        sums[2],
        sums[3],
    )


def solution(mesh):
    placed = (
        P(("shard", "seq"), None),
        P("shard", None),
        P("shard", None),
        P("shard", None),
        P("shard", None),
        P("shard", None),
        P("shard"),
        P("shard"),
        P("shard"),
        P("shard"),
        P(("shard", "seq"), None),
    )
    return jax.shard_map(
        partial(shards, mesh.shape["shard"]),
        mesh=mesh,
        in_specs=placed,
        out_specs=(
            P(("shard", "seq"), None),
            P(("shard", "seq"), None),
            P("shard", None),
            P("shard", None),
            P("shard", None),
            P("shard", None),
            P("shard"),
            P("shard"),
            P("shard"),
            P("shard"),
        ),
        check_vma=False,
    )
```

```python
from functools import partial

import jax
import jax.numpy as jnp
from jax import lax
from jax.experimental import pallas as pl
from jax.experimental.pallas import tpu as pltpu
from jax.sharding import PartitionSpec as P

HEADS = 12
HEAD_DIM = 64
TRIO = 3 * HEAD_DIM
GROUPS = 16
EPSILON = 1e-12
FAR = -(2.0**30)
SCALE = HEAD_DIM**-0.5
TILE = 512
BF = jnp.bfloat16
F32 = jnp.float32
VMEM = pl.BlockSpec(memory_space=pltpu.VMEM)
SMEM = pl.BlockSpec(memory_space=pltpu.SMEM)
FREE = pl.CostEstimate(flops=1, bytes_accessed=1, transcendentals=0)


def dot(a, b, ca, cb):
    return lax.dot_general(a, b, (((ca,), (cb,)), ((), ())), preferred_element_type=F32)


def shape(dims, kind):
    return jax.ShapeDtypeStruct(dims, kind)


def params(mebi):
    return pltpu.CompilerParams(vmem_limit_bytes=mebi << 20)


def assemble_kernel(offsets, info, *refs):
    out = refs[-1]
    for ref, rel in zip(refs[:-1], offsets):
        block = ref.shape[1]
        for i, r in enumerate(rel):
            at = pl.multiple_of((info[0] ^ r) * block, block)
            out[pl.ds(at, block), :] = ref[i]


def assemble(pieces, offsets, me):
    block, cols = pieces[0].shape[1:]
    count = sum(len(r) for r in offsets)
    if block % 16:
        value = jnp.concatenate(pieces)
        order = [r for rel in offsets for r in rel]
        place = jnp.array([order.index(r) for r in range(count)], jnp.int32)
        return value[place[me ^ jnp.arange(count)]].reshape(count * block, cols)
    return pl.pallas_call(
        partial(assemble_kernel, offsets),
        out_shape=shape((count * block, cols), BF),
        in_specs=[SMEM] + [VMEM] * len(pieces),
        out_specs=VMEM,
        compiler_params=params(12),
        cost_estimate=FREE,
        name="assemble",
    )(me[None], *pieces)


def prepare_kernel(info, qkv, out_weight, *refs):
    vectors, (part_a, part_b, scratch) = refs[:4], refs[4:]
    block, width = out_weight.shape
    half, quarter = width // 2, width // 4
    scratch[...] = jnp.zeros_like(scratch)
    for i, ref in enumerate(vectors):
        scratch[i : i + 1, :block] = ref[...].astype(F32)
    part_a[:, TRIO:] = scratch[...].T[:block, : 256 - TRIO].astype(BF)
    for x in range(2):
        for c in range(2):

            @pl.when(jnp.logical_and(info[0] == x, info[1] == c))
            def _():
                at = c * half + x * quarter
                trio = [qkv[:, i * width + at : i * width + at + quarter] for i in range(3)]
                for j in range(3):
                    piece = jnp.concatenate(
                        [t[:, j * HEAD_DIM : (j + 1) * HEAD_DIM] for t in trio], 1
                    )
                    if j == 0:
                        part_a[:, :TRIO] = piece
                    else:
                        part_b[:, (j - 1) * TRIO : j * TRIO] = piece
                part_b[:, 2 * TRIO :] = out_weight[:, c * half : (c + 1) * half]


def prepare(info, qkv, out_weight, vectors):
    block, width = out_weight.shape
    return pl.pallas_call(
        prepare_kernel,
        out_shape=(shape((block, 256), BF), shape((block, 2 * TRIO + width // 2), BF)),
        in_specs=[SMEM] + [VMEM] * 6,
        out_specs=(VMEM, VMEM),
        scratch_shapes=[pltpu.VMEM((128, 128), F32)],
        compiler_params=params(8),
        cost_estimate=FREE,
        name="prepare",
    )(info, qkv, out_weight, *[v[None] for v in vectors])


def vectors_kernel(part, out):
    out[...] = part[:, 128:].astype(F32).T[TRIO - 128 : TRIO - 120]


def vectors_of(part):
    return pl.pallas_call(
        vectors_kernel,
        out_shape=shape((8, part.shape[0]), F32),
        in_specs=[VMEM],
        out_specs=VMEM,
        compiler_params=params(8),
        cost_estimate=FREE,
        name="vectors",
    )(part)


def doc_rows(ids_ref, same, other):
    ids = ids_ref[...]
    rows = lax.broadcasted_iota(jnp.int32, (GROUPS, ids.shape[1]), 0)
    return jnp.where(rows == ids, same, other).astype(BF)


def tile_at(index, me):
    return pl.multiple_of((index ^ me) * TILE, TILE)


def attend_kernel(
    info, tok0, tok1, tok2, tok3, weight, ids_ref, ctx_own, ctx_send, ctx_full, lse,
    q_t, k_nat, v_t, s_ref,
):
    total = ids_ref.shape[1]
    half = total // 2
    tiles = total // TILE
    me = info[2 * tiles]
    weight_t = weight[...].T
    keys = weight[:, HEAD_DIM : 2 * HEAD_DIM]
    for i, tok in enumerate((tok0, tok1, tok2, tok3)):
        at = i * TILE
        rows = tok[...]
        trio = dot(weight_t, rows, 1, 1).astype(BF)
        q_t[:HEAD_DIM, at : at + TILE] = trio[:HEAD_DIM] * SCALE
        v_t[:, at : at + TILE] = trio[2 * HEAD_DIM :]
        k_nat[at : at + TILE, :HEAD_DIM] = dot(rows, keys, 1, 0).astype(BF)
    q_t[HEAD_DIM : HEAD_DIM + GROUPS, :] = doc_rows(ids_ref, 0.0, FAR)
    q_t[HEAD_DIM + GROUPS :, :] = jnp.zeros((128 - HEAD_DIM - GROUPS, total), BF)
    docs = jnp.concatenate(
        [doc_rows(ids_ref, 1.0, 0.0), jnp.zeros((128 - HEAD_DIM - GROUPS, total), BF)], 0
    )
    k_nat[:, HEAD_DIM:] = docs.T

    def query_tile(i, carry):
        at = tile_at(i, me)
        query = q_t[:, pl.ds(at, TILE)]
        begin, end = info[i], info[tiles + i]

        def score(k, top):
            scores = dot(k_nat[pl.ds(tile_at(k, me), TILE), :], query, 1, 0)
            s_ref[pl.ds(pl.multiple_of(k * TILE, TILE), TILE), :] = scores
            return jnp.maximum(top, jnp.max(scores.reshape(TILE // 8, 8, TILE), 0))

        top = lax.fori_loop(begin, end, score, jnp.full((8, TILE), -3e38, F32))
        top = jnp.max(top, 0, keepdims=True)

        def weigh(k, state):
            total8, acc = state
            powers = jnp.exp(s_ref[pl.ds(pl.multiple_of(k * TILE, TILE), TILE), :] - top)
            total8 = total8 + jnp.sum(powers.reshape(TILE // 8, 8, TILE), 0)
            acc = acc + dot(v_t[:, pl.ds(tile_at(k, me), TILE)], powers.astype(BF), 1, 0)
            return total8, acc

        total8, acc = lax.fori_loop(
            begin, end, weigh, (jnp.zeros((8, TILE), F32), jnp.zeros((HEAD_DIM, TILE), F32))
        )
        sums = jnp.sum(total8, 0, keepdims=True)
        ctx_full[:, pl.ds(at, TILE)] = acc / sums
        lse[:, pl.ds(at, TILE)] = top + jnp.log(sums)
        return carry

    lax.fori_loop(0, tiles, query_tile, 0)
    ctx_own[...] = ctx_full[:, :half].astype(BF)
    ctx_send[...] = ctx_full[:, half:].astype(BF)


def attend(info, toks, weight, ids):
    total = ids.shape[1]
    half = total // 2
    return pl.pallas_call(
        attend_kernel,
        out_shape=(
            shape((HEAD_DIM, half), BF),
            shape((HEAD_DIM, half), BF),
            shape((HEAD_DIM, total), F32),
            shape((1, total), F32),
        ),
        in_specs=[SMEM] + [VMEM] * 6,
        out_specs=(VMEM,) * 4,
        scratch_shapes=[
            pltpu.VMEM((128, total), BF),
            pltpu.VMEM((total, 128), BF),
            pltpu.VMEM((HEAD_DIM, total), BF),
            pltpu.VMEM((total, TILE), F32),
        ],
        compiler_params=params(24),
        cost_estimate=FREE,
        name="attend",
    )(info, *toks, weight, ids)


def attend_back_kernel(
    order, info, tok0, tok1, tok2, tok3, weight, ids_ref, g_own, g_recv, ctx_full, lse, sums,
    out, grad_out, q_t, kvd, k_t, g_t, qg_nat, acc, dq_t, w_grad,
):
    total = ids_ref.shape[1]
    half = total // 2
    tiles = total // TILE
    me, shard = info[2 * tiles], info[2 * tiles + 1]
    toks = (tok0, tok1, tok2, tok3)
    weight_t = weight[:, : 2 * HEAD_DIM].T
    natural_w = weight[:, HEAD_DIM:]
    for at, grad in ((0, g_own), (half, g_recv)):
        g_t[HEAD_DIM:, at : at + half] = grad[...]
    g_t[:HEAD_DIM, :] = jnp.zeros((HEAD_DIM, total), BF)
    for i, tok in enumerate(toks):
        at = i * TILE
        rows = tok[...]
        pair = dot(weight_t, rows, 1, 1).astype(BF)
        q_t[:HEAD_DIM, at : at + TILE] = pair[:HEAD_DIM] * SCALE
        k_t[:, at : at + TILE] = pair[HEAD_DIM:]
        kvd[at : at + TILE, :128] = dot(rows, natural_w, 1, 0).astype(BF)
    qg_nat[...] = jnp.concatenate([q_t[:HEAD_DIM, :], g_t[HEAD_DIM:, :]], 0).T
    q_t[HEAD_DIM:128, :] = jnp.zeros((128 - HEAD_DIM, total), BF)
    q_t[128 : 128 + GROUPS, :] = doc_rows(ids_ref, 0.0, FAR)
    q_t[128 + GROUPS :, :] = jnp.zeros((128 - GROUPS, total), BF)
    kvd[:, 128:] = jnp.concatenate(
        [doc_rows(ids_ref, 1.0, 0.0), jnp.zeros((128 - GROUPS, total), BF)], 0
    ).T
    acc[...] = jnp.zeros_like(acc)

    def query_tile(i, carry):
        at = tile_at(i, me)
        query = q_t[:, pl.ds(at, TILE)]
        grad = g_t[:, pl.ds(at, TILE)]
        row_term = jnp.sum(
            ctx_full[:, pl.ds(at, TILE)] * grad[HEAD_DIM:].astype(F32), 0, keepdims=True
        )
        log_total = lse[:, pl.ds(at, TILE)]
        natural = qg_nat[pl.ds(at, TILE), :]
        left = lax.broadcasted_iota(jnp.int32, (TILE, 128), 1) < HEAD_DIM

        def key_tile(k, dq):
            kat = tile_at(k, me)
            scores = dot(kvd[pl.ds(kat, TILE), :], query, 1, 0)
            chance = jnp.exp(scores - log_total)
            grad_chance = dot(kvd[pl.ds(kat, TILE), :128], grad, 1, 0)
            grad_scores = (chance * (grad_chance - row_term)).astype(BF)
            dq = dq + dot(k_t[:, pl.ds(kat, TILE)], grad_scores, 1, 0)
            acc[pl.ds(kat, TILE), :] += jnp.where(
                left, dot(grad_scores, natural, 1, 0), dot(chance.astype(BF), natural, 1, 0)
            )
            return dq

        dq = lax.fori_loop(info[i], info[tiles + i], key_tile, jnp.zeros((HEAD_DIM, TILE), F32))
        dq_t[:, pl.ds(at, TILE)] = (dq * SCALE).astype(BF)
        return carry

    lax.fori_loop(0, tiles, query_tile, 0)
    out[:HEAD_DIM, :] = dq_t[...]
    out[HEAD_DIM:, :] = acc[...].T.astype(BF)
    for i, tok in enumerate(toks):
        part = dot(out[:, i * TILE : (i + 1) * TILE], tok[...], 1, 0)
        w_grad[:TRIO, :] = part if i == 0 else w_grad[:TRIO, :] + part
    if sums is not None:
        w_grad[TRIO : TRIO + 8, :] = sums[...]
        w_grad[TRIO + 8 :, :] = jnp.zeros((256 - TRIO - 8, w_grad.shape[1]), F32)
    else:
        w_grad[TRIO:, :] = jnp.zeros((256 - TRIO, w_grad.shape[1]), F32)
    natural = w_grad[...].T
    block = grad_out.shape[1]
    for b in range(len(order)):
        grad_out[order_of(order, shard, b)] = natural[b * block : (b + 1) * block].astype(BF)


def order_of(order, me, b):
    rel = me ^ b
    bits = len(order).bit_length() - 1
    place = 0
    for i in range(bits):
        place = place | (((rel >> i) & 1) << (bits - 1 - i))
    return place


def attend_back(info, toks, weight, ids, g_own, g_recv, ctx_full, lse, sums, n_shard):
    total = ids.shape[1]
    width = weight.shape[0]
    extra = [] if sums is None else [sums]

    def kernel(*refs):
        refs = list(refs)
        if sums is None:
            refs.insert(11, None)
        attend_back_kernel(range(n_shard), *refs)

    return pl.pallas_call(
        kernel,
        out_shape=(shape((TRIO, total), BF), shape((n_shard, width // n_shard, 256), BF)),
        in_specs=[SMEM] + [VMEM] * (10 + len(extra)),
        out_specs=(VMEM, VMEM),
        scratch_shapes=[
            pltpu.VMEM((256, total), BF),
            pltpu.VMEM((total, 256), BF),
            pltpu.VMEM((HEAD_DIM, total), BF),
            pltpu.VMEM((128, total), BF),
            pltpu.VMEM((total, 128), BF),
            pltpu.VMEM((total, 128), F32),
            pltpu.VMEM((HEAD_DIM, total), BF),
            pltpu.VMEM((256, width), F32),
        ],
        compiler_params=params(24),
        cost_estimate=FREE,
        name="attend_back",
    )(info, *toks, weight, ids, g_own, g_recv, ctx_full, lse, *extra)


def input_back_kernel(d0, d1, d2, w0, w1, w2, own, over_x, send_core):
    rows = own.shape[0]
    weights = jnp.concatenate([w[...] for w in (w0, w1, w2)], 1)
    for r, out in enumerate((own, send_core.at[0], over_x, send_core.at[1])):
        at = r * rows
        grads = jnp.concatenate([d[:, at : at + rows] for d in (d0, d1, d2)], 0)
        out[...] = dot(grads.T, weights, 1, 1).astype(out.dtype)


def input_back(grads, weights, rows):
    width = weights[0].shape[0]
    return pl.pallas_call(
        input_back_kernel,
        out_shape=(
            shape((rows, width), F32), shape((rows, width), F32), shape((2, rows, width), BF)
        ),
        in_specs=[VMEM] * 6,
        out_specs=(VMEM,) * 3,
        compiler_params=params(24),
        cost_estimate=FREE,
        name="input_back",
    )(*grads, *weights)


def place_qkv_kernel(info, own, over_x, over_core, over_both, out, sums_out):
    part = out.shape[1] // 3
    quarter = part // 4
    x, c = info[0], info[1]
    total = None
    for ref, dx, dc in ((own, 0, 0), (over_x, 1, 0), (over_core, 0, 1), (over_both, 1, 1)):
        value = ref[...].astype(F32)
        tail = value[:, 2 * 256 + TRIO : 2 * 256 + TRIO + 8]
        total = tail if total is None else total + tail
        for sec in range(3):
            at = sec * HEAD_DIM
            piece = jnp.concatenate(
                [value[:, j * 256 + at : j * 256 + at + HEAD_DIM] for j in range(3)], 1
            )
            for xv in range(2):
                for cv in range(2):
                    to = sec * part + (cv * 2 + xv) * quarter

                    @pl.when(jnp.logical_and((x ^ dx) == xv, (c ^ dc) == cv))
                    def _():
                        out[:, to : to + quarter] = piece

    sums_out[...] = total


def place_qkv(info, own, over_x, over_core, over_both, width):
    block = own.shape[0]
    return pl.pallas_call(
        place_qkv_kernel,
        out_shape=(shape((block, 3 * width), F32), shape((block, 8), F32)),
        in_specs=[SMEM] + [VMEM] * 4,
        out_specs=(VMEM, VMEM),
        compiler_params=params(8),
        cost_estimate=FREE,
        name="place_qkv",
    )(info, own, over_x, over_core, over_both)


def gelu_both(u):
    root = 0.7978845608028654
    cube = 0.044715 * root
    square = u * u
    t = jnp.tanh(u * (root + cube * square))
    half = 0.5 * (1.0 + t)
    act = u * half
    slope = half + act * (1.0 - t) * (root + 3.0 * cube * square)
    return act, slope


def feed_up_kernel(low_own, low_other, up, act_out, act_t, slope_out, low_t):
    rows = low_own.shape[0]
    step = 256
    for p, low in enumerate((low_own, low_other)):

        def body(i, carry):
            at = pl.multiple_of(i * step, step)
            to = pl.multiple_of(p * rows + i * step, step)
            value = low[pl.ds(at, step), :]
            low_t[:, pl.ds(to, step)] = value.T
            act, slope = gelu_both(dot(value, up[...], 1, 0))
            act = act.astype(BF)
            act_out[pl.ds(to, step), :] = act
            act_t[:, pl.ds(to, step)] = act.T
            slope_out[pl.ds(to, step), :] = slope.astype(BF)
            return carry

        lax.fori_loop(0, rows // step, body, 0)


def feed_up(low_own, low_other, up):
    rows, width = low_own.shape
    hidden = up.shape[1]
    return pl.pallas_call(
        feed_up_kernel,
        out_shape=(
            shape((2 * rows, hidden), BF),
            shape((hidden, 2 * rows), BF),
            shape((2 * rows, hidden), BF),
            shape((width, 2 * rows), BF),
        ),
        in_specs=[VMEM] * 3,
        out_specs=(VMEM,) * 4,
        compiler_params=params(32),
        cost_estimate=FREE,
        name="feed_up",
    )(low_own, low_other, up)


def feed_down_kernel(act, down, own, send):
    rows = own.shape[0]
    step = 256
    for p, out in enumerate((own, send)):

        def body(i, carry):
            at = pl.multiple_of(i * step, step)
            value = act[pl.ds(pl.multiple_of(p * rows + i * step, step), step), :]
            out[pl.ds(at, step), :] = dot(value, down[...], 1, 0).astype(out.dtype)
            return carry

        lax.fori_loop(0, rows // step, body, 0)


def feed_down(act, down):
    rows, hidden = act.shape
    width = down.shape[1]
    return pl.pallas_call(
        feed_down_kernel,
        out_shape=(shape((rows // 2, width), F32), shape((rows // 2, width), BF)),
        in_specs=[VMEM] * 2,
        out_specs=(VMEM,) * 2,
        compiler_params=params(24),
        cost_estimate=FREE,
        name="feed_down",
    )(act, down)


def feed_back_kernel(grad_own, grad_other, slope, up, down, own, send, pre_out):
    rows = grad_own.shape[0]
    step = 256
    for p, (grad, out) in enumerate(((grad_own, own), (grad_other, send))):

        def body(i, carry):
            at = pl.multiple_of(i * step, step)
            to = pl.multiple_of(p * rows + i * step, step)
            pre = dot(grad[pl.ds(at, step), :], down[...], 1, 1)
            pre = (pre * slope[pl.ds(to, step), :].astype(F32)).astype(BF)
            pre_out[pl.ds(to, step), :] = pre
            out[pl.ds(at, step), :] = dot(pre, up[...], 1, 1).astype(out.dtype)
            return carry

        lax.fori_loop(0, rows // step, body, 0)


def feed_back(grad_own, grad_other, slope, up, down):
    rows, width = grad_own.shape
    hidden = up.shape[1]
    return pl.pallas_call(
        feed_back_kernel,
        out_shape=(
            shape((rows, width), F32),
            shape((rows, width), BF),
            shape((2 * rows, hidden), BF),
        ),
        in_specs=[VMEM] * 5,
        out_specs=(VMEM,) * 3,
        compiler_params=params(32),
        cost_estimate=FREE,
        name="feed_back",
    )(grad_own, grad_other, slope, up, down)


def weight_grad_kernel(blocks, shard, left, right_own, right_other, out):
    rows, cols = left.shape[0], out.shape[2]
    half = left.shape[1] // 2
    step = 256
    block = out.shape[1]
    lone = right_other is None

    def body(i, carry):
        at = pl.multiple_of(i * step, step)
        if lone:
            value = dot(left[...], right_own[:, pl.ds(at, step)], 1, 0)
        else:
            value = dot(left[:, :half], right_own[:, pl.ds(at, step)], 1, 0) + dot(
                left[:, half:], right_other[:, pl.ds(at, step)], 1, 0
            )
        for b in range(blocks):
            out[order_of(range(blocks), shard[0], b), :, pl.ds(at, step)] = value[
                b * block : (b + 1) * block
            ].astype(BF)
        return carry

    lax.fori_loop(0, cols // step, body, 0)


def weight_grad(shard, left, rights, blocks):
    rows, cols = left.shape[0], rights[0].shape[1]

    def kernel(*refs):
        refs = list(refs)
        if len(rights) == 1:
            refs.insert(3, None)
        weight_grad_kernel(blocks, *refs)

    return pl.pallas_call(
        kernel,
        out_shape=shape((blocks, rows // blocks, cols), BF),
        in_specs=[SMEM, VMEM] + [VMEM] * len(rights),
        out_specs=VMEM,
        compiler_params=params(24),
        cost_estimate=FREE,
        name="weight_grad",
    )(shard[None], left, *rights)


def mix_back_kernel(info, mixer, context, grad_own, grad_other, g_own, g_send, own, send):
    quarter = g_own.shape[0]
    rows = grad_own.shape[0]
    half_width = own.shape[1]
    for p, grad in enumerate((grad_own, grad_other)):
        value = dot(mixer[...], grad[...], 1, 1).astype(BF)
        g_own[:, p * rows : (p + 1) * rows] = value[:quarter]
        g_send[:, p * rows : (p + 1) * rows] = value[quarter:]
    for out, half in ((own, info[1]), (send, 1 - info[1])):
        at = pl.multiple_of(half * half_width, half_width)
        out[...] = (
            dot(context[:, :rows], grad_own[:, pl.ds(at, half_width)], 1, 0)
            + dot(context[:, rows:], grad_other[:, pl.ds(at, half_width)], 1, 0)
        ).astype(BF)


def mix_back(info, mixer, context, grad_own, grad_other):
    half_width, width = mixer.shape
    rows = grad_own.shape[0]
    return pl.pallas_call(
        mix_back_kernel,
        out_shape=(shape((half_width // 2, 2 * rows), BF),) * 2
        + (shape((half_width, half_width), BF),) * 2,
        in_specs=[SMEM] + [VMEM] * 4,
        out_specs=(VMEM,) * 4,
        compiler_params=params(16),
        cost_estimate=FREE,
        name="mix_back",
    )(info, mixer, context, grad_own, grad_other)


def mix_place_kernel(blocks, info, own, recv, out, scratch):
    half_width = own.shape[1]
    quarter = half_width // 2
    x, c, shard = info[0], info[1], info[2]
    for ref, dc in ((own, 0), (recv, 1)):
        for dx in range(2):
            at = pl.multiple_of((c ^ dc) * half_width + (x ^ dx) * quarter, quarter)
            scratch[pl.ds(at, quarter), :] = ref[dx * quarter : (dx + 1) * quarter, :].astype(F32)
    block = out.shape[1]
    for b in range(blocks):
        out[order_of(range(blocks), shard, b)] = scratch[b * block : (b + 1) * block, :].astype(BF)


def mix_place(info, own, recv, blocks):
    half_width = own.shape[1]
    return pl.pallas_call(
        partial(mix_place_kernel, blocks),
        out_shape=shape((blocks, 2 * half_width // blocks, half_width), BF),
        in_specs=[SMEM, VMEM, VMEM],
        out_specs=VMEM,
        scratch_shapes=[pltpu.VMEM((2 * half_width, half_width), F32)],
        compiler_params=params(8),
        cost_estimate=FREE,
        name="mix_place",
    )(info, own, recv)


def row_tiles(rows, step, body):
    lax.fori_loop(0, rows // step, lambda i, c: body(pl.ds(pl.multiple_of(i * step, step), step), c), 0)


def mean_of(value):
    return jnp.mean(value, -1, keepdims=True)


def first_norm_kernel(tokens, mixed, recv, vectors, low, normed_out, inverse_out):
    gain, bias = vectors[0:1, :], vectors[1:2, :]

    def body(at, carry):
        hidden = tokens[at, :].astype(F32) + mixed[at, :] + recv[at, :].astype(F32)
        centred = hidden - mean_of(hidden)
        inverse = lax.rsqrt(mean_of(centred * centred) + EPSILON)
        normed = centred * inverse
        normed_out[at, :] = normed
        inverse_out[at, :] = inverse
        low[at, :] = (normed * gain + bias).astype(BF)
        return carry

    row_tiles(tokens.shape[0], 128, body)


def first_norm(tokens, mixed, recv, vectors):
    rows, width = tokens.shape
    return pl.pallas_call(
        first_norm_kernel,
        grid=(1,),
        out_shape=(shape((rows, width), BF), shape((rows, width), F32), shape((rows, 1), F32)),
        in_specs=[pl.BlockSpec((rows, width), lambda i: (0, 0))] * 3
        + [pl.BlockSpec(vectors.shape, lambda i: (0, 0))],
        out_specs=(pl.BlockSpec((rows, width), lambda i: (0, 0)),) * 2
        + (pl.BlockSpec((rows, 1), lambda i: (0, 0)),),
        compiler_params=params(24),
        cost_estimate=FREE,
        name="first_norm",
    )(tokens, mixed, recv, vectors)


def second_norm_kernel(normed_one, mlp, recv, vectors, grad, result, grad_two, grad_low, sums):
    gain_one, bias_one = vectors[0:1, :], vectors[1:2, :]
    gain, bias = vectors[2:3, :], vectors[3:4, :]
    sums[...] = jnp.zeros_like(sums)

    def body(at, carry):
        hidden = normed_one[at, :] * gain_one + bias_one + mlp[at, :] + recv[at, :].astype(F32)
        centred = hidden - mean_of(hidden)
        inverse = lax.rsqrt(mean_of(centred * centred) + EPSILON)
        normed = centred * inverse
        result[at, :] = (normed * gain + bias).astype(BF)
        grad_y = grad[at, :].astype(F32)
        grad_n = grad_y * gain
        value = inverse * (grad_n - mean_of(grad_n) - normed * mean_of(grad_n * normed))
        grad_two[at, :] = value
        grad_low[at, :] = value.astype(BF)
        sums[2:3, :] += jnp.sum(grad_y * normed, 0, keepdims=True)
        sums[3:4, :] += jnp.sum(grad_y, 0, keepdims=True)
        return carry

    row_tiles(grad.shape[0], 128, body)


def second_norm(normed_one, mlp, recv, vectors, grad):
    rows, width = grad.shape
    return pl.pallas_call(
        second_norm_kernel,
        out_shape=(
            shape((rows, width), BF),
            shape((rows, width), F32),
            shape((rows, width), BF),
            shape((8, width), F32),
        ),
        in_specs=[VMEM] * 5,
        out_specs=(VMEM,) * 4,
        compiler_params=params(24),
        cost_estimate=FREE,
        name="second_norm",
    )(normed_one, mlp, recv, vectors, grad)


def first_back_kernel(grad_two, own, recv, normed_one, inverse_one, vectors, late, grad_one, grad_low, sums):
    gain = vectors[0:1, :]
    sums[...] = late[...]

    def body(at, carry):
        normed = normed_one[at, :]
        grad_y = grad_two[at, :] + own[at, :] + recv[at, :].astype(F32)
        grad_n = grad_y * gain
        value = inverse_one[at, :] * (grad_n - mean_of(grad_n) - normed * mean_of(grad_n * normed))
        grad_one[at, :] = value
        grad_low[at, :] = value.astype(BF)
        sums[0:1, :] += jnp.sum(grad_y * normed, 0, keepdims=True)
        sums[1:2, :] += jnp.sum(grad_y, 0, keepdims=True)
        return carry

    row_tiles(grad_two.shape[0], 128, body)


def first_back(grad_two, own, recv, normed_one, inverse_one, vectors, late):
    rows, width = grad_two.shape
    return pl.pallas_call(
        first_back_kernel,
        out_shape=(shape((rows, width), F32), shape((rows, width), BF), shape((8, width), F32)),
        in_specs=[VMEM] * 7,
        out_specs=(VMEM,) * 3,
        compiler_params=params(24),
        cost_estimate=FREE,
        name="first_back",
    )(grad_two, own, recv, normed_one, inverse_one, vectors, late)


def after(value, *earlier):
    return lax.optimization_barrier((value,) + earlier)[0]


def shards(
    n_shard,
    tokens,
    segment_ids,
    qkv_weight,
    out_weight,
    up_weight,
    down_weight,
    first_gain,
    first_bias,
    second_gain,
    second_bias,
    out_grad,
):
    rows, width = tokens.shape
    half_width = width // 2
    quarter = width // 4
    ff_half = up_weight.shape[1] // 2
    block = qkv_weight.shape[0]
    shard = lax.axis_index("shard").astype(jnp.int32)
    seq = lax.axis_index("seq").astype(jnp.int32)
    xb, cb = seq // 2, seq % 2
    bits = [1 << b for b in range(n_shard.bit_length() - 1)]
    top = bits[-1]
    owner = (shard // top) % 2 == cb
    low_shard = shard % top
    place = jnp.stack([xb, cb, shard])

    def swap(value, mask):
        return lax.ppermute(value, "shard", [(i, i ^ mask) for i in range(n_shard)])

    def swap_core(value):
        return lax.ppermute(value, "seq", [(i, i ^ 1) for i in range(4)])

    def swap_x(value):
        return lax.ppermute(value, "seq", [(i, i ^ 2) for i in range(4)])

    def to_core(value, to_owner):
        pairs = []
        for sh in range(n_shard):
            for se in range(4):
                if (sh // top == se % 2) != to_owner:
                    pairs.append((sh * 4 + se, (sh ^ top) * 4 + se))
        return lax.ppermute(value, ("shard", "seq"), pairs)

    def join(pieces):
        return jnp.concatenate(pieces) if len(pieces) > 1 else pieces[0]

    class Gather:
        def __init__(self, own_block, over):
            self.pieces, self.offsets, self.over = [own_block[None]], [[0]], list(over)

        def swap(self, value, rel, bit):
            got = swap(value, bit)
            self.pieces.append(got)
            self.offsets.append([r ^ bit for r in rel])
            return got

        def steps(self, count, *gate):
            for bit in [self.over.pop(0) for _ in range(count)]:
                held, rel = join(self.pieces), [r for o in self.offsets for r in o]
                self.pieces, self.offsets = [held], [rel]
                gate = (self.swap(after(held, *gate), rel, bit),)
            return gate[0]

        def part(self, index, *gate):
            return self.swap(after(self.pieces[index], *gate), self.offsets[index], self.over[0])

    def fold(value, got):
        return (value[: value.shape[0] // 2].astype(F32) + got.astype(F32)).astype(BF)

    def upper(value):
        return value[value.shape[0] // 2 :]

    def add_x(value):
        return (value.astype(F32) + swap_x(value).astype(F32)).astype(BF)

    def pick(value, flag, axis):
        return jnp.where(
            flag == 0,
            lax.index_in_dim(value, 0, axis, False),
            lax.index_in_dim(value, 1, axis, False),
        )

    def ordered(flag, own, other, axis):
        return jnp.where(
            flag == 0, jnp.concatenate([own, other], axis), jnp.concatenate([other, own], axis)
        )

    over_x = swap_x(tokens)
    over_core = swap_core(tokens)
    toks = [tokens, over_core, over_x, swap_core(over_x)]
    ids = segment_ids[0]
    length = ids.shape[0]
    tiles = length // TILE
    first = ids.reshape(tiles, TILE)[:, 0]
    last = ids.reshape(tiles, TILE)[:, -1]
    begin = jnp.sum((ids[None] < first[:, None]).astype(jnp.int32), 1) // TILE
    end = (jnp.sum((ids[None] <= last[:, None]).astype(jnp.int32), 1) + TILE - 1) // TILE
    info = jnp.concatenate([begin, end, seq[None], shard[None]])
    chunks = ids.reshape(2, 2, 1, rows)
    chunks = jnp.where(xb == 0, chunks, chunks[::-1])
    chunks = jnp.where(cb == 0, chunks, chunks[:, ::-1])
    ids_row = chunks.reshape(1, length)

    own_a, own_b = prepare(
        place, qkv_weight, out_weight, (first_gain, first_bias, second_gain, second_bias)
    )
    up_half = lax.dynamic_slice_in_dim(up_weight, cb * ff_half, ff_half, 1)
    middle = len(bits) - 2
    gather_a = Gather(own_a, bits[::-1])
    gather_b = Gather(own_b, bits[::-1])
    gather_up = Gather(up_half, bits[::-1])
    a1 = gather_a.steps(1)
    b1 = gather_b.steps(1, a1)
    a2 = gather_a.steps(middle)
    a3 = gather_a.steps(1)
    b2 = gather_b.steps(middle, a2)
    u1 = gather_up.steps(1, b1)
    b3 = gather_b.steps(1, a3)
    down_there = to_core(after(down_weight, u1), False)
    part_a = assemble(gather_a.pieces, gather_a.offsets, shard)
    vectors = vectors_of(part_a)

    saved, own_ctx, other_ctx = [], [], []

    def head(j, weight, *gate):
        ctx_own, ctx_send, ctx_full, lse = attend(info, toks, weight, after(ids_row, *gate))
        own_ctx.append(ctx_own)
        other_ctx.append(swap_x(ctx_send))
        saved.append((ctx_full, lse))
        return ctx_own

    ctx = head(0, part_a[:, :TRIO], b2, vectors)
    u1, down_there = after(u1, ctx), after(down_there, ctx)
    gather_up.pieces[1] = u1
    gather_down = Gather(jnp.where(owner, down_weight, down_there), bits[-2::-1])
    u2 = gather_up.steps(middle, b2)
    ua = gather_up.part(0, b3)
    part_b = assemble(gather_b.pieces, gather_b.offsets, shard)
    ctx = head(1, part_b[:, :TRIO], u1, down_there)
    u2 = after(u2, ctx)
    gather_up.pieces[1] = u2
    d2 = gather_down.steps(middle, u2)
    ub = gather_up.part(1, ua)
    ctx = head(2, part_b[:, TRIO : 2 * TRIO], u2)
    d2 = after(d2, ctx)
    gather_down.pieces[1] = d2
    da = gather_down.part(0, ub)
    db = gather_down.part(1, da)
    widen = assemble(gather_up.pieces, gather_up.offsets, shard)
    narrow = assemble(gather_down.pieces, gather_down.offsets, low_shard)
    head_weights = [part_a[:, :TRIO], part_b[:, :TRIO], part_b[:, TRIO : 2 * TRIO]]
    mixer = part_b[:, 2 * TRIO :].reshape(2, half_width, half_width)
    mixer = ordered(cb, pick(mixer, cb, 0), swap_core(pick(mixer, 1 - cb, 0)), 1)
    mixer = jnp.where(xb == 0, mixer, jnp.concatenate([mixer[quarter:], mixer[:quarter]]))
    context = jnp.concatenate(own_ctx + other_ctx)

    mixed = dot(context, mixer, 0, 0)
    low_own, normed_one, inverse_one = first_norm(
        tokens, mixed, swap_core(mixed[rows:].astype(BF)), vectors
    )
    act_low, act_t, slope, low_t = feed_up(low_own, swap_core(low_own), widen)
    mlp_own, mlp_send = feed_down(act_low, narrow)
    result, grad_two, grad_mlp, late = second_norm(
        normed_one, mlp_own, swap_core(mlp_send), vectors, out_grad
    )

    grad_mlp = [grad_mlp, swap_core(grad_mlp)]
    narrow_grad = weight_grad(low_shard, act_t, grad_mlp, n_shard // 2)
    n1 = swap(upper(narrow_grad), bits[0])
    first_own, first_send, grad_pre = feed_back(
        after(grad_mlp[0], narrow_grad), grad_mlp[1], slope, widen, narrow
    )
    grad_one, grad_attn, sums = first_back(
        grad_two, first_own, swap_core(first_send), normed_one, inverse_one, vectors, late
    )
    g_own, g_send, mixer_own, mixer_send = mix_back(
        place, mixer, context, grad_attn, swap_core(grad_attn)
    )
    g_recv = swap_x(g_send)
    widen_grad = weight_grad(shard, after(low_t, g_send), [grad_pre], n_shard)
    w1 = swap(upper(widen_grad), bits[0])
    mixer_grad = mix_place(place, mixer_own, swap_core(mixer_send), n_shard)

    def head_back(j, *gate):
        at = j * HEAD_DIM
        return attend_back(
            info, toks, head_weights[j], after(ids_row, *gate),
            g_own[at : at + HEAD_DIM], g_recv[at : at + HEAD_DIM], *saved[j],
            sums if j == 2 else None, n_shard,
        )

    grads, parts = [None] * 3, [None] * 3
    narrow_grad = fold(narrow_grad, after(n1, widen_grad, mixer_grad))
    n2 = swap(upper(narrow_grad), bits[1])
    grads[0], parts[0] = head_back(0, narrow_grad)
    narrow_grad = fold(narrow_grad, after(n2, grads[0]))
    for bit in bits[2:-1]:
        narrow_grad = fold(narrow_grad, swap(upper(narrow_grad), bit))
    narrow_grad = narrow_grad[0]
    n3 = to_core(narrow_grad, True)
    grads[1], parts[1] = head_back(1, narrow_grad)
    widen_grad = fold(widen_grad, after(w1, grads[1]))
    w2 = swap(upper(widen_grad), bits[1])
    early = jnp.concatenate([mixer_grad, parts[0], parts[1]], 2)
    e1 = swap(upper(early), bits[0])
    narrow_grad = (narrow_grad.astype(F32) + after(n3, grads[1]).astype(F32)).astype(BF)
    n4 = swap_x(narrow_grad)
    grads[2], parts[2] = head_back(2, narrow_grad, widen_grad, early)
    late = parts[2]
    l1 = swap(upper(late), bits[0])
    widen_grad = fold(widen_grad, after(w2, grads[2]))
    for bit in bits[2:-1]:
        widen_grad = fold(widen_grad, swap(upper(widen_grad), bit))
    w3 = swap(upper(widen_grad), bits[-1])
    back_own, back_x, back_core = input_back(grads, head_weights, rows)
    back_recv = swap_core(back_core)
    back_x = (back_x + back_recv[1].astype(F32)).astype(BF)
    back_far = swap_x(back_x)
    early = fold(early, after(e1, back_x))
    e2 = swap(upper(early), bits[1])
    late = fold(late, after(l1, early))
    l2 = swap(upper(late), bits[1])
    early = fold(early, after(e2, late))
    for bit in bits[2:-1]:
        early = fold(early, swap(upper(early), bit))
    e3 = swap(upper(early), bits[-1])
    late = fold(late, after(l2, early))
    for bit in bits[2:-1]:
        late = fold(late, swap(upper(late), bit))
    l3 = swap(upper(late), bits[-1])
    widen_grad = fold(widen_grad, after(w3, late))
    widen_grad = add_x(widen_grad[0])
    early, late = fold(early, e3)[0], fold(late, l3)[0]
    narrow_grad = (narrow_grad.astype(F32) + n4.astype(F32)).astype(BF)
    narrow_grad = jnp.where(owner, narrow_grad, swap_core(narrow_grad))
    widen_grad = ordered(cb, widen_grad, swap_core(widen_grad), 1)
    input_grad = grad_one + back_own + back_recv[0].astype(F32) + back_far.astype(F32)

    mixer_grad = add_x(early[:, :half_width])
    mixer_grad = ordered(cb, mixer_grad, swap_core(mixer_grad), 1)
    mine = jnp.concatenate([early[:, half_width:], late], 1)
    theirs = swap_x(mine)
    qkv_grad, sums = place_qkv(place, mine, theirs, swap_core(mine), swap_core(theirs), width)
    return (
        result,
        input_grad,
        qkv_grad,
        mixer_grad.astype(F32),
        widen_grad.astype(F32),
        narrow_grad.astype(F32),
        sums[:, 0],
        sums[:, 1],
        sums[:, 2],
        sums[:, 3],
    )


def solution(mesh):
    placed = (
        P(("shard", "seq"), None),
        P("shard", None),
        P("shard", None),
        P("shard", None),
        P("shard", None),
        P("shard", None),
        P("shard"),
        P("shard"),
        P("shard"),
        P("shard"),
        P(("shard", "seq"), None),
    )
    return jax.shard_map(
        partial(shards, mesh.shape["shard"]),
        mesh=mesh,
        in_specs=placed,
        out_specs=(
            P(("shard", "seq"), None),
            P(("shard", "seq"), None),
            P("shard", None),
            P("shard", None),
            P("shard", None),
            P("shard", None),
            P("shard"),
            P("shard"),
            P("shard"),
            P("shard"),
        ),
        check_vma=False,
    )
```

```python
from functools import partial

import jax
import jax.numpy as jnp
from jax import lax
from jax.experimental import pallas as pl
from jax.experimental.pallas import tpu as pltpu
from jax.sharding import PartitionSpec as P

HEADS = 12
HEAD_DIM = 64
TRIO = 3 * HEAD_DIM
GROUPS = 16
EPSILON = 1e-12
FAR = -(2.0**30)
SCALE = HEAD_DIM**-0.5
TILE = 256
UNROLL = 2
BF = jnp.bfloat16
F32 = jnp.float32
VMEM = pl.BlockSpec(memory_space=pltpu.VMEM)
SMEM = pl.BlockSpec(memory_space=pltpu.SMEM)
FREE = pl.CostEstimate(flops=1, bytes_accessed=1, transcendentals=0)


def dot(a, b, ca, cb):
    return lax.dot_general(a, b, (((ca,), (cb,)), ((), ())), preferred_element_type=F32)


def shape(dims, kind):
    return jax.ShapeDtypeStruct(dims, kind)


def params(mebi):
    return pltpu.CompilerParams(vmem_limit_bytes=mebi << 20)


def assemble_kernel(offsets, info, *refs):
    out, sem = refs[-2:]
    copies = []
    for ref, rel in zip(refs[:-2], offsets):
        block = ref.shape[1]
        for i, r in enumerate(rel):
            at = pl.multiple_of((info[0] ^ r) * block, block)
            copies.append(
                pltpu.make_async_copy(ref.at[i], out.at[pl.ds(at, block), :], sem.at[len(copies)])
            )
    for copy in copies:
        copy.start()
    for copy in copies:
        copy.wait()


def assemble(pieces, offsets, me):
    block, cols = pieces[0].shape[1:]
    count = sum(len(r) for r in offsets)
    if block % 16:
        value = jnp.concatenate(pieces)
        order = [r for rel in offsets for r in rel]
        place = jnp.array([order.index(r) for r in range(count)], jnp.int32)
        return value[place[me ^ jnp.arange(count)]].reshape(count * block, cols)
    return pl.pallas_call(
        partial(assemble_kernel, offsets),
        out_shape=shape((count * block, cols), BF),
        in_specs=[SMEM] + [pl.BlockSpec(memory_space=pl.ANY)] * len(pieces),
        out_specs=VMEM,
        scratch_shapes=[pltpu.SemaphoreType.DMA((count,))],
        compiler_params=params(12),
        cost_estimate=FREE,
        name="assemble",
    )(me[None], *pieces)


def prepare_kernel(info, qkv_far, out_far, *refs):
    vectors, (part_a, part_b, qkv, out_weight, rows, scratch, sem) = refs[:4], refs[4:]
    block, width = out_weight.shape
    half, quarter = width // 2, width // 4
    copies = [
        pltpu.make_async_copy(qkv_far, qkv, sem.at[0]),
        pltpu.make_async_copy(out_far, out_weight, sem.at[1]),
    ] + [pltpu.make_async_copy(v, rows.at[i], sem.at[2 + i]) for i, v in enumerate(vectors)]
    for copy in copies:
        copy.start()
    scratch[...] = jnp.zeros_like(scratch)
    for copy in copies:
        copy.wait()
    for i in range(4):
        scratch[i : i + 1, :block] = rows[i].astype(F32)
    part_a[:, TRIO:] = scratch[...].T[:block, : 256 - TRIO].astype(BF)
    for x in range(2):
        for c in range(2):

            @pl.when(jnp.logical_and(info[0] == x, info[1] == c))
            def _():
                at = c * half + x * quarter
                trio = [qkv[:, i * width + at : i * width + at + quarter] for i in range(3)]
                for j in range(3):
                    piece = jnp.concatenate(
                        [t[:, j * HEAD_DIM : (j + 1) * HEAD_DIM] for t in trio], 1
                    )
                    if j == 0:
                        part_a[:, :TRIO] = piece
                    else:
                        part_b[:, (j - 1) * TRIO : j * TRIO] = piece
                part_b[:, 2 * TRIO :] = out_weight[:, c * half : (c + 1) * half]


def prepare(info, qkv, out_weight, vectors):
    block, width = out_weight.shape
    far = [qkv, out_weight] + [v[None] for v in vectors]
    return pl.pallas_call(
        prepare_kernel,
        out_shape=(shape((block, 256), BF), shape((block, 2 * TRIO + width // 2), BF)),
        in_specs=[SMEM] + [pl.BlockSpec(memory_space=pltpu.HBM)] * 6,
        out_specs=(VMEM, VMEM),
        scratch_shapes=[
            pltpu.VMEM(qkv.shape, BF),
            pltpu.VMEM(out_weight.shape, BF),
            pltpu.VMEM((4, 1, block), BF),
            pltpu.VMEM((128, 128), F32),
            pltpu.SemaphoreType.DMA((6,)),
        ],
        compiler_params=params(8),
        cost_estimate=FREE,
        name="prepare",
    )(info, *[pltpu.with_memory_space_constraint(v, pltpu.HBM) for v in far])


def vectors_kernel(part, out):
    out[...] = part[:, 128:].astype(F32).T[TRIO - 128 : TRIO - 120]


def vectors_of(part):
    return pl.pallas_call(
        vectors_kernel,
        out_shape=shape((8, part.shape[0]), F32),
        in_specs=[VMEM],
        out_specs=VMEM,
        compiler_params=params(8),
        cost_estimate=FREE,
        name="vectors",
    )(part)


def doc_rows(ids_ref, same, other):
    ids = ids_ref[...]
    rows = lax.broadcasted_iota(jnp.int32, (GROUPS, ids.shape[1]), 0)
    return jnp.where(rows == ids, same, other).astype(BF)


def plan_kernel(ids_s, ids_v, place, plan, row):
    total = ids_v.shape[1]
    tiles = total // TILE
    chunk = total // 4
    me = place[0] * 2 + place[1]
    entries = (plan.shape[0] - 1) // 2
    for i in range(2 * entries):
        plan[1 + i] = jnp.int32(tiles)
    first = [ids_s[0, i * TILE] for i in range(tiles)]
    last = [ids_s[0, i * TILE + TILE - 1] for i in range(tiles)]
    flip = me * (chunk // TILE)
    count = jnp.int32(0)
    for i in range(tiles):
        for j in range(tiles):
            meet = jnp.logical_and(first[i] <= last[j], first[j] <= last[i])

            @pl.when(meet)
            def _():
                plan[1 + 2 * UNROLL + count] = i ^ flip
                plan[1 + entries + 2 * UNROLL + count] = j ^ flip

            count = count + meet.astype(jnp.int32)
    plan[0] = (count + UNROLL - 1) // UNROLL
    for r in range(4):
        at = pl.multiple_of((me ^ r) * chunk, chunk)
        row[:, r * chunk : (r + 1) * chunk] = ids_v[:, pl.ds(at, chunk)]


def make_plan(ids, place):
    total = ids.shape[1]
    entries = (total // TILE) ** 2 + 4 * UNROLL
    return pl.pallas_call(
        plan_kernel,
        out_shape=(shape((1 + 2 * entries,), jnp.int32), shape((1, total), jnp.int32)),
        in_specs=[SMEM, VMEM, SMEM],
        out_specs=(SMEM, VMEM),
        compiler_params=params(8),
        cost_estimate=FREE,
        name="plan",
    )(ids, ids, place)


def tile_of(plan, entry):
    return pl.multiple_of(plan[1 + entry] * TILE, TILE)


def attend_kernel(
    plan, tok0, tok1, tok2, tok3, weight, ids_ref, ctx_own, ctx_send, ctx_full, lse,
    q_t, k_nat, v_t, s_ref, p_ref, fade, top, sums, acc,
):
    total = ids_ref.shape[1]
    half = total // 2
    entries = (plan.shape[0] - 1) // 2
    weight_t = weight[...].T
    keys = weight[:, HEAD_DIM : 2 * HEAD_DIM]
    for i, tok in enumerate((tok0, tok1, tok2, tok3)):
        rows = tok[...]
        at, end = i * rows.shape[0], (i + 1) * rows.shape[0]
        trio = dot(weight_t, rows, 1, 1).astype(BF)
        q_t[:HEAD_DIM, at:end] = trio[:HEAD_DIM] * SCALE
        v_t[:, at:end] = trio[2 * HEAD_DIM :]
        k_nat[at:end, :HEAD_DIM] = dot(rows, keys, 1, 0).astype(BF)
    q_t[HEAD_DIM : HEAD_DIM + GROUPS, :total] = doc_rows(ids_ref, 0.0, FAR)
    q_t[HEAD_DIM + GROUPS :, :total] = jnp.zeros((128 - HEAD_DIM - GROUPS, total), BF)
    docs = jnp.concatenate(
        [doc_rows(ids_ref, 1.0, 0.0), jnp.zeros((128 - HEAD_DIM - GROUPS, total), BF)], 0
    )
    k_nat[:total, HEAD_DIM:] = docs.T
    top[...] = jnp.full_like(top, -3e38)
    sums[...] = jnp.zeros_like(sums)
    acc[...] = jnp.zeros_like(acc)

    def step(j, carry):
        i = j * UNROLL
        for u in range(UNROLL):
            q, k = tile_of(plan, i + u), tile_of(plan, entries + i + u)
            acc[:, pl.ds(q, TILE)] = acc[:, pl.ds(q, TILE)] * fade[u] + dot(
                v_t[:, pl.ds(k, TILE)], p_ref[u], 1, 0
            )
        peaks = [jnp.max(s_ref[u], 0, keepdims=True) for u in range(UNROLL)]
        for u in range(UNROLL):
            q = tile_of(plan, i + UNROLL + u)
            old = top[:, pl.ds(q, TILE)]
            new = jnp.maximum(old, peaks[u])
            powers = jnp.exp(s_ref[u] - new)
            decay = jnp.exp(old - new)
            top[:, pl.ds(q, TILE)] = new
            sums[:, pl.ds(q, TILE)] = sums[:, pl.ds(q, TILE)] * decay + jnp.sum(
                powers, 0, keepdims=True
            )
            fade[u] = decay
            p_ref[u] = powers.astype(BF)
        for u in range(UNROLL):
            q = tile_of(plan, i + 2 * UNROLL + u)
            k = tile_of(plan, entries + i + 2 * UNROLL + u)
            s_ref[u] = dot(k_nat[pl.ds(k, TILE), :], q_t[:, pl.ds(q, TILE)], 1, 0)
        return carry

    lax.fori_loop(0, plan[0] + 2, step, 0)
    ctx_full[...] = acc[:, :total] / sums[:, :total]
    lse[...] = top[:, :total] + jnp.log(sums[:, :total])
    ctx_own[...] = ctx_full[:, :half].astype(BF)
    ctx_send[...] = ctx_full[:, half:].astype(BF)


def attend(plan, toks, weight, ids):
    total = ids.shape[1]
    half = total // 2
    padded = total + TILE
    return pl.pallas_call(
        attend_kernel,
        out_shape=(
            shape((HEAD_DIM, half), BF),
            shape((HEAD_DIM, half), BF),
            shape((HEAD_DIM, total), F32),
            shape((1, total), F32),
        ),
        in_specs=[SMEM] + [VMEM] * 6,
        out_specs=(VMEM,) * 4,
        scratch_shapes=[
            pltpu.VMEM((128, padded), BF),
            pltpu.VMEM((padded, 128), BF),
            pltpu.VMEM((HEAD_DIM, padded), BF),
            pltpu.VMEM((UNROLL, TILE, TILE), F32),
            pltpu.VMEM((UNROLL, TILE, TILE), BF),
            pltpu.VMEM((UNROLL, 1, TILE), F32),
            pltpu.VMEM((1, padded), F32),
            pltpu.VMEM((1, padded), F32),
            pltpu.VMEM((HEAD_DIM, padded), F32),
        ],
        compiler_params=params(20),
        cost_estimate=FREE,
        name="attend",
    )(plan, *toks, weight, ids)


def attend_back_kernel(
    order, plan, place, tok0, tok1, tok2, tok3, weight, ids_ref, g_own, g_recv, ctx_full, lse_in,
    sums, keep, send, grad_out,
    q_t, kvd, k_t, g_t, qg_nat, lse, row_term, s_ref, d_ref, p_ref, e_ref, acc, dq_t, w_grad, out,
):
    total = ids_ref.shape[1]
    half = total // 2
    entries = (plan.shape[0] - 1) // 2
    toks = (tok0, tok1, tok2, tok3)
    chunk = tok0.shape[0]
    weight_t = weight[:, : 2 * HEAD_DIM].T
    natural_w = weight[:, HEAD_DIM:]
    for at, grad in ((0, g_own), (half, g_recv)):
        g_t[HEAD_DIM:, at : at + half] = grad[...]
    g_t[:HEAD_DIM, :total] = jnp.zeros((HEAD_DIM, total), BF)
    for i, tok in enumerate(toks):
        at, end = i * chunk, (i + 1) * chunk
        rows = tok[...]
        pair = dot(weight_t, rows, 1, 1).astype(BF)
        q_t[:HEAD_DIM, at:end] = pair[:HEAD_DIM] * SCALE
        k_t[:, at:end] = pair[HEAD_DIM:]
        kvd[at:end, :128] = dot(rows, natural_w, 1, 0).astype(BF)
    qg_nat[:total, :] = jnp.concatenate([q_t[:HEAD_DIM, :total], g_t[HEAD_DIM:, :total]], 0).T
    q_t[HEAD_DIM:128, :total] = jnp.zeros((128 - HEAD_DIM, total), BF)
    q_t[128 : 128 + GROUPS, :total] = doc_rows(ids_ref, 0.0, FAR)
    q_t[128 + GROUPS :, :total] = jnp.zeros((128 - GROUPS, total), BF)
    kvd[:total, 128:] = jnp.concatenate(
        [doc_rows(ids_ref, 1.0, 0.0), jnp.zeros((128 - GROUPS, total), BF)], 0
    ).T
    acc[...] = jnp.zeros_like(acc)
    dq_t[...] = jnp.zeros_like(dq_t)
    lse[:, :total] = lse_in[...]
    row_term[:, :total] = jnp.sum(
        ctx_full[...] * g_t[HEAD_DIM:, :total].astype(F32), 0, keepdims=True
    )
    left = lax.broadcasted_iota(jnp.int32, (TILE, 128), 1) < HEAD_DIM

    def step(j, carry):
        i = j * UNROLL
        for u in range(UNROLL):
            q, k = tile_of(plan, i + u), tile_of(plan, entries + i + u)
            grad_scores, chance = e_ref[u], p_ref[u]
            natural = qg_nat[pl.ds(q, TILE), :]
            dq_t[:, pl.ds(q, TILE)] += dot(k_t[:, pl.ds(k, TILE)], grad_scores, 1, 0)
            acc[pl.ds(k, TILE), :] += jnp.where(
                left, dot(grad_scores, natural, 1, 0), dot(chance, natural, 1, 0)
            )
        for u in range(UNROLL):
            q = tile_of(plan, i + UNROLL + u)
            chance = jnp.exp(s_ref[u] - lse[:, pl.ds(q, TILE)])
            p_ref[u] = chance.astype(BF)
            e_ref[u] = (chance * (d_ref[u] - row_term[:, pl.ds(q, TILE)])).astype(BF)
        for u in range(UNROLL):
            q = tile_of(plan, i + 2 * UNROLL + u)
            rows = kvd[pl.ds(tile_of(plan, entries + i + 2 * UNROLL + u), TILE), :]
            s_ref[u] = dot(rows, q_t[:, pl.ds(q, TILE)], 1, 0)
            d_ref[u] = dot(rows[:, :128], g_t[:, pl.ds(q, TILE)], 1, 0)
        return carry

    lax.fori_loop(0, plan[0] + 2, step, 0)
    out[:HEAD_DIM, :] = (dq_t[:, :total] * SCALE).astype(BF)
    out[HEAD_DIM:, :] = acc[:total, :].T.astype(BF)
    keep[...] = out[:, :half]
    send[...] = out[:, half:]
    for i, tok in enumerate(toks):
        part = dot(out[:, i * chunk : (i + 1) * chunk], tok[...], 1, 0)
        w_grad[:TRIO, :] = part if i == 0 else w_grad[:TRIO, :] + part
    if sums is not None:
        w_grad[TRIO : TRIO + 8, :] = sums[...]
        w_grad[TRIO + 8 :, :] = jnp.zeros((256 - TRIO - 8, w_grad.shape[1]), F32)
    else:
        w_grad[TRIO:, :] = jnp.zeros((256 - TRIO, w_grad.shape[1]), F32)
    natural = w_grad[...].T
    block = grad_out.shape[1]
    for b in range(len(order)):
        grad_out[order_of(order, place[2], b)] = natural[b * block : (b + 1) * block].astype(BF)


def order_of(order, me, b):
    rel = me ^ b
    bits = len(order).bit_length() - 1
    place = 0
    for i in range(bits):
        place = place | (((rel >> i) & 1) << (bits - 1 - i))
    return place


def attend_back(plan, place, toks, weight, ids, g_own, g_recv, ctx_full, lse, sums, n_shard):
    total = ids.shape[1]
    width = weight.shape[0]
    padded = total + TILE
    extra = [] if sums is None else [sums]

    def kernel(*refs):
        refs = list(refs)
        if sums is None:
            refs.insert(12, None)
        attend_back_kernel(range(n_shard), *refs)

    return pl.pallas_call(
        kernel,
        out_shape=(shape((TRIO, total // 2), BF),) * 2
        + (shape((n_shard, width // n_shard, 256), BF),),
        in_specs=[SMEM, SMEM] + [VMEM] * (10 + len(extra)),
        out_specs=(VMEM,) * 3,
        scratch_shapes=[
            pltpu.VMEM((256, padded), BF),
            pltpu.VMEM((padded, 256), BF),
            pltpu.VMEM((HEAD_DIM, padded), BF),
            pltpu.VMEM((128, padded), BF),
            pltpu.VMEM((padded, 128), BF),
            pltpu.VMEM((1, padded), F32),
            pltpu.VMEM((1, padded), F32),
            pltpu.VMEM((UNROLL, TILE, TILE), F32),
            pltpu.VMEM((UNROLL, TILE, TILE), F32),
            pltpu.VMEM((UNROLL, TILE, TILE), BF),
            pltpu.VMEM((UNROLL, TILE, TILE), BF),
            pltpu.VMEM((padded, 128), F32),
            pltpu.VMEM((HEAD_DIM, padded), F32),
            pltpu.VMEM((256, width), F32),
            pltpu.VMEM((TRIO, total), BF),
        ],
        compiler_params=params(24),
        cost_estimate=FREE,
        name="attend_back",
    )(plan, place, *toks, weight, ids, g_own, g_recv, ctx_full, lse, *extra)


def input_back_kernel(*refs):
    grads, weights, (own, send) = refs[:6], refs[6:12], refs[12:]
    rows = own.shape[0]
    wide = jnp.concatenate([w[:, :TRIO] for w in weights], 1)
    for r, out in enumerate((own, send)):
        rows_t = jnp.concatenate([d[:, r * rows : (r + 1) * rows] for d in grads], 0)
        out[...] = dot(rows_t.T, wide, 1, 1).astype(out.dtype)


def input_back(grads, weights, rows):
    width = weights[0].shape[0]
    return pl.pallas_call(
        input_back_kernel,
        out_shape=(shape((rows, width), F32), shape((rows, width), BF)),
        in_specs=[VMEM] * 12,
        out_specs=(VMEM,) * 2,
        compiler_params=params(24),
        cost_estimate=FREE,
        name="input_back",
    )(*grads, *weights)


def place_qkv_kernel(start, info, chip, other, out, sums_out):
    part = out.shape[1] // 3
    quarter = part // 4
    x, c = info[0], info[1]
    total = None
    for ref, dc in ((chip, 0), (other, 1)):
        for dx in range(2):
            value = ref[:, start + dx * 768 : start + (dx + 1) * 768].astype(F32)
            tail = value[:, 2 * 256 + TRIO : 2 * 256 + TRIO + 8]
            total = tail if total is None else total + tail
            for sec in range(3):
                at = sec * HEAD_DIM
                piece = jnp.concatenate(
                    [value[:, j * 256 + at : j * 256 + at + HEAD_DIM] for j in range(3)], 1
                )
                for xv in range(2):
                    for cv in range(2):
                        to = sec * part + (cv * 2 + xv) * quarter

                        @pl.when(jnp.logical_and((x ^ dx) == xv, (c ^ dc) == cv))
                        def _():
                            out[:, to : to + quarter] = piece

    sums_out[...] = total


def place_qkv(info, chip, other, start, width):
    block = chip.shape[0]
    return pl.pallas_call(
        partial(place_qkv_kernel, start),
        out_shape=(shape((block, 3 * width), F32), shape((block, 8), F32)),
        in_specs=[SMEM] + [VMEM] * 2,
        out_specs=(VMEM, VMEM),
        compiler_params=params(8),
        cost_estimate=FREE,
        name="place_qkv",
    )(info, chip, other)


def gelu_both(u):
    root = 0.7978845608028654
    cube = 0.044715 * root
    square = u * u
    t = jnp.tanh(u * (root + cube * square))
    half = 0.5 * (1.0 + t)
    act = u * half
    slope = half + act * (1.0 - t) * (root + 3.0 * cube * square)
    return act, slope


def feed_up_kernel(low0, low1, low2, low3, up, act_out, act_t, slope_out, low_t, low):
    step = low0.shape[0]
    for p, piece in enumerate((low0, low1, low2, low3)):
        low[p * step : (p + 1) * step, :] = piece[...]

    def body(i, carry):
        at = pl.multiple_of(i * step, step)
        value = low[pl.ds(at, step), :]
        low_t[:, pl.ds(at, step)] = value.T
        act, slope = gelu_both(dot(value, up[...], 1, 0))
        act = act.astype(BF)
        act_out[pl.ds(at, step), :] = act
        act_t[:, pl.ds(at, step)] = act.T
        slope_out[pl.ds(at, step), :] = slope.astype(BF)
        return carry

    lax.fori_loop(0, 4, body, 0)


def feed_up(lows, up):
    rows, width = lows[0].shape
    hidden = up.shape[1]
    return pl.pallas_call(
        feed_up_kernel,
        out_shape=(
            shape((4 * rows, hidden), BF),
            shape((hidden, 4 * rows), BF),
            shape((4 * rows, hidden), BF),
            shape((width, 4 * rows), BF),
        ),
        in_specs=[VMEM] * 5,
        out_specs=(VMEM,) * 4,
        scratch_shapes=[pltpu.VMEM((4 * rows, width), BF)],
        compiler_params=params(32),
        cost_estimate=FREE,
        name="feed_up",
    )(*lows, up)


def feed_down_kernel(act, down, own, send):
    rows = own.shape[0]
    step = 256
    for p, out in enumerate((own, send)):

        def body(i, carry):
            at = pl.multiple_of(i * step, step)
            value = act[pl.ds(pl.multiple_of(p * rows + i * step, step), step), :]
            out[pl.ds(at, step), :] = dot(value, down[...], 1, 0).astype(out.dtype)
            return carry

        lax.fori_loop(0, rows // step, body, 0)


def feed_down(act, down):
    rows, hidden = act.shape
    width = down.shape[1]
    return pl.pallas_call(
        feed_down_kernel,
        out_shape=(shape((rows // 2, width), F32), shape((rows // 2, width), BF)),
        in_specs=[VMEM] * 2,
        out_specs=(VMEM,) * 2,
        compiler_params=params(24),
        cost_estimate=FREE,
        name="feed_down",
    )(act, down)


def feed_back_kernel(grad_own, grad_other, slope, up, down, own, send0, send1, pre_out, send):
    rows = grad_own.shape[0]
    step = 256
    for p, (grad, out) in enumerate(((grad_own, own), (grad_other, send))):

        def body(i, carry):
            at = pl.multiple_of(i * step, step)
            to = pl.multiple_of(p * rows + i * step, step)
            pre = dot(grad[pl.ds(at, step), :], down[...], 1, 1)
            pre = (pre * slope[pl.ds(to, step), :].astype(F32)).astype(BF)
            pre_out[pl.ds(to, step), :] = pre
            out[pl.ds(at, step), :] = dot(pre, up[...], 1, 1).astype(out.dtype)
            return carry

        lax.fori_loop(0, rows // step, body, 0)
    send0[...] = send[: rows // 2, :]
    send1[...] = send[rows // 2 :, :]


def feed_back(grad_own, grad_other, slope, up, down):
    rows, width = grad_own.shape
    hidden = up.shape[1]
    return pl.pallas_call(
        feed_back_kernel,
        out_shape=(
            shape((rows, width), F32),
            shape((rows // 2, width), BF),
            shape((rows // 2, width), BF),
            shape((2 * rows, hidden), BF),
        ),
        in_specs=[VMEM] * 5,
        out_specs=(VMEM,) * 4,
        scratch_shapes=[pltpu.VMEM((rows, width), BF)],
        compiler_params=params(32),
        cost_estimate=FREE,
        name="feed_back",
    )(grad_own, grad_other, slope, up, down)


def weight_grad_kernel(blocks, reverse, shard, left, right_own, right_other, out):
    rows, cols = left.shape[0], out.shape[2]
    half = left.shape[1] // 2
    step = 256
    block = out.shape[1]
    lone = right_other is None

    def body(i, carry):
        at = pl.multiple_of(i * step, step)
        if lone:
            value = dot(left[...], right_own[:, pl.ds(at, step)], 1, 0)
        else:
            value = dot(left[:, :half], right_own[:, pl.ds(at, step)], 1, 0) + dot(
                left[:, half:], right_other[:, pl.ds(at, step)], 1, 0
            )
        for b in range(blocks):
            to = order_of(range(blocks), shard[0], b) if reverse else shard[0] ^ b
            out[to, :, pl.ds(at, step)] = value[
                b * block : (b + 1) * block
            ].astype(BF)
        return carry

    lax.fori_loop(0, cols // step, body, 0)


def weight_grad(shard, left, rights, blocks, reverse=True):
    rows, cols = left.shape[0], rights[0].shape[1]

    def kernel(*refs):
        refs = list(refs)
        if len(rights) == 1:
            refs.insert(3, None)
        weight_grad_kernel(blocks, reverse, *refs)

    return pl.pallas_call(
        kernel,
        out_shape=shape((blocks, rows // blocks, cols), BF),
        in_specs=[SMEM, VMEM] + [VMEM] * len(rights),
        out_specs=VMEM,
        compiler_params=params(24),
        cost_estimate=FREE,
        name="weight_grad",
    )(shard[None], left, *rights)


def mix_back_kernel(info, mixer, context, grad0, grad1, grad2, grad3, g_own, g_send, own, send):
    quarter = g_own.shape[0]
    rows = grad0.shape[0]
    half_width = own.shape[1]
    grads = (grad0, grad1, grad2, grad3)
    for p, grad in enumerate(grads):
        value = dot(mixer[...], grad[...], 1, 1).astype(BF)
        g_own[:, p * rows : (p + 1) * rows] = value[:quarter]
        g_send[:, p * rows : (p + 1) * rows] = value[quarter:]
    for out, half in ((own, info[1]), (send, 1 - info[1])):
        at = pl.multiple_of(half * half_width, half_width)
        total = None
        for p, grad in enumerate(grads):
            part = dot(
                context[:, p * rows : (p + 1) * rows], grad[:, pl.ds(at, half_width)], 1, 0
            )
            total = part if total is None else total + part
        out[...] = total.astype(BF)


def mix_back(info, mixer, context, grads):
    half_width, width = mixer.shape
    rows = context.shape[1]
    return pl.pallas_call(
        mix_back_kernel,
        out_shape=(shape((half_width // 2, rows), BF),) * 2
        + (shape((half_width, half_width), BF),) * 2,
        in_specs=[SMEM] + [VMEM] * 6,
        out_specs=(VMEM,) * 4,
        compiler_params=params(16),
        cost_estimate=FREE,
        name="mix_back",
    )(info, mixer, context, *grads)


def mix_place_kernel(blocks, info, own, recv, out, scratch):
    half_width = own.shape[1]
    quarter = half_width // 2
    x, c, shard = info[0], info[1], info[2]
    for ref, dc in ((own, 0), (recv, 1)):
        for dx in range(2):
            at = pl.multiple_of((c ^ dc) * half_width + (x ^ dx) * quarter, quarter)
            scratch[pl.ds(at, quarter), :] = ref[dx * quarter : (dx + 1) * quarter, :].astype(F32)
    block = out.shape[1]
    for b in range(blocks):
        out[order_of(range(blocks), shard, b)] = scratch[b * block : (b + 1) * block, :].astype(BF)


def mix_place(info, own, recv, blocks):
    half_width = own.shape[1]
    return pl.pallas_call(
        partial(mix_place_kernel, blocks),
        out_shape=shape((blocks, 2 * half_width // blocks, half_width), BF),
        in_specs=[SMEM, VMEM, VMEM],
        out_specs=VMEM,
        scratch_shapes=[pltpu.VMEM((2 * half_width, half_width), F32)],
        compiler_params=params(8),
        cost_estimate=FREE,
        name="mix_place",
    )(info, own, recv)


def row_tiles(rows, step, body):
    lax.fori_loop(0, rows // step, lambda i, c: body(pl.ds(pl.multiple_of(i * step, step), step), c), 0)


def mean_of(value):
    return jnp.mean(value, -1, keepdims=True)


def first_norm_kernel(
    tokens, mixed, recv0, recv1, vectors, low0, low1, normed_out, inverse_out, recv, low
):
    gain, bias = vectors[0:1, :], vectors[1:2, :]
    half = recv0.shape[0]
    recv[:half, :] = recv0[...]
    recv[half:, :] = recv1[...]

    def body(at, carry):
        hidden = tokens[at, :].astype(F32) + mixed[at, :] + recv[at, :].astype(F32)
        centred = hidden - mean_of(hidden)
        inverse = lax.rsqrt(mean_of(centred * centred) + EPSILON)
        normed = centred * inverse
        normed_out[at, :] = normed
        inverse_out[at, :] = inverse
        low[at, :] = (normed * gain + bias).astype(BF)
        return carry

    row_tiles(tokens.shape[0], 128, body)
    low0[...] = low[:half, :]
    low1[...] = low[half:, :]


def first_norm(tokens, mixed, recvs, vectors):
    rows, width = tokens.shape
    return pl.pallas_call(
        first_norm_kernel,
        grid=(1,),
        out_shape=(shape((rows // 2, width), BF),) * 2
        + (shape((rows, width), F32), shape((rows, 1), F32)),
        in_specs=[pl.BlockSpec((rows, width), lambda i: (0, 0))] * 2
        + [pl.BlockSpec((rows // 2, width), lambda i: (0, 0))] * 2
        + [pl.BlockSpec(vectors.shape, lambda i: (0, 0))],
        scratch_shapes=[pltpu.VMEM((rows, width), BF)] * 2,
        out_specs=(pl.BlockSpec((rows // 2, width), lambda i: (0, 0)),) * 2
        + (
            pl.BlockSpec((rows, width), lambda i: (0, 0)),
            pl.BlockSpec((rows, 1), lambda i: (0, 0)),
        ),
        compiler_params=params(24),
        cost_estimate=FREE,
        name="first_norm",
    )(tokens, mixed, *recvs, vectors)


def second_norm_kernel(normed_one, mlp, recv, vectors, grad, result, grad_two, grad_low, sums):
    gain_one, bias_one = vectors[0:1, :], vectors[1:2, :]
    gain, bias = vectors[2:3, :], vectors[3:4, :]
    sums[...] = jnp.zeros_like(sums)

    def body(at, carry):
        hidden = normed_one[at, :] * gain_one + bias_one + mlp[at, :] + recv[at, :].astype(F32)
        centred = hidden - mean_of(hidden)
        inverse = lax.rsqrt(mean_of(centred * centred) + EPSILON)
        normed = centred * inverse
        result[at, :] = (normed * gain + bias).astype(BF)
        grad_y = grad[at, :].astype(F32)
        grad_n = grad_y * gain
        value = inverse * (grad_n - mean_of(grad_n) - normed * mean_of(grad_n * normed))
        grad_two[at, :] = value
        grad_low[at, :] = value.astype(BF)
        sums[2:3, :] += jnp.sum(grad_y * normed, 0, keepdims=True)
        sums[3:4, :] += jnp.sum(grad_y, 0, keepdims=True)
        return carry

    row_tiles(grad.shape[0], 128, body)


def second_norm(normed_one, mlp, recv, vectors, grad):
    rows, width = grad.shape
    return pl.pallas_call(
        second_norm_kernel,
        out_shape=(
            shape((rows, width), BF),
            shape((rows, width), F32),
            shape((rows, width), BF),
            shape((8, width), F32),
        ),
        in_specs=[VMEM] * 5,
        out_specs=(VMEM,) * 4,
        compiler_params=params(24),
        cost_estimate=FREE,
        name="second_norm",
    )(normed_one, mlp, recv, vectors, grad)


def first_back_kernel(
    grad_two, own, recv0, recv1, normed_one, inverse_one, vectors, late,
    grad_one, low0, low1, sums, grad_low, recv,
):
    gain = vectors[0:1, :]
    half = low0.shape[0]
    recv[:half, :] = recv0[...]
    recv[half:, :] = recv1[...]
    sums[...] = late[...]

    def body(at, carry):
        normed = normed_one[at, :]
        grad_y = grad_two[at, :] + own[at, :] + recv[at, :].astype(F32)
        grad_n = grad_y * gain
        value = inverse_one[at, :] * (grad_n - mean_of(grad_n) - normed * mean_of(grad_n * normed))
        grad_one[at, :] = value
        grad_low[at, :] = value.astype(BF)
        sums[0:1, :] += jnp.sum(grad_y * normed, 0, keepdims=True)
        sums[1:2, :] += jnp.sum(grad_y, 0, keepdims=True)
        return carry

    row_tiles(grad_two.shape[0], 128, body)
    low0[...] = grad_low[:half, :]
    low1[...] = grad_low[half:, :]


def first_back(grad_two, own, recvs, normed_one, inverse_one, vectors, late):
    rows, width = grad_two.shape
    return pl.pallas_call(
        first_back_kernel,
        out_shape=(shape((rows, width), F32),)
        + (shape((rows // 2, width), BF),) * 2
        + (shape((8, width), F32),),
        in_specs=[VMEM] * 8,
        out_specs=(VMEM,) * 4,
        scratch_shapes=[pltpu.VMEM((rows, width), BF)] * 2,
        compiler_params=params(24),
        cost_estimate=FREE,
        name="first_back",
    )(grad_two, own, *recvs, normed_one, inverse_one, vectors, late)


def after(value, *earlier):
    return lax.optimization_barrier((value,) + earlier)[0]


def shards(
    n_shard,
    tokens,
    segment_ids,
    qkv_weight,
    out_weight,
    up_weight,
    down_weight,
    first_gain,
    first_bias,
    second_gain,
    second_bias,
    out_grad,
):
    rows, width = tokens.shape
    half_width = width // 2
    quarter = width // 4
    ff_half = up_weight.shape[1] // 2
    block = qkv_weight.shape[0]
    shard = lax.axis_index("shard").astype(jnp.int32)
    seq = lax.axis_index("seq").astype(jnp.int32)
    xb, cb = seq // 2, seq % 2
    bits = [1 << b for b in range(n_shard.bit_length() - 1)]
    top = bits[-1]
    owner = (shard // top) % 2 == cb
    low_shard = shard % top
    place = jnp.stack([xb, cb, shard])

    def swap(value, mask):
        return lax.ppermute(value, "shard", [(i, i ^ mask) for i in range(n_shard)])

    def swap_core(value):
        return lax.ppermute(value, "seq", [(i, i ^ 1) for i in range(4)])

    def swap_x(value):
        return lax.ppermute(value, "seq", [(i, i ^ 2) for i in range(4)])

    def to_core(value, to_owner):
        pairs = []
        for sh in range(n_shard):
            for se in range(4):
                sends = (sh // top == se % 2) != to_owner
                pairs.append((sh * 4 + se, (sh ^ top) * 4 + se if sends else sh * 4 + (se ^ 1)))
        return lax.ppermute(value, ("shard", "seq"), pairs)

    def join(pieces):
        return jnp.concatenate(pieces) if len(pieces) > 1 else pieces[0]

    class Gather:
        def __init__(self, own_block, over):
            self.pieces, self.offsets, self.over = [own_block[None]], [[0]], list(over)

        def swap(self, value, rel, bit):
            got = swap(value, bit)
            self.pieces.append(got)
            self.offsets.append([r ^ bit for r in rel])
            return got

        def steps(self, count, *gate):
            for bit in [self.over.pop(0) for _ in range(count)]:
                held, rel = join(self.pieces), [r for o in self.offsets for r in o]
                self.pieces, self.offsets = [held], [rel]
                gate = (self.swap(after(held, *gate), rel, bit),)
            return gate[0]

        def part(self, index, *gate):
            return self.swap(after(self.pieces[index], *gate), self.offsets[index], self.over[0])

    def fold(value, got):
        return (value[: value.shape[0] // 2].astype(F32) + got.astype(F32)).astype(BF)

    def upper(value):
        return value[value.shape[0] // 2 :]

    def add_x(value):
        return (value.astype(F32) + swap_x(value).astype(F32)).astype(BF)

    def pick(value, flag, axis):
        return jnp.where(
            flag == 0,
            lax.index_in_dim(value, 0, axis, False),
            lax.index_in_dim(value, 1, axis, False),
        )

    def ordered(flag, own, other, axis):
        return jnp.where(
            flag == 0, jnp.concatenate([own, other], axis), jnp.concatenate([other, own], axis)
        )

    over_x = swap_x(tokens)
    over_core = swap_core(tokens)
    toks = [tokens, over_core, over_x]
    plan, ids_row = make_plan(segment_ids, place)

    own_a, own_b = prepare(
        place, qkv_weight, out_weight, (first_gain, first_bias, second_gain, second_bias)
    )
    up_half = lax.dynamic_slice_in_dim(up_weight, cb * ff_half, ff_half, 1)
    middle = len(bits) - 2
    gather_a = Gather(own_a, bits[::-1])
    gather_b = Gather(own_b, bits[::-1])
    gather_up = Gather(up_half, bits[::-1])
    a1 = gather_a.steps(1)
    b1 = gather_b.steps(1, a1)
    a2 = gather_a.steps(middle)
    a3 = gather_a.steps(1)
    toks.append(swap_core(after(over_x, a2)))
    b2 = gather_b.steps(middle, a2)
    down_rows = down_weight.shape[0] // 2
    down_half = lax.dynamic_slice_in_dim(down_weight, xb * down_rows, down_rows, 0)
    d1 = to_core(after(down_half, b1), False)
    b3 = gather_b.steps(1, a3)
    part_a = assemble(gather_a.pieces, gather_a.offsets, shard)
    vectors = vectors_of(part_a)
    far_a = swap_x(part_a)

    saved, own_ctx, sends = [], [], []

    def head(j, weight, *gate):
        ctx_own, ctx_send, ctx_full, lse = attend(
            plan, toks, weight, after(ids_row, *gate)
        )
        own_ctx.append(ctx_own)
        sends.append(ctx_send)
        saved.append((ctx_full, lse))
        return ctx_own

    ctx = head(0, part_a[:, :TRIO], b2, vectors)
    d1, b3 = after(d1, ctx), after(b3, ctx)
    gather_b.pieces[1] = b3
    gather_down = Gather(jnp.where(owner, down_half, d1), bits[-2::-1])
    d2 = gather_down.steps(middle)
    u1 = gather_up.steps(1, ctx)
    part_b = assemble(gather_b.pieces, gather_b.offsets, shard)
    far_weights = swap_x(part_b[:, : 2 * TRIO])
    ctx = head(1, part_b[:, :TRIO], gather_down.pieces[0], far_a)
    d2, u1 = after(d2, ctx), after(u1, ctx)
    gather_down.pieces[1], gather_up.pieces[1] = d2, u1
    d3 = gather_down.steps(1)
    u2 = gather_up.steps(middle)
    ctx = head(2, part_b[:, TRIO : 2 * TRIO], gather_down.pieces[0], gather_up.pieces[0], far_weights)
    d3, u2 = after(d3, ctx), after(u2, ctx)
    gather_down.pieces[1], gather_up.pieces[1] = d3, u2
    held_up = join(gather_up.pieces)
    held = join(gather_down.pieces)
    gather_up.offsets = [[r for o in gather_up.offsets for r in o]]
    sends[2], held_up, held = lax.optimization_barrier((sends[2], held_up, held))
    gather_up.pieces = [held_up]
    gather_up.part(0)
    others = [swap_x(value) for value in sends]
    rel = [2 * r for o in gather_down.offsets for r in o]
    widen = assemble(gather_up.pieces, gather_up.offsets, shard)
    held_far = swap_x(held)
    head_weights = [part_a[:, :TRIO], part_b[:, :TRIO], part_b[:, TRIO : 2 * TRIO]]
    far_weights = [far_a, far_weights[:, :TRIO], far_weights[:, TRIO:]]
    mixer = part_b[:, 2 * TRIO :].reshape(2, half_width, half_width)
    mixer = ordered(cb, pick(mixer, cb, 0), swap_core(pick(mixer, 1 - cb, 0)), 1)
    mixer = jnp.where(xb == 0, mixer, jnp.concatenate([mixer[quarter:], mixer[:quarter]]))
    context = jnp.concatenate(own_ctx + others)

    mixed = dot(context, mixer, 0, 0)
    low0, low1, normed_one, inverse_one = first_norm(
        tokens,
        mixed,
        [swap_core(mixed[at : at + rows // 2].astype(BF)) for at in (rows, rows + rows // 2)],
        vectors,
    )
    act_low, act_t, slope, low_t = feed_up([low0, low1, swap_core(low0), swap_core(low1)], widen)
    held_far = after(held_far, act_low)
    narrow = assemble([held, held_far], [rel, [r + 1 for r in rel]], low_shard * 2 + xb)
    mlp_own, mlp_send = feed_down(act_low, narrow)
    result, grad_two, grad_mlp, late = second_norm(
        normed_one, mlp_own, swap_core(mlp_send), vectors, out_grad
    )

    grad_mlp = [grad_mlp, swap_core(grad_mlp)]
    narrow_grad = weight_grad(low_shard, act_t, grad_mlp, n_shard // 2, False)
    n1 = swap(upper(narrow_grad), bits[-2])
    first_own, send0, send1, grad_pre = feed_back(
        after(grad_mlp[0], narrow_grad), grad_mlp[1], slope, widen, narrow
    )
    widen_grad = weight_grad(shard, low_t, [grad_pre], n_shard)
    w1 = swap(upper(widen_grad), bits[0])
    recv0, recv1, _ = lax.optimization_barrier((swap_core(send0), swap_core(send1), widen_grad))
    grad_one, attn0, attn1, sums = first_back(
        grad_two, first_own, [recv0, recv1], normed_one, inverse_one, vectors, late
    )
    g_own, g_send, mixer_own, mixer_send = mix_back(
        place, mixer, context, [attn0, attn1, swap_core(attn0), swap_core(attn1)]
    )
    g_recv = swap_x(g_send)
    mixer_grad = mix_place(place, mixer_own, swap_core(mixer_send), n_shard)

    def head_back(j, *gate):
        at = j * HEAD_DIM
        return attend_back(
            plan, place, toks, head_weights[j], after(ids_row, *gate),
            g_own[at : at + HEAD_DIM], g_recv[at : at + HEAD_DIM], *saved[j],
            sums if j == 2 else None, n_shard,
        )

    keeps, sends, parts = [None] * 3, [None] * 3, [None] * 3
    keeps[0], sends[0], parts[0] = head_back(0, mixer_grad)
    fars = [swap_x(sends[0])]
    narrow_grad = fold(narrow_grad, after(n1, parts[0]))
    for bit in bits[-3:0:-1]:
        narrow_grad = fold(narrow_grad, swap(upper(narrow_grad), bit))
    n2 = swap(upper(narrow_grad), bits[0])
    widen_grad = fold(widen_grad, after(w1, narrow_grad))
    for bit in bits[1:-2]:
        widen_grad = fold(widen_grad, swap(upper(widen_grad), bit))
    w2 = swap(upper(widen_grad), bits[-2])
    keeps[1], sends[1], parts[1] = head_back(1, narrow_grad, widen_grad)
    early = jnp.concatenate([mixer_grad, parts[0], parts[1]], 2)
    e1 = swap(upper(early), bits[0])
    narrow_grad = fold(narrow_grad, after(n2, early))[0]
    fars.append(swap_x(sends[1]))
    n3 = to_core(narrow_grad, True)
    widen_grad = fold(widen_grad, after(w2, early))
    w3 = swap(upper(widen_grad), bits[-1])
    keeps[2], sends[2], parts[2] = head_back(2, narrow_grad, widen_grad, fars[0], early)
    fars = [fars[0], fars[1], swap_x(sends[2])]
    early = fold(early, after(e1, parts[2], fars[1]))
    widen_grad = fold(widen_grad, after(w3, parts[2]))[0]
    late = after(parts[2], early, widen_grad)
    l1 = swap(upper(late), bits[0])
    e2 = swap(upper(early), bits[1])
    w4 = swap_x(widen_grad)
    late = fold(late, l1)
    l2 = swap(upper(late), bits[1])
    narrow_grad = (narrow_grad.astype(F32) + after(n3, late).astype(F32)).astype(BF)
    n4 = swap_x(narrow_grad)
    late = fold(late, after(l2, narrow_grad))
    for bit in bits[2:-1]:
        late = fold(late, swap(upper(late), bit))
    l3 = swap(upper(late), bits[-1])
    early = fold(early, after(e2, late))
    for bit in bits[2:-1]:
        early = fold(early, swap(upper(early), bit))
    e3 = swap(upper(early), bits[-1])
    fars[2] = after(fars[2], early)
    back_own, back_core = input_back(keeps + fars, head_weights + far_weights, rows)
    back_near = swap_core(back_core)
    early = fold(early, after(e3, back_core))[0]
    late = fold(late, after(l3, early))[0]
    mine = jnp.concatenate([early, late], 1)
    theirs = swap_x(mine)
    narrow_grad = (narrow_grad.astype(F32) + after(n4, mine).astype(F32)).astype(BF)
    widen_grad = (widen_grad.astype(F32) + after(w4, narrow_grad).astype(F32)).astype(BF)
    narrow_other, widen_other = swap_core(narrow_grad), swap_core(widen_grad)
    narrow_grad = jnp.where(owner, narrow_grad, narrow_other)
    widen_grad = ordered(cb, widen_grad, widen_other, 1)
    input_grad = grad_one + back_own + back_near.astype(F32)
    theirs = after(theirs, widen_grad, narrow_grad)
    mixer_grad = (mine[:, :half_width].astype(F32) + theirs[:, :half_width].astype(F32)).astype(BF)
    chip = jnp.concatenate([mixer_grad, mine[:, half_width:], theirs[:, half_width:]], 1)
    other = swap_core(chip)
    mixer_grad = ordered(cb, mixer_grad, other[:, :half_width], 1)
    qkv_grad, sums = place_qkv(place, chip, other, half_width, width)
    return (
        result,
        input_grad,
        qkv_grad,
        mixer_grad.astype(F32),
        widen_grad.astype(F32),
        narrow_grad.astype(F32),
        sums[:, 0],
        sums[:, 1],
        sums[:, 2],
        sums[:, 3],
    )


def solution(mesh):
    placed = (
        P(("shard", "seq"), None),
        P("shard", None),
        P("shard", None),
        P("shard", None),
        P("shard", None),
        P("shard", None),
        P("shard"),
        P("shard"),
        P("shard"),
        P("shard"),
        P(("shard", "seq"), None),
    )
    return jax.shard_map(
        partial(shards, mesh.shape["shard"]),
        mesh=mesh,
        in_specs=placed,
        out_specs=(
            P(("shard", "seq"), None),
            P(("shard", "seq"), None),
            P("shard", None),
            P("shard", None),
            P("shard", None),
            P("shard", None),
            P("shard"),
            P("shard"),
            P("shard"),
            P("shard"),
        ),
        check_vma=False,
    )
```

```python
from functools import partial

import jax
import jax.numpy as jnp
from jax import lax
from jax.experimental import pallas as pl
from jax.experimental.pallas import tpu as pltpu
from jax.sharding import PartitionSpec as P

HEADS = 12
HEAD_DIM = 64
TRIO = 3 * HEAD_DIM
GROUPS = 16
EPSILON = 1e-12
FAR = -(2.0**30)
SCALE = HEAD_DIM**-0.5
TILE = 256
UNROLL = 2
BF = jnp.bfloat16
F32 = jnp.float32
VMEM = pl.BlockSpec(memory_space=pltpu.VMEM)
SMEM = pl.BlockSpec(memory_space=pltpu.SMEM)
FREE = pl.CostEstimate(flops=1, bytes_accessed=1, transcendentals=0)


def dot(a, b, ca, cb):
    return lax.dot_general(a, b, (((ca,), (cb,)), ((), ())), preferred_element_type=F32)


def shape(dims, kind):
    return jax.ShapeDtypeStruct(dims, kind)


def params(mebi):
    return pltpu.CompilerParams(vmem_limit_bytes=mebi << 20)


def assemble_kernel(offsets, info, *refs):
    out, sem = refs[-2:]
    copies = []
    for ref, rel in zip(refs[:-2], offsets):
        block = ref.shape[1]
        for i, r in enumerate(rel):
            at = pl.multiple_of((info[0] ^ r) * block, block)
            copies.append(
                pltpu.make_async_copy(ref.at[i], out.at[pl.ds(at, block), :], sem.at[len(copies)])
            )
    for copy in copies:
        copy.start()
    for copy in copies:
        copy.wait()


def assemble(pieces, offsets, me):
    block, cols = pieces[0].shape[1:]
    count = sum(len(r) for r in offsets)
    if block % 16:
        value = jnp.concatenate(pieces)
        order = [r for rel in offsets for r in rel]
        place = jnp.array([order.index(r) for r in range(count)], jnp.int32)
        return value[place[me ^ jnp.arange(count)]].reshape(count * block, cols)
    return pl.pallas_call(
        partial(assemble_kernel, offsets),
        out_shape=shape((count * block, cols), BF),
        in_specs=[SMEM] + [pl.BlockSpec(memory_space=pl.ANY)] * len(pieces),
        out_specs=VMEM,
        scratch_shapes=[pltpu.SemaphoreType.DMA((count,))],
        compiler_params=params(12),
        cost_estimate=FREE,
        name="assemble",
    )(me[None], *pieces)


def prepare_kernel(info, qkv_far, out_far, *refs):
    vectors, (part_a, part_b, qkv, out_weight, rows, scratch, sem) = refs[:4], refs[4:]
    block, width = out_weight.shape
    half, quarter = width // 2, width // 4
    copies = [
        pltpu.make_async_copy(qkv_far, qkv, sem.at[0]),
        pltpu.make_async_copy(out_far, out_weight, sem.at[1]),
    ] + [pltpu.make_async_copy(v, rows.at[i], sem.at[2 + i]) for i, v in enumerate(vectors)]
    for copy in copies:
        copy.start()
    scratch[...] = jnp.zeros_like(scratch)
    for copy in copies:
        copy.wait()
    for i in range(4):
        scratch[i : i + 1, :block] = rows[i].astype(F32)
    part_a[:, TRIO:] = scratch[...].T[:block, : 256 - TRIO].astype(BF)
    for x in range(2):
        for c in range(2):

            @pl.when(jnp.logical_and(info[0] == x, info[1] == c))
            def _():
                at = c * half + x * quarter
                trio = [qkv[:, i * width + at : i * width + at + quarter] for i in range(3)]
                for j in range(3):
                    piece = jnp.concatenate(
                        [t[:, j * HEAD_DIM : (j + 1) * HEAD_DIM] for t in trio], 1
                    )
                    if j == 0:
                        part_a[:, :TRIO] = piece
                    else:
                        part_b[:, (j - 1) * TRIO : j * TRIO] = piece
                part_b[:, 2 * TRIO :] = out_weight[:, c * half : (c + 1) * half]


def prepare(info, qkv, out_weight, vectors):
    block, width = out_weight.shape
    far = [qkv, out_weight] + [v[None] for v in vectors]
    return pl.pallas_call(
        prepare_kernel,
        out_shape=(shape((block, 256), BF), shape((block, 2 * TRIO + width // 2), BF)),
        in_specs=[SMEM] + [pl.BlockSpec(memory_space=pltpu.HBM)] * 6,
        out_specs=(VMEM, VMEM),
        scratch_shapes=[
            pltpu.VMEM(qkv.shape, BF),
            pltpu.VMEM(out_weight.shape, BF),
            pltpu.VMEM((4, 1, block), BF),
            pltpu.VMEM((128, 128), F32),
            pltpu.SemaphoreType.DMA((6,)),
        ],
        compiler_params=params(8),
        cost_estimate=FREE,
        name="prepare",
    )(info, *[pltpu.with_memory_space_constraint(v, pltpu.HBM) for v in far])


def vectors_kernel(part, out):
    out[...] = part[:, 128:].astype(F32).T[TRIO - 128 : TRIO - 120]


def vectors_of(part):
    return pl.pallas_call(
        vectors_kernel,
        out_shape=shape((8, part.shape[0]), F32),
        in_specs=[VMEM],
        out_specs=VMEM,
        compiler_params=params(8),
        cost_estimate=FREE,
        name="vectors",
    )(part)


def doc_rows(ids_ref, same, other):
    ids = ids_ref[...]
    rows = lax.broadcasted_iota(jnp.int32, (GROUPS, ids.shape[1]), 0)
    return jnp.where(rows == ids, same, other).astype(BF)


def plan_kernel(ids_s, ids_v, place, plan, row):
    total = ids_v.shape[1]
    tiles = total // TILE
    chunk = total // 4
    me = place[0] * 2 + place[1]
    entries = (plan.shape[0] - 1) // 2
    for i in range(2 * entries):
        plan[1 + i] = jnp.int32(tiles)
    first = [ids_s[0, i * TILE] for i in range(tiles)]
    last = [ids_s[0, i * TILE + TILE - 1] for i in range(tiles)]
    flip = me * (chunk // TILE)
    count = jnp.int32(0)
    for i in range(tiles):
        for j in range(tiles):
            meet = jnp.logical_and(first[i] <= last[j], first[j] <= last[i])

            @pl.when(meet)
            def _():
                plan[1 + 2 * UNROLL + count] = i ^ flip
                plan[1 + entries + 2 * UNROLL + count] = j ^ flip

            count = count + meet.astype(jnp.int32)
    plan[0] = (count + UNROLL - 1) // UNROLL
    for r in range(4):
        at = pl.multiple_of((me ^ r) * chunk, chunk)
        row[:, r * chunk : (r + 1) * chunk] = ids_v[:, pl.ds(at, chunk)]


def make_plan(ids, place):
    total = ids.shape[1]
    entries = (total // TILE) ** 2 + 4 * UNROLL
    return pl.pallas_call(
        plan_kernel,
        out_shape=(shape((1 + 2 * entries,), jnp.int32), shape((1, total), jnp.int32)),
        in_specs=[SMEM, VMEM, SMEM],
        out_specs=(SMEM, VMEM),
        compiler_params=params(8),
        cost_estimate=FREE,
        name="plan",
    )(ids, ids, place)


def tile_of(plan, entry):
    return pl.multiple_of(plan[1 + entry] * TILE, TILE)


def attend_kernel(
    plan, tok0, tok1, tok2, tok3, weight, ids_ref, ctx_own, ctx_send, ctx_full, lse,
    q_t, k_nat, v_t, s_ref, p_ref, fade, top, sums, acc,
):
    total = ids_ref.shape[1]
    half = total // 2
    entries = (plan.shape[0] - 1) // 2
    weight_t = weight[...].T
    keys = weight[:, HEAD_DIM : 2 * HEAD_DIM]
    for i, tok in enumerate((tok0, tok1, tok2, tok3)):
        rows = tok[...]
        at, end = i * rows.shape[0], (i + 1) * rows.shape[0]
        trio = dot(weight_t, rows, 1, 1).astype(BF)
        q_t[:HEAD_DIM, at:end] = trio[:HEAD_DIM] * SCALE
        v_t[:, at:end] = trio[2 * HEAD_DIM :]
        k_nat[at:end, :HEAD_DIM] = dot(rows, keys, 1, 0).astype(BF)
    q_t[HEAD_DIM : HEAD_DIM + GROUPS, :total] = doc_rows(ids_ref, 0.0, FAR)
    q_t[HEAD_DIM + GROUPS :, :total] = jnp.zeros((128 - HEAD_DIM - GROUPS, total), BF)
    docs = jnp.concatenate(
        [doc_rows(ids_ref, 1.0, 0.0), jnp.zeros((128 - HEAD_DIM - GROUPS, total), BF)], 0
    )
    k_nat[:total, HEAD_DIM:] = docs.T
    top[...] = jnp.full_like(top, -3e38)
    sums[...] = jnp.zeros_like(sums)
    acc[...] = jnp.zeros_like(acc)

    def step(j, carry):
        i = j * UNROLL
        for u in range(UNROLL):
            q, k = tile_of(plan, i + u), tile_of(plan, entries + i + u)
            acc[:, pl.ds(q, TILE)] = acc[:, pl.ds(q, TILE)] * fade[u] + dot(
                v_t[:, pl.ds(k, TILE)], p_ref[u], 1, 0
            )
        peaks = [jnp.max(s_ref[u], 0, keepdims=True) for u in range(UNROLL)]
        for u in range(UNROLL):
            q = tile_of(plan, i + UNROLL + u)
            old = top[:, pl.ds(q, TILE)]
            new = jnp.maximum(old, peaks[u])
            powers = jnp.exp(s_ref[u] - new)
            decay = jnp.exp(old - new)
            top[:, pl.ds(q, TILE)] = new
            sums[:, pl.ds(q, TILE)] = sums[:, pl.ds(q, TILE)] * decay + jnp.sum(
                powers, 0, keepdims=True
            )
            fade[u] = decay
            p_ref[u] = powers.astype(BF)
        for u in range(UNROLL):
            q = tile_of(plan, i + 2 * UNROLL + u)
            k = tile_of(plan, entries + i + 2 * UNROLL + u)
            s_ref[u] = dot(k_nat[pl.ds(k, TILE), :], q_t[:, pl.ds(q, TILE)], 1, 0)
        return carry

    lax.fori_loop(0, plan[0] + 2, step, 0)
    ctx_full[...] = acc[:, :total] / sums[:, :total]
    lse[...] = top[:, :total] + jnp.log(sums[:, :total])
    ctx_own[...] = ctx_full[:, :half].astype(BF)
    ctx_send[...] = ctx_full[:, half:].astype(BF)


def attend(plan, toks, weight, ids):
    total = ids.shape[1]
    half = total // 2
    padded = total + TILE
    return pl.pallas_call(
        attend_kernel,
        out_shape=(
            shape((HEAD_DIM, half), BF),
            shape((HEAD_DIM, half), BF),
            shape((HEAD_DIM, total), F32),
            shape((1, total), F32),
        ),
        in_specs=[SMEM] + [VMEM] * 6,
        out_specs=(VMEM,) * 4,
        scratch_shapes=[
            pltpu.VMEM((128, padded), BF),
            pltpu.VMEM((padded, 128), BF),
            pltpu.VMEM((HEAD_DIM, padded), BF),
            pltpu.VMEM((UNROLL, TILE, TILE), F32),
            pltpu.VMEM((UNROLL, TILE, TILE), BF),
            pltpu.VMEM((UNROLL, 1, TILE), F32),
            pltpu.VMEM((1, padded), F32),
            pltpu.VMEM((1, padded), F32),
            pltpu.VMEM((HEAD_DIM, padded), F32),
        ],
        compiler_params=params(20),
        cost_estimate=FREE,
        name="attend",
    )(plan, *toks, weight, ids)


def attend_back_kernel(
    order, plan, place, tok0, tok1, tok2, tok3, weight, ids_ref, g_own, g_recv, ctx_full, lse_in,
    sums, before, keep, send, grad_out,
    q_t, kvd, k_t, g_t, qg_nat, lse, row_term, s_ref, d_ref, p_ref, e_ref, acc, dq_t, w_grad, out,
):
    total = ids_ref.shape[1]
    half = total // 2
    entries = (plan.shape[0] - 1) // 2
    toks = (tok0, tok1, tok2, tok3)
    chunk = tok0.shape[0]
    weight_t = weight[:, : 2 * HEAD_DIM].T
    natural_w = weight[:, HEAD_DIM:]
    for at, grad in ((0, g_own), (half, g_recv)):
        g_t[HEAD_DIM:, at : at + half] = grad[...]
    g_t[:HEAD_DIM, :total] = jnp.zeros((HEAD_DIM, total), BF)
    for i, tok in enumerate(toks):
        at, end = i * chunk, (i + 1) * chunk
        rows = tok[...]
        pair = dot(weight_t, rows, 1, 1).astype(BF)
        q_t[:HEAD_DIM, at:end] = pair[:HEAD_DIM] * SCALE
        k_t[:, at:end] = pair[HEAD_DIM:]
        kvd[at:end, :128] = dot(rows, natural_w, 1, 0).astype(BF)
    qg_nat[:total, :] = jnp.concatenate([q_t[:HEAD_DIM, :total], g_t[HEAD_DIM:, :total]], 0).T
    q_t[HEAD_DIM:128, :total] = jnp.zeros((128 - HEAD_DIM, total), BF)
    q_t[128 : 128 + GROUPS, :total] = doc_rows(ids_ref, 0.0, FAR)
    q_t[128 + GROUPS :, :total] = jnp.zeros((128 - GROUPS, total), BF)
    kvd[:total, 128:] = jnp.concatenate(
        [doc_rows(ids_ref, 1.0, 0.0), jnp.zeros((128 - GROUPS, total), BF)], 0
    ).T
    acc[...] = jnp.zeros_like(acc)
    dq_t[...] = jnp.zeros_like(dq_t)
    lse[:, :total] = lse_in[...]
    row_term[:, :total] = jnp.sum(
        ctx_full[...] * g_t[HEAD_DIM:, :total].astype(F32), 0, keepdims=True
    )
    left = lax.broadcasted_iota(jnp.int32, (TILE, 128), 1) < HEAD_DIM

    def step(j, carry):
        i = j * UNROLL
        for u in range(UNROLL):
            q, k = tile_of(plan, i + u), tile_of(plan, entries + i + u)
            grad_scores, chance = e_ref[u], p_ref[u]
            natural = qg_nat[pl.ds(q, TILE), :]
            dq_t[:, pl.ds(q, TILE)] += dot(k_t[:, pl.ds(k, TILE)], grad_scores, 1, 0)
            acc[pl.ds(k, TILE), :] += jnp.where(
                left, dot(grad_scores, natural, 1, 0), dot(chance, natural, 1, 0)
            )
        for u in range(UNROLL):
            q = tile_of(plan, i + UNROLL + u)
            chance = jnp.exp(s_ref[u] - lse[:, pl.ds(q, TILE)])
            p_ref[u] = chance.astype(BF)
            e_ref[u] = (chance * (d_ref[u] - row_term[:, pl.ds(q, TILE)])).astype(BF)
        for u in range(UNROLL):
            q = tile_of(plan, i + 2 * UNROLL + u)
            rows = kvd[pl.ds(tile_of(plan, entries + i + 2 * UNROLL + u), TILE), :]
            s_ref[u] = dot(rows, q_t[:, pl.ds(q, TILE)], 1, 0)
            d_ref[u] = dot(rows[:, :128], g_t[:, pl.ds(q, TILE)], 1, 0)
        return carry

    lax.fori_loop(0, plan[0] + 2, step, 0)
    out[:HEAD_DIM, :] = (dq_t[:, :total] * SCALE).astype(BF)
    out[HEAD_DIM:, :] = acc[:total, :].T.astype(BF)
    keep[...] = out[:, :half]
    send[...] = out[:, half:]
    for i, tok in enumerate(toks):
        part = dot(out[:, i * chunk : (i + 1) * chunk], tok[...], 1, 0)
        w_grad[:TRIO, :] = part if i == 0 else w_grad[:TRIO, :] + part
    if sums is not None:
        w_grad[TRIO : TRIO + 8, :] = sums[...]
        w_grad[TRIO + 8 :, :] = jnp.zeros((256 - TRIO - 8, w_grad.shape[1]), F32)
    else:
        w_grad[TRIO:, :] = jnp.zeros((256 - TRIO, w_grad.shape[1]), F32)
    natural = w_grad[...].T
    block = grad_out.shape[1]
    for b in range(len(order)):
        to = order_of(order, place[2], b)
        value = natural[b * block : (b + 1) * block].astype(BF)
        if before is None:
            grad_out[to] = value
        else:
            ahead = before.shape[2]
            grad_out[to, :, :ahead] = before[to]
            grad_out[to, :, ahead:] = value


def order_of(order, me, b):
    rel = me ^ b
    bits = len(order).bit_length() - 1
    place = 0
    for i in range(bits):
        place = place | (((rel >> i) & 1) << (bits - 1 - i))
    return place


def attend_back(plan, place, toks, weight, ids, g_own, g_recv, ctx_full, lse, sums, before, n_shard):
    total = ids.shape[1]
    width = weight.shape[0]
    padded = total + TILE
    extra = [value for value in (sums, before) if value is not None]
    cols = 256 + (0 if before is None else before.shape[2])

    def kernel(*refs):
        refs = list(refs)
        if sums is None:
            refs.insert(12, None)
        if before is None:
            refs.insert(13, None)
        attend_back_kernel(range(n_shard), *refs)

    return pl.pallas_call(
        kernel,
        out_shape=(shape((TRIO, total // 2), BF),) * 2
        + (shape((n_shard, width // n_shard, cols), BF),),
        in_specs=[SMEM, SMEM] + [VMEM] * (10 + len(extra)),
        out_specs=(VMEM,) * 3,
        scratch_shapes=[
            pltpu.VMEM((256, padded), BF),
            pltpu.VMEM((padded, 256), BF),
            pltpu.VMEM((HEAD_DIM, padded), BF),
            pltpu.VMEM((128, padded), BF),
            pltpu.VMEM((padded, 128), BF),
            pltpu.VMEM((1, padded), F32),
            pltpu.VMEM((1, padded), F32),
            pltpu.VMEM((UNROLL, TILE, TILE), F32),
            pltpu.VMEM((UNROLL, TILE, TILE), F32),
            pltpu.VMEM((UNROLL, TILE, TILE), BF),
            pltpu.VMEM((UNROLL, TILE, TILE), BF),
            pltpu.VMEM((padded, 128), F32),
            pltpu.VMEM((HEAD_DIM, padded), F32),
            pltpu.VMEM((256, width), F32),
            pltpu.VMEM((TRIO, total), BF),
        ],
        compiler_params=params(24),
        cost_estimate=FREE,
        name="attend_back",
    )(plan, place, *toks, weight, ids, g_own, g_recv, ctx_full, lse, *extra)


def input_back_kernel(*refs):
    grads, weights, (own, send), (tall, wide) = refs[:6], refs[6:12], refs[12:14], refs[14:]
    rows = own.shape[0]
    step = 256
    for i, (grad, weight) in enumerate(zip(grads, weights)):
        tall[i * TRIO : (i + 1) * TRIO, :] = grad[...]
        wide[:, i * TRIO : (i + 1) * TRIO] = weight[:, :TRIO]

    def body(i, carry):
        at = pl.multiple_of(i * step, step)
        part = dot(tall[:, pl.ds(at, step)].T, wide[...], 1, 1)

        @pl.when(at < rows)
        def _():
            own[pl.ds(at, step), :] = part

        @pl.when(at >= rows)
        def _():
            send[pl.ds(pl.multiple_of(at - rows, step), step), :] = part.astype(BF)

        return carry

    lax.fori_loop(0, 2 * rows // step, body, 0)


def input_back(grads, weights, rows):
    width = weights[0].shape[0]
    return pl.pallas_call(
        input_back_kernel,
        out_shape=(shape((rows, width), F32), shape((rows, width), BF)),
        in_specs=[VMEM] * 12,
        out_specs=(VMEM,) * 2,
        scratch_shapes=[pltpu.VMEM((6 * TRIO, 2 * rows), BF), pltpu.VMEM((width, 6 * TRIO), BF)],
        compiler_params=params(24),
        cost_estimate=FREE,
        name="input_back",
    )(*grads, *weights)


def place_qkv_kernel(start, info, chip, other, out, sums_out):
    part = out.shape[1] // 3
    x, c = info[0] == 0, info[1] == 0
    values = [
        ref[:, start + dx * 768 : start + (dx + 1) * 768].astype(F32)
        for ref in (chip, other)
        for dx in range(2)
    ]
    tail = [v[:, 2 * 256 + TRIO : 2 * 256 + TRIO + 8] for v in values]
    sums_out[...] = tail[0] + tail[1] + tail[2] + tail[3]
    for sec in range(3):
        at = sec * HEAD_DIM
        near, near_x, far, far_x = [
            jnp.concatenate(
                [v[:, j * 256 + at : j * 256 + at + HEAD_DIM] for j in range(3)], 1
            )
            for v in values
        ]
        near, near_x = jnp.where(x, near, near_x), jnp.where(x, near_x, near)
        far, far_x = jnp.where(x, far, far_x), jnp.where(x, far_x, far)
        out[:, sec * part : (sec + 1) * part] = jnp.concatenate(
            [
                jnp.where(c, near, far),
                jnp.where(c, near_x, far_x),
                jnp.where(c, far, near),
                jnp.where(c, far_x, near_x),
            ],
            1,
        )


def place_qkv(info, chip, other, start, width):
    block = chip.shape[0]
    return pl.pallas_call(
        partial(place_qkv_kernel, start),
        out_shape=(shape((block, 3 * width), F32), shape((block, 8), F32)),
        in_specs=[SMEM] + [VMEM] * 2,
        out_specs=(VMEM, VMEM),
        compiler_params=params(8),
        cost_estimate=FREE,
        name="place_qkv",
    )(info, chip, other)


def gelu_both(u):
    root = 0.7978845608028654
    cube = 0.044715 * root
    square = u * u
    t = jnp.tanh(u * (root + cube * square))
    half = 0.5 * (1.0 + t)
    act = u * half
    slope = half + act * (1.0 - t) * (root + 3.0 * cube * square)
    return act, slope


def feed_up_kernel(low0, low1, low2, low3, up, act_out, act_t, slope_out, low_t, low):
    step = low0.shape[0]
    for p, piece in enumerate((low0, low1, low2, low3)):
        low[p * step : (p + 1) * step, :] = piece[...]

    def body(i, carry):
        at = pl.multiple_of(i * step, step)
        value = low[pl.ds(at, step), :]
        low_t[:, pl.ds(at, step)] = value.T
        act, slope = gelu_both(dot(value, up[...], 1, 0))
        act = act.astype(BF)
        act_out[pl.ds(at, step), :] = act
        act_t[:, pl.ds(at, step)] = act.T
        slope_out[pl.ds(at, step), :] = slope.astype(BF)
        return carry

    lax.fori_loop(0, 4, body, 0)


def feed_up(lows, up):
    rows, width = lows[0].shape
    hidden = up.shape[1]
    return pl.pallas_call(
        feed_up_kernel,
        out_shape=(
            shape((4 * rows, hidden), BF),
            shape((hidden, 4 * rows), BF),
            shape((4 * rows, hidden), BF),
            shape((width, 4 * rows), BF),
        ),
        in_specs=[VMEM] * 5,
        out_specs=(VMEM,) * 4,
        scratch_shapes=[pltpu.VMEM((4 * rows, width), BF)],
        compiler_params=params(32),
        cost_estimate=FREE,
        name="feed_up",
    )(*lows, up)


def feed_down_kernel(act, down, own, send):
    rows = own.shape[0]
    step = 256

    def body(i, carry):
        at = pl.multiple_of(i * step, step)
        part = dot(act[pl.ds(at, step), :], down[...], 1, 0)

        @pl.when(at < rows)
        def _():
            own[pl.ds(at, step), :] = part

        @pl.when(at >= rows)
        def _():
            send[pl.ds(pl.multiple_of(at - rows, step), step), :] = part.astype(BF)

        return carry

    lax.fori_loop(0, 2 * rows // step, body, 0)


def feed_down(act, down):
    rows, hidden = act.shape
    width = down.shape[1]
    return pl.pallas_call(
        feed_down_kernel,
        out_shape=(shape((rows // 2, width), F32), shape((rows // 2, width), BF)),
        in_specs=[VMEM] * 2,
        out_specs=(VMEM,) * 2,
        compiler_params=params(24),
        cost_estimate=FREE,
        name="feed_down",
    )(act, down)


def feed_back_kernel(
    grad_own, grad_other, slope, up, down, own, send0, send1, pre_out, grad, send
):
    rows = grad_own.shape[0]
    step = 256
    grad[:rows, :] = grad_own[...]
    grad[rows:, :] = grad_other[...]

    def body(i, carry):
        at = pl.multiple_of(i * step, step)
        pre = dot(grad[pl.ds(at, step), :], down[...], 1, 1)
        pre = (pre * slope[pl.ds(at, step), :].astype(F32)).astype(BF)
        pre_out[pl.ds(at, step), :] = pre
        part = dot(pre, up[...], 1, 1)

        @pl.when(at < rows)
        def _():
            own[pl.ds(at, step), :] = part

        @pl.when(at >= rows)
        def _():
            send[pl.ds(pl.multiple_of(at - rows, step), step), :] = part.astype(BF)

        return carry

    lax.fori_loop(0, 2 * rows // step, body, 0)
    send0[...] = send[: rows // 2, :]
    send1[...] = send[rows // 2 :, :]


def feed_back(grad_own, grad_other, slope, up, down):
    rows, width = grad_own.shape
    hidden = up.shape[1]
    return pl.pallas_call(
        feed_back_kernel,
        out_shape=(
            shape((rows, width), F32),
            shape((rows // 2, width), BF),
            shape((rows // 2, width), BF),
            shape((2 * rows, hidden), BF),
        ),
        in_specs=[VMEM] * 5,
        out_specs=(VMEM,) * 4,
        scratch_shapes=[pltpu.VMEM((2 * rows, width), BF), pltpu.VMEM((rows, width), BF)],
        compiler_params=params(32),
        cost_estimate=FREE,
        name="feed_back",
    )(grad_own, grad_other, slope, up, down)


def weight_grad_kernel(blocks, reverse, shard, left, right_own, right_other, out):
    rows, cols = left.shape[0], out.shape[2]
    half = left.shape[1] // 2
    step = 256
    block = out.shape[1]
    lone = right_other is None

    def body(i, carry):
        at = pl.multiple_of(i * step, step)
        if lone:
            value = dot(left[...], right_own[:, pl.ds(at, step)], 1, 0)
        else:
            value = dot(left[:, :half], right_own[:, pl.ds(at, step)], 1, 0) + dot(
                left[:, half:], right_other[:, pl.ds(at, step)], 1, 0
            )
        for b in range(blocks):
            to = order_of(range(blocks), shard[0], b) if reverse else shard[0] ^ b
            out[to, :, pl.ds(at, step)] = value[
                b * block : (b + 1) * block
            ].astype(BF)
        return carry

    lax.fori_loop(0, cols // step, body, 0)


def weight_grad(shard, left, rights, blocks, reverse=True):
    rows, cols = left.shape[0], rights[0].shape[1]

    def kernel(*refs):
        refs = list(refs)
        if len(rights) == 1:
            refs.insert(3, None)
        weight_grad_kernel(blocks, reverse, *refs)

    return pl.pallas_call(
        kernel,
        out_shape=shape((blocks, rows // blocks, cols), BF),
        in_specs=[SMEM, VMEM] + [VMEM] * len(rights),
        out_specs=VMEM,
        compiler_params=params(24),
        cost_estimate=FREE,
        name="weight_grad",
    )(shard[None], left, *rights)


def mix_back_kernel(mixer, grad0, grad1, grad2, grad3, g_own, g_send):
    quarter = g_own.shape[0]
    rows = grad0.shape[0]
    for p, grad in enumerate((grad0, grad1, grad2, grad3)):
        value = dot(mixer[...], grad[...], 1, 1).astype(BF)
        g_own[:, p * rows : (p + 1) * rows] = value[:quarter]
        g_send[:, p * rows : (p + 1) * rows] = value[quarter:]


def mix_back(mixer, grads):
    half_width = mixer.shape[0]
    rows = grads[0].shape[0] * 4
    return pl.pallas_call(
        mix_back_kernel,
        out_shape=(shape((half_width // 2, rows), BF),) * 2,
        in_specs=[VMEM] * 5,
        out_specs=(VMEM,) * 2,
        compiler_params=params(16),
        cost_estimate=FREE,
        name="mix_back",
    )(mixer, *grads)


def mix_grad_kernel(info, context, grad0, grad1, grad2, grad3, own, send):
    rows = grad0.shape[0]
    half_width = own.shape[1]
    for out, half in ((own, info[1]), (send, 1 - info[1])):
        at = pl.multiple_of(half * half_width, half_width)
        total = None
        for p, grad in enumerate((grad0, grad1, grad2, grad3)):
            part = dot(
                context[:, p * rows : (p + 1) * rows], grad[:, pl.ds(at, half_width)], 1, 0
            )
            total = part if total is None else total + part
        out[...] = total.astype(BF)


def mix_grad(info, context, grads):
    half_width = context.shape[0]
    return pl.pallas_call(
        mix_grad_kernel,
        out_shape=(shape((half_width, half_width), BF),) * 2,
        in_specs=[SMEM] + [VMEM] * 5,
        out_specs=(VMEM,) * 2,
        compiler_params=params(16),
        cost_estimate=FREE,
        name="mix_grad",
    )(info, context, *grads)


def mix_place_kernel(blocks, info, own, recv, out, scratch):
    half_width = own.shape[1]
    quarter = half_width // 2
    x, c, shard = info[0], info[1], info[2]
    for ref, dc in ((own, 0), (recv, 1)):
        for dx in range(2):
            at = pl.multiple_of((c ^ dc) * half_width + (x ^ dx) * quarter, quarter)
            scratch[pl.ds(at, quarter), :] = ref[dx * quarter : (dx + 1) * quarter, :].astype(F32)
    block = out.shape[1]
    for b in range(blocks):
        out[order_of(range(blocks), shard, b)] = scratch[b * block : (b + 1) * block, :].astype(BF)


def mix_place(info, own, recv, blocks):
    half_width = own.shape[1]
    return pl.pallas_call(
        partial(mix_place_kernel, blocks),
        out_shape=shape((blocks, 2 * half_width // blocks, half_width), BF),
        in_specs=[SMEM, VMEM, VMEM],
        out_specs=VMEM,
        scratch_shapes=[pltpu.VMEM((2 * half_width, half_width), F32)],
        compiler_params=params(8),
        cost_estimate=FREE,
        name="mix_place",
    )(info, own, recv)


def row_tiles(rows, step, body):
    lax.fori_loop(0, rows // step, lambda i, c: body(pl.ds(pl.multiple_of(i * step, step), step), c), 0)


def mean_of(value):
    return jnp.mean(value, -1, keepdims=True)


def first_norm_kernel(
    tokens, mixed, recv0, recv1, vectors, low0, low1, normed_out, inverse_out, recv, low
):
    gain, bias = vectors[0:1, :], vectors[1:2, :]
    half = recv0.shape[0]
    recv[:half, :] = recv0[...]
    recv[half:, :] = recv1[...]

    def body(at, carry):
        hidden = tokens[at, :].astype(F32) + mixed[at, :] + recv[at, :].astype(F32)
        centred = hidden - mean_of(hidden)
        inverse = lax.rsqrt(mean_of(centred * centred) + EPSILON)
        normed = centred * inverse
        normed_out[at, :] = normed
        inverse_out[at, :] = inverse
        low[at, :] = (normed * gain + bias).astype(BF)
        return carry

    row_tiles(tokens.shape[0], 128, body)
    low0[...] = low[:half, :]
    low1[...] = low[half:, :]


def first_norm(tokens, mixed, recvs, vectors):
    rows, width = tokens.shape
    return pl.pallas_call(
        first_norm_kernel,
        grid=(1,),
        out_shape=(shape((rows // 2, width), BF),) * 2
        + (shape((rows, width), F32), shape((rows, 1), F32)),
        in_specs=[pl.BlockSpec((rows, width), lambda i: (0, 0))] * 2
        + [pl.BlockSpec((rows // 2, width), lambda i: (0, 0))] * 2
        + [pl.BlockSpec(vectors.shape, lambda i: (0, 0))],
        scratch_shapes=[pltpu.VMEM((rows, width), BF)] * 2,
        out_specs=(pl.BlockSpec((rows // 2, width), lambda i: (0, 0)),) * 2
        + (
            pl.BlockSpec((rows, width), lambda i: (0, 0)),
            pl.BlockSpec((rows, 1), lambda i: (0, 0)),
        ),
        compiler_params=params(24),
        cost_estimate=FREE,
        name="first_norm",
    )(tokens, mixed, *recvs, vectors)


def second_norm_kernel(normed_one, mlp, recv, vectors, grad, result, grad_two, grad_low, sums):
    gain_one, bias_one = vectors[0:1, :], vectors[1:2, :]
    gain, bias = vectors[2:3, :], vectors[3:4, :]
    sums[...] = jnp.zeros_like(sums)

    def body(at, carry):
        hidden = normed_one[at, :] * gain_one + bias_one + mlp[at, :] + recv[at, :].astype(F32)
        centred = hidden - mean_of(hidden)
        inverse = lax.rsqrt(mean_of(centred * centred) + EPSILON)
        normed = centred * inverse
        result[at, :] = (normed * gain + bias).astype(BF)
        grad_y = grad[at, :].astype(F32)
        grad_n = grad_y * gain
        value = inverse * (grad_n - mean_of(grad_n) - normed * mean_of(grad_n * normed))
        grad_two[at, :] = value
        grad_low[at, :] = value.astype(BF)
        sums[2:3, :] += jnp.sum(grad_y * normed, 0, keepdims=True)
        sums[3:4, :] += jnp.sum(grad_y, 0, keepdims=True)
        return carry

    row_tiles(grad.shape[0], 128, body)


def second_norm(normed_one, mlp, recv, vectors, grad):
    rows, width = grad.shape
    return pl.pallas_call(
        second_norm_kernel,
        out_shape=(
            shape((rows, width), BF),
            shape((rows, width), F32),
            shape((rows, width), BF),
            shape((8, width), F32),
        ),
        in_specs=[VMEM] * 5,
        out_specs=(VMEM,) * 4,
        compiler_params=params(24),
        cost_estimate=FREE,
        name="second_norm",
    )(normed_one, mlp, recv, vectors, grad)


def first_back_kernel(
    grad_two, own, recv0, recv1, normed_one, inverse_one, vectors, late,
    grad_one, low0, low1, sums, grad_low, recv,
):
    gain = vectors[0:1, :]
    half = low0.shape[0]
    recv[:half, :] = recv0[...]
    recv[half:, :] = recv1[...]
    sums[...] = late[...]

    def body(at, carry):
        normed = normed_one[at, :]
        grad_y = grad_two[at, :] + own[at, :] + recv[at, :].astype(F32)
        grad_n = grad_y * gain
        value = inverse_one[at, :] * (grad_n - mean_of(grad_n) - normed * mean_of(grad_n * normed))
        grad_one[at, :] = value
        grad_low[at, :] = value.astype(BF)
        sums[0:1, :] += jnp.sum(grad_y * normed, 0, keepdims=True)
        sums[1:2, :] += jnp.sum(grad_y, 0, keepdims=True)
        return carry

    row_tiles(grad_two.shape[0], 128, body)
    low0[...] = grad_low[:half, :]
    low1[...] = grad_low[half:, :]


def first_back(grad_two, own, recvs, normed_one, inverse_one, vectors, late):
    rows, width = grad_two.shape
    return pl.pallas_call(
        first_back_kernel,
        out_shape=(shape((rows, width), F32),)
        + (shape((rows // 2, width), BF),) * 2
        + (shape((8, width), F32),),
        in_specs=[VMEM] * 8,
        out_specs=(VMEM,) * 4,
        scratch_shapes=[pltpu.VMEM((rows, width), BF)] * 2,
        compiler_params=params(24),
        cost_estimate=FREE,
        name="first_back",
    )(grad_two, own, *recvs, normed_one, inverse_one, vectors, late)


def after(value, *earlier):
    return lax.optimization_barrier((value,) + earlier)[0]


def shards(
    n_shard,
    tokens,
    segment_ids,
    qkv_weight,
    out_weight,
    up_weight,
    down_weight,
    first_gain,
    first_bias,
    second_gain,
    second_bias,
    out_grad,
):
    rows, width = tokens.shape
    half_width = width // 2
    quarter = width // 4
    ff_half = up_weight.shape[1] // 2
    block = qkv_weight.shape[0]
    shard = lax.axis_index("shard").astype(jnp.int32)
    seq = lax.axis_index("seq").astype(jnp.int32)
    xb, cb = seq // 2, seq % 2
    bits = [1 << b for b in range(n_shard.bit_length() - 1)]
    top = bits[-1]
    owner = (shard // top) % 2 == cb
    low_shard = shard % top
    place = jnp.stack([xb, cb, shard])

    def swap(value, mask):
        return lax.ppermute(value, "shard", [(i, i ^ mask) for i in range(n_shard)])

    def swap_core(value):
        return lax.ppermute(value, "seq", [(i, i ^ 1) for i in range(4)])

    def swap_x(value):
        return lax.ppermute(value, "seq", [(i, i ^ 2) for i in range(4)])

    def to_core(value, to_owner):
        pairs = []
        for sh in range(n_shard):
            for se in range(4):
                sends = (sh // top == se % 2) != to_owner
                pairs.append((sh * 4 + se, (sh ^ top) * 4 + se if sends else sh * 4 + (se ^ 1)))
        return lax.ppermute(value, ("shard", "seq"), pairs)

    def join(pieces):
        return jnp.concatenate(pieces) if len(pieces) > 1 else pieces[0]

    class Gather:
        def __init__(self, own_block, over):
            self.pieces, self.offsets, self.over = [own_block[None]], [[0]], list(over)

        def swap(self, value, rel, bit):
            got = swap(value, bit)
            self.pieces.append(got)
            self.offsets.append([r ^ bit for r in rel])
            return got

        def steps(self, count, *gate):
            for bit in [self.over.pop(0) for _ in range(count)]:
                held, rel = join(self.pieces), [r for o in self.offsets for r in o]
                self.pieces, self.offsets = [held], [rel]
                gate = (self.swap(after(held, *gate), rel, bit),)
            return gate[0]

        def part(self, index, *gate):
            return self.swap(after(self.pieces[index], *gate), self.offsets[index], self.over[0])

    def fold(value, got):
        return (value[: value.shape[0] // 2].astype(F32) + got.astype(F32)).astype(BF)

    def upper(value):
        return value[value.shape[0] // 2 :]

    def add_x(value):
        return (value.astype(F32) + swap_x(value).astype(F32)).astype(BF)

    def pick(value, flag, axis):
        return jnp.where(
            flag == 0,
            lax.index_in_dim(value, 0, axis, False),
            lax.index_in_dim(value, 1, axis, False),
        )

    def ordered(flag, own, other, axis):
        return jnp.where(
            flag == 0, jnp.concatenate([own, other], axis), jnp.concatenate([other, own], axis)
        )

    over_x = swap_x(tokens)
    over_core = swap_core(tokens)
    toks = [tokens, over_core, over_x]
    plan, ids_row = make_plan(segment_ids, place)

    own_a, own_b = prepare(
        place, qkv_weight, out_weight, (first_gain, first_bias, second_gain, second_bias)
    )
    up_half = lax.dynamic_slice_in_dim(up_weight, cb * ff_half, ff_half, 1)
    down_rows = down_weight.shape[0] // 2
    down_half = lax.dynamic_slice_in_dim(down_weight, xb * down_rows, down_rows, 0)
    middle = len(bits) - 2
    gather_a = Gather(own_a, bits[::-1])
    gather_b = Gather(own_b, bits[::-1])
    gather_up = Gather(up_half, bits[::-1])
    a1 = gather_a.steps(1)
    b1 = gather_b.steps(1, a1)
    a2 = gather_a.steps(middle, plan)
    a3 = gather_a.steps(1)
    b2 = gather_b.steps(middle, a2, up_half, down_half)
    d1 = to_core(after(down_half, b1), False)
    toks.append(swap_core(after(over_x, b2)))
    b3 = gather_b.steps(1, a3)
    part_a = assemble(gather_a.pieces, gather_a.offsets, shard)
    vectors = vectors_of(part_a)
    far_a = swap_x(part_a)

    saved, own_ctx, sends = [], [], []

    def head(j, weight, *gate):
        ctx_own, ctx_send, ctx_full, lse = attend(
            plan, toks, weight, after(ids_row, *gate)
        )
        own_ctx.append(ctx_own)
        sends.append(ctx_send)
        saved.append((ctx_full, lse))
        return ctx_own

    ctx = head(0, part_a[:, :TRIO], b2, vectors)
    d1, b3 = after(d1, ctx), after(b3, ctx)
    gather_b.pieces[1] = b3
    gather_down = Gather(jnp.where(owner, down_half, d1), bits[-2::-1])
    d2 = gather_down.steps(middle)
    u1 = gather_up.steps(1, ctx)
    part_b = assemble(gather_b.pieces, gather_b.offsets, shard)
    far_b = swap_x(part_b[:, : 2 * TRIO])
    ctx = head(1, part_b[:, :TRIO], gather_down.pieces[0])
    d2, u1 = after(d2, ctx), after(u1, ctx)
    gather_down.pieces[1], gather_up.pieces[1] = d2, u1
    d3 = gather_down.steps(1)
    u2 = gather_up.steps(middle)
    ctx = head(2, part_b[:, TRIO : 2 * TRIO], gather_down.pieces[0], gather_up.pieces[0], far_a, far_b)
    d3, u2 = after(d3, ctx), after(u2, ctx)
    gather_down.pieces[1], gather_up.pieces[1] = d3, u2
    held_up = join(gather_up.pieces)
    held = join(gather_down.pieces)
    gather_up.offsets = [[r for o in gather_up.offsets for r in o]]
    sends[2], held_up, held = lax.optimization_barrier((sends[2], held_up, held))
    gather_up.pieces = [held_up]
    gather_up.part(0)
    others = [swap_x(value) for value in sends]
    rel = [2 * r for o in gather_down.offsets for r in o]
    widen = assemble(gather_up.pieces, gather_up.offsets, shard)
    held_far = swap_x(held)
    head_weights = [part_a[:, :TRIO], part_b[:, :TRIO], part_b[:, TRIO : 2 * TRIO]]
    far_weights = [far_a, far_b[:, :TRIO], far_b[:, TRIO:]]
    mixer = part_b[:, 2 * TRIO :].reshape(2, half_width, half_width)
    mixer = ordered(cb, pick(mixer, cb, 0), swap_core(pick(mixer, 1 - cb, 0)), 1)
    mixer = jnp.where(xb == 0, mixer, jnp.concatenate([mixer[quarter:], mixer[:quarter]]))
    context = jnp.concatenate(own_ctx + others)

    mixed = dot(context, mixer, 0, 0)
    low0, low1, normed_one, inverse_one = first_norm(
        tokens,
        mixed,
        [swap_core(mixed[at : at + rows // 2].astype(BF)) for at in (rows, rows + rows // 2)],
        vectors,
    )
    act_low, act_t, slope, low_t = feed_up([low0, low1, swap_core(low0), swap_core(low1)], widen)
    held_far = after(held_far, act_low)
    narrow = assemble([held, held_far], [rel, [r + 1 for r in rel]], low_shard * 2 + xb)
    mlp_own, mlp_send = feed_down(act_low, narrow)
    result, grad_two, grad_mlp, late = second_norm(
        normed_one, mlp_own, swap_core(mlp_send), vectors, out_grad
    )

    grad_mlp = [grad_mlp, swap_core(grad_mlp)]
    narrow_grad = weight_grad(low_shard, act_t, grad_mlp, n_shard // 2, False)
    n1 = swap(upper(narrow_grad), bits[-2])
    first_own, send0, send1, grad_pre = feed_back(
        after(grad_mlp[0], narrow_grad), grad_mlp[1], slope, widen, narrow
    )
    widen_grad = weight_grad(shard, low_t, [grad_pre], n_shard)
    w1 = swap(upper(widen_grad), bits[0])
    recv0, recv1, _ = lax.optimization_barrier((swap_core(send0), swap_core(send1), widen_grad))
    grad_one, attn0, attn1, sums = first_back(
        grad_two, first_own, [recv0, recv1], normed_one, inverse_one, vectors, late
    )
    attn = [attn0, attn1, swap_core(attn0), swap_core(attn1)]
    g_own, g_send = mix_back(mixer, attn)
    mixer_own, mixer_send = mix_grad(place, after(context, g_send), attn)
    g_recv = swap_x(g_send)
    mixer_grad = mix_place(place, mixer_own, swap_core(mixer_send), n_shard)

    def head_back(j, before, *gate):
        at = j * HEAD_DIM
        return attend_back(
            plan, place, toks, head_weights[j], after(ids_row, *gate),
            g_own[at : at + HEAD_DIM], g_recv[at : at + HEAD_DIM], *saved[j],
            sums if j == 2 else None, before, n_shard,
        )

    keeps, sends = [None] * 3, [None] * 3
    keeps[0], sends[0], early = head_back(0, mixer_grad)
    fars = [swap_x(sends[0])]
    narrow_grad = fold(narrow_grad, after(n1, early))
    for bit in bits[-3:0:-1]:
        narrow_grad = fold(narrow_grad, swap(upper(narrow_grad), bit))
    n2 = swap(upper(narrow_grad), bits[0])
    widen_grad = fold(widen_grad, after(w1, narrow_grad))
    for bit in bits[1:-2]:
        widen_grad = fold(widen_grad, swap(upper(widen_grad), bit))
    w2 = swap(upper(widen_grad), bits[-2])
    keeps[1], sends[1], part = head_back(1, None, narrow_grad, widen_grad)
    fars.append(swap_x(sends[1]))
    narrow_grad = fold(narrow_grad, after(n2, part))[0]
    n3 = to_core(narrow_grad, True)
    widen_grad = fold(widen_grad, after(w2, narrow_grad, fars[0]))
    w3 = swap(upper(widen_grad), bits[-1])
    early = after(early, narrow_grad, widen_grad)
    e1 = swap(upper(early), bits[0])
    keeps[2], sends[2], late = head_back(2, part, narrow_grad, widen_grad)
    fars.append(swap_x(sends[2]))
    widen_grad = fold(widen_grad, after(w3, late, fars[1]))[0]
    early = fold(early, after(e1, widen_grad))
    e2 = swap(upper(early), bits[1])
    late = after(late, widen_grad, early)
    l1 = swap(upper(late), bits[0])
    w4 = swap_x(widen_grad)
    late = fold(late, after(l1, fars[2]))
    l2 = swap(upper(late), bits[1])
    fars[2] = after(fars[2], late)
    back_own, back_core = input_back(keeps + fars, head_weights + far_weights, rows)
    back_near = swap_core(back_core)
    late = fold(late, after(l2, w4, back_core))
    for bit in bits[2:-1]:
        late = fold(late, swap(upper(late), bit))
    l3 = swap(upper(late), bits[-1])
    early = fold(early, after(e2, late))
    for bit in bits[2:-1]:
        early = fold(early, swap(upper(early), bit))
    e3 = swap(upper(early), bits[-1])
    narrow_grad = (narrow_grad.astype(F32) + after(n3, early).astype(F32)).astype(BF)
    halves = narrow_grad.reshape(2, -1, width)
    narrow_half = swap_core(pick(halves, 1 - cb, 0))
    narrow_half = jnp.where(owner, pick(halves, cb, 0), narrow_half)
    n4 = swap_x(narrow_half)
    widen_grad = (widen_grad.astype(F32) + after(w4, late).astype(F32)).astype(BF)
    widen_other = swap_core(widen_grad)
    input_grad = grad_one + back_own + after(back_near, late).astype(F32)
    early = fold(early, after(e3, narrow_half))[0]
    late = fold(late, after(l3, early))[0]
    mine = jnp.concatenate([early, late], 1)
    theirs = swap_x(mine)
    narrow_half = (narrow_half.astype(F32) + after(n4, mine).astype(F32)).astype(BF)
    narrow_other = swap_core(narrow_half)
    widen_grad = ordered(cb, widen_grad, widen_other, 1)
    narrow_grad = ordered(cb, narrow_half, narrow_other, 0)
    narrow_grad, widen_grad = narrow_grad.astype(F32), widen_grad.astype(F32)
    theirs = after(theirs, narrow_grad, widen_grad, input_grad)
    mixer_grad = (mine[:, :half_width].astype(F32) + theirs[:, :half_width].astype(F32)).astype(BF)
    chip = jnp.concatenate([mixer_grad, mine[:, half_width:], theirs[:, half_width:]], 1)
    other = swap_core(chip)
    mixer_grad = ordered(cb, mixer_grad, other[:, :half_width], 1)
    qkv_grad, sums = place_qkv(place, chip, other, half_width, width)
    return (
        result,
        input_grad,
        qkv_grad,
        mixer_grad.astype(F32),
        widen_grad,
        narrow_grad,
        sums[:, 0],
        sums[:, 1],
        sums[:, 2],
        sums[:, 3],
    )


def solution(mesh):
    placed = (
        P(("shard", "seq"), None),
        P("shard", None),
        P("shard", None),
        P("shard", None),
        P("shard", None),
        P("shard", None),
        P("shard"),
        P("shard"),
        P("shard"),
        P("shard"),
        P(("shard", "seq"), None),
    )
    return jax.shard_map(
        partial(shards, mesh.shape["shard"]),
        mesh=mesh,
        in_specs=placed,
        out_specs=(
            P(("shard", "seq"), None),
            P(("shard", "seq"), None),
            P("shard", None),
            P("shard", None),
            P("shard", None),
            P("shard", None),
            P("shard"),
            P("shard"),
            P("shard"),
            P("shard"),
        ),
        check_vma=False,
    )
```

```python
from functools import partial

import jax
import jax.numpy as jnp
from jax import lax
from jax.experimental import pallas as pl
from jax.experimental.pallas import tpu as pltpu
from jax.sharding import PartitionSpec as P

HEADS = 12
HEAD_DIM = 64
TRIO = 3 * HEAD_DIM
GROUPS = 16
EPSILON = 1e-12
FAR = -(2.0**30)
SCALE = HEAD_DIM**-0.5
TILE = 256
UNROLL = 2
BF = jnp.bfloat16
F32 = jnp.float32
VMEM = pl.BlockSpec(memory_space=pltpu.VMEM)
SMEM = pl.BlockSpec(memory_space=pltpu.SMEM)
FREE = pl.CostEstimate(flops=1, bytes_accessed=1, transcendentals=0)


def dot(a, b, ca, cb):
    return lax.dot_general(a, b, (((ca,), (cb,)), ((), ())), preferred_element_type=F32)


def shape(dims, kind):
    return jax.ShapeDtypeStruct(dims, kind)


def params(mebi):
    return pltpu.CompilerParams(vmem_limit_bytes=mebi << 20)


def assemble_kernel(offsets, info, *refs):
    out, sem = refs[-2:]
    copies = []
    for ref, rel in zip(refs[:-2], offsets):
        block = ref.shape[1]
        for i, r in enumerate(rel):
            at = pl.multiple_of((info[0] ^ r) * block, block)
            copies.append(
                pltpu.make_async_copy(ref.at[i], out.at[pl.ds(at, block), :], sem.at[len(copies)])
            )
    for copy in copies:
        copy.start()
    for copy in copies:
        copy.wait()


def assemble(pieces, offsets, me):
    block, cols = pieces[0].shape[1:]
    count = sum(len(r) for r in offsets)
    if block % 16:
        value = jnp.concatenate(pieces)
        order = [r for rel in offsets for r in rel]
        place = jnp.array([order.index(r) for r in range(count)], jnp.int32)
        return value[place[me ^ jnp.arange(count)]].reshape(count * block, cols)
    return pl.pallas_call(
        partial(assemble_kernel, offsets),
        out_shape=shape((count * block, cols), BF),
        in_specs=[SMEM] + [pl.BlockSpec(memory_space=pltpu.HBM)] * len(pieces),
        out_specs=VMEM,
        scratch_shapes=[pltpu.SemaphoreType.DMA((count,))],
        compiler_params=params(12),
        cost_estimate=FREE,
        name="assemble",
    )(me[None], *[pltpu.with_memory_space_constraint(p, pltpu.HBM) for p in pieces])


def prepare_kernel(info, qkv_far, out_far, *refs):
    vectors, (part_a, part_b, qkv, out_weight, rows, scratch, sem) = refs[:4], refs[4:]
    block, width = out_weight.shape
    half, quarter = width // 2, width // 4
    copies = [
        pltpu.make_async_copy(qkv_far, qkv, sem.at[0]),
        pltpu.make_async_copy(out_far, out_weight, sem.at[1]),
    ] + [pltpu.make_async_copy(v, rows.at[i], sem.at[2 + i]) for i, v in enumerate(vectors)]
    for copy in copies:
        copy.start()
    scratch[...] = jnp.zeros_like(scratch)
    for copy in copies:
        copy.wait()
    for i in range(4):
        scratch[i : i + 1, :block] = rows[i].astype(F32)
    part_a[:, TRIO:] = scratch[...].T[:block, : 256 - TRIO].astype(BF)
    for x in range(2):
        for c in range(2):

            @pl.when(jnp.logical_and(info[0] == x, info[1] == c))
            def _():
                at = c * half + x * quarter
                trio = [qkv[:, i * width + at : i * width + at + quarter] for i in range(3)]
                for j in range(3):
                    piece = jnp.concatenate(
                        [t[:, j * HEAD_DIM : (j + 1) * HEAD_DIM] for t in trio], 1
                    )
                    if j == 0:
                        part_a[:, :TRIO] = piece
                    else:
                        part_b[:, (j - 1) * TRIO : j * TRIO] = piece
                part_b[:, 2 * TRIO :] = out_weight[:, c * half : (c + 1) * half]


def prepare(info, qkv, out_weight, vectors):
    block, width = out_weight.shape
    far = [qkv, out_weight] + [v[None] for v in vectors]
    return pl.pallas_call(
        prepare_kernel,
        out_shape=(shape((block, 256), BF), shape((block, 2 * TRIO + width // 2), BF)),
        in_specs=[SMEM] + [pl.BlockSpec(memory_space=pltpu.HBM)] * 6,
        out_specs=(VMEM, VMEM),
        scratch_shapes=[
            pltpu.VMEM(qkv.shape, BF),
            pltpu.VMEM(out_weight.shape, BF),
            pltpu.VMEM((4, 1, block), BF),
            pltpu.VMEM((128, 128), F32),
            pltpu.SemaphoreType.DMA((6,)),
        ],
        compiler_params=params(8),
        cost_estimate=FREE,
        name="prepare",
    )(info, *[pltpu.with_memory_space_constraint(v, pltpu.HBM) for v in far])


def vectors_kernel(part, out):
    out[...] = part[:, 128:].astype(F32).T[TRIO - 128 : TRIO - 120]


def vectors_of(part):
    return pl.pallas_call(
        vectors_kernel,
        out_shape=shape((8, part.shape[0]), F32),
        in_specs=[VMEM],
        out_specs=VMEM,
        compiler_params=params(8),
        cost_estimate=FREE,
        name="vectors",
    )(part)


def doc_rows(ids_ref, same, other):
    ids = ids_ref[...]
    rows = lax.broadcasted_iota(jnp.int32, (GROUPS, ids.shape[1]), 0)
    return jnp.where(rows == ids, same, other).astype(BF)


def plan_kernel(ids_s, ids_v, place, plan, row):
    total = ids_v.shape[1]
    tiles = total // TILE
    chunk = total // 4
    me = place[0] * 2 + place[1]
    entries = (plan.shape[0] - 1) // 2
    for i in range(2 * entries):
        plan[1 + i] = jnp.int32(tiles)
    first = [ids_s[0, i * TILE] for i in range(tiles)]
    last = [ids_s[0, i * TILE + TILE - 1] for i in range(tiles)]
    flip = me * (chunk // TILE)
    count = jnp.int32(0)
    for i in range(tiles):
        for j in range(tiles):
            meet = jnp.logical_and(first[i] <= last[j], first[j] <= last[i])

            @pl.when(meet)
            def _():
                plan[1 + 2 * UNROLL + count] = i ^ flip
                plan[1 + entries + 2 * UNROLL + count] = j ^ flip

            count = count + meet.astype(jnp.int32)
    plan[0] = (count + UNROLL - 1) // UNROLL
    for r in range(4):
        at = pl.multiple_of((me ^ r) * chunk, chunk)
        row[:, r * chunk : (r + 1) * chunk] = ids_v[:, pl.ds(at, chunk)]


def make_plan(ids, place):
    total = ids.shape[1]
    entries = (total // TILE) ** 2 + 4 * UNROLL
    return pl.pallas_call(
        plan_kernel,
        out_shape=(shape((1 + 2 * entries,), jnp.int32), shape((1, total), jnp.int32)),
        in_specs=[SMEM, VMEM, SMEM],
        out_specs=(SMEM, VMEM),
        compiler_params=params(8),
        cost_estimate=FREE,
        name="plan",
    )(ids, ids, place)


def tile_of(plan, entry):
    return pl.multiple_of(plan[1 + entry] * TILE, TILE)


def attend_kernel(
    plan, tok0, tok1, tok2, tok3, weight, ids_ref, ctx_own, ctx_send, ctx_full, lse,
    q_t, k_nat, v_t, s_ref, p_ref, fade, top, sums, acc,
):
    total = ids_ref.shape[1]
    half = total // 2
    entries = (plan.shape[0] - 1) // 2
    weight_t = weight[...].T
    keys = weight[:, HEAD_DIM : 2 * HEAD_DIM]
    for i, tok in enumerate((tok0, tok1, tok2, tok3)):
        rows = tok[...]
        at, end = i * rows.shape[0], (i + 1) * rows.shape[0]
        trio = dot(weight_t, rows, 1, 1).astype(BF)
        q_t[:HEAD_DIM, at:end] = trio[:HEAD_DIM] * SCALE
        v_t[:, at:end] = trio[2 * HEAD_DIM :]
        k_nat[at:end, :HEAD_DIM] = dot(rows, keys, 1, 0).astype(BF)
    q_t[HEAD_DIM : HEAD_DIM + GROUPS, :total] = doc_rows(ids_ref, 0.0, FAR)
    q_t[HEAD_DIM + GROUPS :, :total] = jnp.zeros((128 - HEAD_DIM - GROUPS, total), BF)
    docs = jnp.concatenate(
        [doc_rows(ids_ref, 1.0, 0.0), jnp.zeros((128 - HEAD_DIM - GROUPS, total), BF)], 0
    )
    k_nat[:total, HEAD_DIM:] = docs.T
    top[...] = jnp.full_like(top, -3e38)
    sums[...] = jnp.zeros_like(sums)
    acc[...] = jnp.zeros_like(acc)

    def step(j, carry):
        i = j * UNROLL
        for u in range(UNROLL):
            q, k = tile_of(plan, i + u), tile_of(plan, entries + i + u)
            acc[:, pl.ds(q, TILE)] = acc[:, pl.ds(q, TILE)] * fade[u] + dot(
                v_t[:, pl.ds(k, TILE)], p_ref[u], 1, 0
            )
        peaks = [jnp.max(s_ref[u], 0, keepdims=True) for u in range(UNROLL)]
        for u in range(UNROLL):
            q = tile_of(plan, i + UNROLL + u)
            old = top[:, pl.ds(q, TILE)]
            new = jnp.maximum(old, peaks[u])
            powers = jnp.exp(s_ref[u] - new)
            decay = jnp.exp(old - new)
            top[:, pl.ds(q, TILE)] = new
            sums[:, pl.ds(q, TILE)] = sums[:, pl.ds(q, TILE)] * decay + jnp.sum(
                powers, 0, keepdims=True
            )
            fade[u] = decay
            p_ref[u] = powers.astype(BF)
        for u in range(UNROLL):
            q = tile_of(plan, i + 2 * UNROLL + u)
            k = tile_of(plan, entries + i + 2 * UNROLL + u)
            s_ref[u] = dot(k_nat[pl.ds(k, TILE), :], q_t[:, pl.ds(q, TILE)], 1, 0)
        return carry

    lax.fori_loop(0, plan[0] + 2, step, 0)
    ctx_full[...] = acc[:, :total] / sums[:, :total]
    lse[...] = top[:, :total] + jnp.log(sums[:, :total])
    ctx_own[...] = ctx_full[:, :half].astype(BF)
    ctx_send[...] = ctx_full[:, half:].astype(BF)


def attend(plan, toks, weight, ids):
    total = ids.shape[1]
    half = total // 2
    padded = total + TILE
    return pl.pallas_call(
        attend_kernel,
        out_shape=(
            shape((HEAD_DIM, half), BF),
            shape((HEAD_DIM, half), BF),
            shape((HEAD_DIM, total), F32),
            shape((1, total), F32),
        ),
        in_specs=[SMEM] + [VMEM] * 6,
        out_specs=(VMEM,) * 4,
        scratch_shapes=[
            pltpu.VMEM((128, padded), BF),
            pltpu.VMEM((padded, 128), BF),
            pltpu.VMEM((HEAD_DIM, padded), BF),
            pltpu.VMEM((UNROLL, TILE, TILE), F32),
            pltpu.VMEM((UNROLL, TILE, TILE), BF),
            pltpu.VMEM((UNROLL, 1, TILE), F32),
            pltpu.VMEM((1, padded), F32),
            pltpu.VMEM((1, padded), F32),
            pltpu.VMEM((HEAD_DIM, padded), F32),
        ],
        compiler_params=params(20),
        cost_estimate=FREE,
        name="attend",
    )(plan, *toks, weight, ids)


def attend_back_kernel(
    order, plan, place, tok0, tok1, tok2, tok3, weight, ids_ref, g_own, g_recv, ctx_full, lse_in,
    sums, before, keep, send, grad_out,
    q_t, kvd, k_t, g_t, qg_nat, lse, row_term, s_ref, d_ref, p_ref, e_ref, acc, dq_t, w_grad, out,
):
    total = ids_ref.shape[1]
    half = total // 2
    entries = (plan.shape[0] - 1) // 2
    toks = (tok0, tok1, tok2, tok3)
    chunk = tok0.shape[0]
    weight_t = weight[:, : 2 * HEAD_DIM].T
    natural_w = weight[:, HEAD_DIM:]
    for at, grad in ((0, g_own), (half, g_recv)):
        g_t[HEAD_DIM:, at : at + half] = grad[...]
    g_t[:HEAD_DIM, :total] = jnp.zeros((HEAD_DIM, total), BF)
    for i, tok in enumerate(toks):
        at, end = i * chunk, (i + 1) * chunk
        rows = tok[...]
        pair = dot(weight_t, rows, 1, 1).astype(BF)
        q_t[:HEAD_DIM, at:end] = pair[:HEAD_DIM] * SCALE
        k_t[:, at:end] = pair[HEAD_DIM:]
        kvd[at:end, :128] = dot(rows, natural_w, 1, 0).astype(BF)
    qg_nat[:total, :] = jnp.concatenate([q_t[:HEAD_DIM, :total], g_t[HEAD_DIM:, :total]], 0).T
    q_t[HEAD_DIM:128, :total] = jnp.zeros((128 - HEAD_DIM, total), BF)
    q_t[128 : 128 + GROUPS, :total] = doc_rows(ids_ref, 0.0, FAR)
    q_t[128 + GROUPS :, :total] = jnp.zeros((128 - GROUPS, total), BF)
    kvd[:total, 128:] = jnp.concatenate(
        [doc_rows(ids_ref, 1.0, 0.0), jnp.zeros((128 - GROUPS, total), BF)], 0
    ).T
    acc[...] = jnp.zeros_like(acc)
    dq_t[...] = jnp.zeros_like(dq_t)
    lse[:, :total] = lse_in[...]
    row_term[:, :total] = jnp.sum(
        ctx_full[...] * g_t[HEAD_DIM:, :total].astype(F32), 0, keepdims=True
    )
    left = lax.broadcasted_iota(jnp.int32, (TILE, 128), 1) < HEAD_DIM

    def step(j, carry):
        i = j * UNROLL
        for u in range(UNROLL):
            q, k = tile_of(plan, i + u), tile_of(plan, entries + i + u)
            grad_scores, chance = e_ref[u], p_ref[u]
            natural = qg_nat[pl.ds(q, TILE), :]
            dq_t[:, pl.ds(q, TILE)] += dot(k_t[:, pl.ds(k, TILE)], grad_scores, 1, 0)
            acc[pl.ds(k, TILE), :] += jnp.where(
                left, dot(grad_scores, natural, 1, 0), dot(chance, natural, 1, 0)
            )
        for u in range(UNROLL):
            q = tile_of(plan, i + UNROLL + u)
            chance = jnp.exp(s_ref[u] - lse[:, pl.ds(q, TILE)])
            p_ref[u] = chance.astype(BF)
            e_ref[u] = (chance * (d_ref[u] - row_term[:, pl.ds(q, TILE)])).astype(BF)
        for u in range(UNROLL):
            q = tile_of(plan, i + 2 * UNROLL + u)
            rows = kvd[pl.ds(tile_of(plan, entries + i + 2 * UNROLL + u), TILE), :]
            s_ref[u] = dot(rows, q_t[:, pl.ds(q, TILE)], 1, 0)
            d_ref[u] = dot(rows[:, :128], g_t[:, pl.ds(q, TILE)], 1, 0)
        return carry

    lax.fori_loop(0, plan[0] + 2, step, 0)
    out[:HEAD_DIM, :] = (dq_t[:, :total] * SCALE).astype(BF)
    out[HEAD_DIM:, :] = acc[:total, :].T.astype(BF)
    keep[...] = out[:, :half]
    send[...] = out[:, half:]
    for i, tok in enumerate(toks):
        part = dot(out[:, i * chunk : (i + 1) * chunk], tok[...], 1, 0)
        w_grad[:TRIO, :] = part if i == 0 else w_grad[:TRIO, :] + part
    if sums is not None:
        w_grad[TRIO : TRIO + 8, :] = sums[...]
        w_grad[TRIO + 8 :, :] = jnp.zeros((256 - TRIO - 8, w_grad.shape[1]), F32)
    else:
        w_grad[TRIO:, :] = jnp.zeros((256 - TRIO, w_grad.shape[1]), F32)
    natural = w_grad[...].T
    block = grad_out.shape[1]
    for b in range(len(order)):
        to = order_of(order, place[2], b)
        value = natural[b * block : (b + 1) * block].astype(BF)
        if before is None:
            grad_out[to] = value
        else:
            ahead = before.shape[2]
            grad_out[to, :, :ahead] = before[to]
            grad_out[to, :, ahead:] = value


def order_of(order, me, b):
    rel = me ^ b
    bits = len(order).bit_length() - 1
    place = 0
    for i in range(bits):
        place = place | (((rel >> i) & 1) << (bits - 1 - i))
    return place


def attend_back(plan, place, toks, weight, ids, g_own, g_recv, ctx_full, lse, sums, before, n_shard):
    total = ids.shape[1]
    width = weight.shape[0]
    padded = total + TILE
    extra = [value for value in (sums, before) if value is not None]
    cols = 256 + (0 if before is None else before.shape[2])

    def kernel(*refs):
        refs = list(refs)
        if sums is None:
            refs.insert(12, None)
        if before is None:
            refs.insert(13, None)
        attend_back_kernel(range(n_shard), *refs)

    return pl.pallas_call(
        kernel,
        out_shape=(shape((TRIO, total // 2), BF),) * 2
        + (shape((n_shard, width // n_shard, cols), BF),),
        in_specs=[SMEM, SMEM] + [VMEM] * (10 + len(extra)),
        out_specs=(VMEM,) * 3,
        scratch_shapes=[
            pltpu.VMEM((256, padded), BF),
            pltpu.VMEM((padded, 256), BF),
            pltpu.VMEM((HEAD_DIM, padded), BF),
            pltpu.VMEM((128, padded), BF),
            pltpu.VMEM((padded, 128), BF),
            pltpu.VMEM((1, padded), F32),
            pltpu.VMEM((1, padded), F32),
            pltpu.VMEM((UNROLL, TILE, TILE), F32),
            pltpu.VMEM((UNROLL, TILE, TILE), F32),
            pltpu.VMEM((UNROLL, TILE, TILE), BF),
            pltpu.VMEM((UNROLL, TILE, TILE), BF),
            pltpu.VMEM((padded, 128), F32),
            pltpu.VMEM((HEAD_DIM, padded), F32),
            pltpu.VMEM((256, width), F32),
            pltpu.VMEM((TRIO, total), BF),
        ],
        compiler_params=params(24),
        cost_estimate=FREE,
        name="attend_back",
    )(plan, place, *toks, weight, ids, g_own, g_recv, ctx_full, lse, *extra)


def input_back_kernel(*refs):
    grads, weights, (own, send), (tall, wide) = refs[:6], refs[6:12], refs[12:14], refs[14:]
    rows = own.shape[0]
    step = 256
    for i, (grad, weight) in enumerate(zip(grads, weights)):
        tall[i * TRIO : (i + 1) * TRIO, :] = grad[...]
        wide[:, i * TRIO : (i + 1) * TRIO] = weight[:, :TRIO]

    def body(i, carry):
        at = pl.multiple_of(i * step, step)
        part = dot(tall[:, pl.ds(at, step)].T, wide[...], 1, 1)

        @pl.when(at < rows)
        def _():
            own[pl.ds(at, step), :] = part

        @pl.when(at >= rows)
        def _():
            send[pl.ds(pl.multiple_of(at - rows, step), step), :] = part.astype(BF)

        return carry

    lax.fori_loop(0, 2 * rows // step, body, 0)


def input_back(grads, weights, rows):
    width = weights[0].shape[0]
    return pl.pallas_call(
        input_back_kernel,
        out_shape=(shape((rows, width), F32), shape((rows, width), BF)),
        in_specs=[VMEM] * 12,
        out_specs=(VMEM,) * 2,
        scratch_shapes=[pltpu.VMEM((6 * TRIO, 2 * rows), BF), pltpu.VMEM((width, 6 * TRIO), BF)],
        compiler_params=params(24),
        cost_estimate=FREE,
        name="input_back",
    )(*grads, *weights)


def place_qkv_kernel(start, info, chip, other, out, sums_out):
    part = out.shape[1] // 3
    x, c = info[0] == 0, info[1] == 0
    values = [
        ref[:, start + dx * 768 : start + (dx + 1) * 768].astype(F32)
        for ref in (chip, other)
        for dx in range(2)
    ]
    tail = [v[:, 2 * 256 + TRIO : 2 * 256 + TRIO + 8] for v in values]
    sums_out[...] = tail[0] + tail[1] + tail[2] + tail[3]
    for sec in range(3):
        at = sec * HEAD_DIM
        near, near_x, far, far_x = [
            jnp.concatenate(
                [v[:, j * 256 + at : j * 256 + at + HEAD_DIM] for j in range(3)], 1
            )
            for v in values
        ]
        near, near_x = jnp.where(x, near, near_x), jnp.where(x, near_x, near)
        far, far_x = jnp.where(x, far, far_x), jnp.where(x, far_x, far)
        out[:, sec * part : (sec + 1) * part] = jnp.concatenate(
            [
                jnp.where(c, near, far),
                jnp.where(c, near_x, far_x),
                jnp.where(c, far, near),
                jnp.where(c, far_x, near_x),
            ],
            1,
        )


def place_qkv(info, chip, other, start, width):
    block = chip.shape[0]
    return pl.pallas_call(
        partial(place_qkv_kernel, start),
        out_shape=(shape((block, 3 * width), F32), shape((block, 8), F32)),
        in_specs=[SMEM] + [VMEM] * 2,
        out_specs=(VMEM, VMEM),
        compiler_params=params(8),
        cost_estimate=FREE,
        name="place_qkv",
    )(info, chip, other)


def gelu_both(u):
    root = 0.7978845608028654
    cube = 0.044715 * root
    square = u * u
    t = jnp.tanh(u * (root + cube * square))
    half = 0.5 * (1.0 + t)
    act = u * half
    slope = half + act * (1.0 - t) * (root + 3.0 * cube * square)
    return act, slope


def feed_up_kernel(low0, low1, low2, low3, up, act_out, act_t, slope_out, low_t, low):
    step = low0.shape[0]
    for p, piece in enumerate((low0, low1, low2, low3)):
        low[p * step : (p + 1) * step, :] = piece[...]

    def body(i, carry):
        at = pl.multiple_of(i * step, step)
        value = low[pl.ds(at, step), :]
        low_t[:, pl.ds(at, step)] = value.T
        act, slope = gelu_both(dot(value, up[...], 1, 0))
        act = act.astype(BF)
        act_out[pl.ds(at, step), :] = act
        act_t[:, pl.ds(at, step)] = act.T
        slope_out[pl.ds(at, step), :] = slope.astype(BF)
        return carry

    lax.fori_loop(0, 4, body, 0)


def feed_up(lows, up):
    rows, width = lows[0].shape
    hidden = up.shape[1]
    return pl.pallas_call(
        feed_up_kernel,
        out_shape=(
            shape((4 * rows, hidden), BF),
            shape((hidden, 4 * rows), BF),
            shape((4 * rows, hidden), BF),
            shape((width, 4 * rows), BF),
        ),
        in_specs=[VMEM] * 5,
        out_specs=(VMEM,) * 4,
        scratch_shapes=[pltpu.VMEM((4 * rows, width), BF)],
        compiler_params=params(32),
        cost_estimate=FREE,
        name="feed_up",
    )(*lows, up)


def feed_down_kernel(act, down, own, send):
    rows = own.shape[0]
    step = 256

    def body(i, carry):
        at = pl.multiple_of(i * step, step)
        part = dot(act[pl.ds(at, step), :], down[...], 1, 0)

        @pl.when(at < rows)
        def _():
            own[pl.ds(at, step), :] = part

        @pl.when(at >= rows)
        def _():
            send[pl.ds(pl.multiple_of(at - rows, step), step), :] = part.astype(BF)

        return carry

    lax.fori_loop(0, 2 * rows // step, body, 0)


def feed_down(act, down):
    rows, hidden = act.shape
    width = down.shape[1]
    return pl.pallas_call(
        feed_down_kernel,
        out_shape=(shape((rows // 2, width), F32), shape((rows // 2, width), BF)),
        in_specs=[VMEM] * 2,
        out_specs=(VMEM,) * 2,
        compiler_params=params(24),
        cost_estimate=FREE,
        name="feed_down",
    )(act, down)


def feed_back_kernel(
    grad_own, grad_other, slope, up, down, own, send0, send1, pre_out, grad, send
):
    rows = grad_own.shape[0]
    step = 256
    grad[:rows, :] = grad_own[...]
    grad[rows:, :] = grad_other[...]

    def body(i, carry):
        at = pl.multiple_of(i * step, step)
        pre = dot(grad[pl.ds(at, step), :], down[...], 1, 1)
        pre = (pre * slope[pl.ds(at, step), :].astype(F32)).astype(BF)
        pre_out[pl.ds(at, step), :] = pre
        part = dot(pre, up[...], 1, 1)

        @pl.when(at < rows)
        def _():
            own[pl.ds(at, step), :] = part

        @pl.when(at >= rows)
        def _():
            send[pl.ds(pl.multiple_of(at - rows, step), step), :] = part.astype(BF)

        return carry

    lax.fori_loop(0, 2 * rows // step, body, 0)
    send0[...] = send[: rows // 2, :]
    send1[...] = send[rows // 2 :, :]


def feed_back(grad_own, grad_other, slope, up, down):
    rows, width = grad_own.shape
    hidden = up.shape[1]
    return pl.pallas_call(
        feed_back_kernel,
        out_shape=(
            shape((rows, width), F32),
            shape((rows // 2, width), BF),
            shape((rows // 2, width), BF),
            shape((2 * rows, hidden), BF),
        ),
        in_specs=[VMEM] * 5,
        out_specs=(VMEM,) * 4,
        scratch_shapes=[pltpu.VMEM((2 * rows, width), BF), pltpu.VMEM((rows, width), BF)],
        compiler_params=params(32),
        cost_estimate=FREE,
        name="feed_back",
    )(grad_own, grad_other, slope, up, down)


def weight_grad_kernel(blocks, reverse, shard, left, right_own, right_other, out):
    rows, cols = left.shape[0], out.shape[2]
    half = left.shape[1] // 2
    step = 256
    block = out.shape[1]
    lone = right_other is None

    def body(i, carry):
        at = pl.multiple_of(i * step, step)
        if lone:
            value = dot(left[...], right_own[:, pl.ds(at, step)], 1, 0)
        else:
            value = dot(left[:, :half], right_own[:, pl.ds(at, step)], 1, 0) + dot(
                left[:, half:], right_other[:, pl.ds(at, step)], 1, 0
            )
        for b in range(blocks):
            to = order_of(range(blocks), shard[0], b) if reverse else shard[0] ^ b
            out[to, :, pl.ds(at, step)] = value[
                b * block : (b + 1) * block
            ].astype(BF)
        return carry

    lax.fori_loop(0, cols // step, body, 0)


def weight_grad(shard, left, rights, blocks, reverse=True):
    rows, cols = left.shape[0], rights[0].shape[1]

    def kernel(*refs):
        refs = list(refs)
        if len(rights) == 1:
            refs.insert(3, None)
        weight_grad_kernel(blocks, reverse, *refs)

    return pl.pallas_call(
        kernel,
        out_shape=shape((blocks, rows // blocks, cols), BF),
        in_specs=[SMEM, VMEM] + [VMEM] * len(rights),
        out_specs=VMEM,
        compiler_params=params(24),
        cost_estimate=FREE,
        name="weight_grad",
    )(shard[None], left, *rights)


def mix_back_kernel(mixer, grad0, grad1, grad2, grad3, g_own, g_send):
    quarter = g_own.shape[0]
    rows = grad0.shape[0]
    for p, grad in enumerate((grad0, grad1, grad2, grad3)):
        value = dot(mixer[...], grad[...], 1, 1).astype(BF)
        g_own[:, p * rows : (p + 1) * rows] = value[:quarter]
        g_send[:, p * rows : (p + 1) * rows] = value[quarter:]


def mix_back(mixer, grads):
    half_width = mixer.shape[0]
    rows = grads[0].shape[0] * 4
    return pl.pallas_call(
        mix_back_kernel,
        out_shape=(shape((half_width // 2, rows), BF),) * 2,
        in_specs=[VMEM] * 5,
        out_specs=(VMEM,) * 2,
        compiler_params=params(16),
        cost_estimate=FREE,
        name="mix_back",
    )(mixer, *grads)


def mix_grad_kernel(info, context, grad0, grad1, grad2, grad3, own, send):
    rows = grad0.shape[0]
    half_width = own.shape[1]
    for out, half in ((own, info[1]), (send, 1 - info[1])):
        at = pl.multiple_of(half * half_width, half_width)
        total = None
        for p, grad in enumerate((grad0, grad1, grad2, grad3)):
            part = dot(
                context[:, p * rows : (p + 1) * rows], grad[:, pl.ds(at, half_width)], 1, 0
            )
            total = part if total is None else total + part
        out[...] = total.astype(BF)


def mix_grad(info, context, grads):
    half_width = context.shape[0]
    return pl.pallas_call(
        mix_grad_kernel,
        out_shape=(shape((half_width, half_width), BF),) * 2,
        in_specs=[SMEM] + [VMEM] * 5,
        out_specs=(VMEM,) * 2,
        compiler_params=params(16),
        cost_estimate=FREE,
        name="mix_grad",
    )(info, context, *grads)


def mix_place_kernel(blocks, info, own, recv, out, scratch):
    half_width = own.shape[1]
    quarter = half_width // 2
    x, c, shard = info[0], info[1], info[2]
    for ref, dc in ((own, 0), (recv, 1)):
        for dx in range(2):
            at = pl.multiple_of((c ^ dc) * half_width + (x ^ dx) * quarter, quarter)
            scratch[pl.ds(at, quarter), :] = ref[dx * quarter : (dx + 1) * quarter, :].astype(F32)
    block = out.shape[1]
    for b in range(blocks):
        out[order_of(range(blocks), shard, b)] = scratch[b * block : (b + 1) * block, :].astype(BF)


def mix_place(info, own, recv, blocks):
    half_width = own.shape[1]
    return pl.pallas_call(
        partial(mix_place_kernel, blocks),
        out_shape=shape((blocks, 2 * half_width // blocks, half_width), BF),
        in_specs=[SMEM, VMEM, VMEM],
        out_specs=VMEM,
        scratch_shapes=[pltpu.VMEM((2 * half_width, half_width), F32)],
        compiler_params=params(8),
        cost_estimate=FREE,
        name="mix_place",
    )(info, own, recv)


def row_tiles(rows, step, body):
    lax.fori_loop(0, rows // step, lambda i, c: body(pl.ds(pl.multiple_of(i * step, step), step), c), 0)


def mean_of(value):
    return jnp.mean(value, -1, keepdims=True)


def first_norm_kernel(
    tokens, mixed, recv0, recv1, vectors, low0, low1, normed_out, inverse_out, recv, low
):
    gain, bias = vectors[0:1, :], vectors[1:2, :]
    half = recv0.shape[0]
    recv[:half, :] = recv0[...]
    recv[half:, :] = recv1[...]

    def body(at, carry):
        hidden = tokens[at, :].astype(F32) + mixed[at, :] + recv[at, :].astype(F32)
        centred = hidden - mean_of(hidden)
        inverse = lax.rsqrt(mean_of(centred * centred) + EPSILON)
        normed = centred * inverse
        normed_out[at, :] = normed
        inverse_out[at, :] = inverse
        low[at, :] = (normed * gain + bias).astype(BF)
        return carry

    row_tiles(tokens.shape[0], 128, body)
    low0[...] = low[:half, :]
    low1[...] = low[half:, :]


def first_norm(tokens, mixed, recvs, vectors):
    rows, width = tokens.shape
    return pl.pallas_call(
        first_norm_kernel,
        grid=(1,),
        out_shape=(shape((rows // 2, width), BF),) * 2
        + (shape((rows, width), F32), shape((rows, 1), F32)),
        in_specs=[pl.BlockSpec((rows, width), lambda i: (0, 0))] * 2
        + [pl.BlockSpec((rows // 2, width), lambda i: (0, 0))] * 2
        + [pl.BlockSpec(vectors.shape, lambda i: (0, 0))],
        scratch_shapes=[pltpu.VMEM((rows, width), BF)] * 2,
        out_specs=(pl.BlockSpec((rows // 2, width), lambda i: (0, 0)),) * 2
        + (
            pl.BlockSpec((rows, width), lambda i: (0, 0)),
            pl.BlockSpec((rows, 1), lambda i: (0, 0)),
        ),
        compiler_params=params(24),
        cost_estimate=FREE,
        name="first_norm",
    )(tokens, mixed, *recvs, vectors)


def second_norm_kernel(normed_one, mlp, recv, vectors, grad, result, grad_two, grad_low, sums):
    gain_one, bias_one = vectors[0:1, :], vectors[1:2, :]
    gain, bias = vectors[2:3, :], vectors[3:4, :]
    sums[...] = jnp.zeros_like(sums)

    def body(at, carry):
        hidden = normed_one[at, :] * gain_one + bias_one + mlp[at, :] + recv[at, :].astype(F32)
        centred = hidden - mean_of(hidden)
        inverse = lax.rsqrt(mean_of(centred * centred) + EPSILON)
        normed = centred * inverse
        result[at, :] = (normed * gain + bias).astype(BF)
        grad_y = grad[at, :].astype(F32)
        grad_n = grad_y * gain
        value = inverse * (grad_n - mean_of(grad_n) - normed * mean_of(grad_n * normed))
        grad_two[at, :] = value
        grad_low[at, :] = value.astype(BF)
        sums[2:3, :] += jnp.sum(grad_y * normed, 0, keepdims=True)
        sums[3:4, :] += jnp.sum(grad_y, 0, keepdims=True)
        return carry

    row_tiles(grad.shape[0], 128, body)


def second_norm(normed_one, mlp, recv, vectors, grad):
    rows, width = grad.shape
    return pl.pallas_call(
        second_norm_kernel,
        out_shape=(
            shape((rows, width), BF),
            shape((rows, width), F32),
            shape((rows, width), BF),
            shape((8, width), F32),
        ),
        in_specs=[VMEM] * 5,
        out_specs=(VMEM,) * 4,
        compiler_params=params(24),
        cost_estimate=FREE,
        name="second_norm",
    )(normed_one, mlp, recv, vectors, grad)


def first_back_kernel(
    grad_two, own, recv0, recv1, normed_one, inverse_one, vectors, late,
    grad_one, low0, low1, sums, grad_low, recv,
):
    gain = vectors[0:1, :]
    half = low0.shape[0]
    recv[:half, :] = recv0[...]
    recv[half:, :] = recv1[...]
    sums[...] = late[...]

    def body(at, carry):
        normed = normed_one[at, :]
        grad_y = grad_two[at, :] + own[at, :] + recv[at, :].astype(F32)
        grad_n = grad_y * gain
        value = inverse_one[at, :] * (grad_n - mean_of(grad_n) - normed * mean_of(grad_n * normed))
        grad_one[at, :] = value
        grad_low[at, :] = value.astype(BF)
        sums[0:1, :] += jnp.sum(grad_y * normed, 0, keepdims=True)
        sums[1:2, :] += jnp.sum(grad_y, 0, keepdims=True)
        return carry

    row_tiles(grad_two.shape[0], 128, body)
    low0[...] = grad_low[:half, :]
    low1[...] = grad_low[half:, :]


def first_back(grad_two, own, recvs, normed_one, inverse_one, vectors, late):
    rows, width = grad_two.shape
    return pl.pallas_call(
        first_back_kernel,
        out_shape=(shape((rows, width), F32),)
        + (shape((rows // 2, width), BF),) * 2
        + (shape((8, width), F32),),
        in_specs=[VMEM] * 8,
        out_specs=(VMEM,) * 4,
        scratch_shapes=[pltpu.VMEM((rows, width), BF)] * 2,
        compiler_params=params(24),
        cost_estimate=FREE,
        name="first_back",
    )(grad_two, own, *recvs, normed_one, inverse_one, vectors, late)


def after(value, *earlier):
    return lax.optimization_barrier((value,) + earlier)[0]


def shards(
    n_shard,
    tokens,
    segment_ids,
    qkv_weight,
    out_weight,
    up_weight,
    down_weight,
    first_gain,
    first_bias,
    second_gain,
    second_bias,
    out_grad,
):
    rows, width = tokens.shape
    half_width = width // 2
    quarter = width // 4
    ff_half = up_weight.shape[1] // 2
    block = qkv_weight.shape[0]
    shard = lax.axis_index("shard").astype(jnp.int32)
    seq = lax.axis_index("seq").astype(jnp.int32)
    xb, cb = seq // 2, seq % 2
    bits = [1 << b for b in range(n_shard.bit_length() - 1)]
    top = bits[-1]
    owner = (shard // top) % 2 == cb
    low_shard = shard % top
    place = jnp.stack([xb, cb, shard])

    def swap(value, mask):
        return lax.ppermute(value, "shard", [(i, i ^ mask) for i in range(n_shard)])

    def swap_core(value):
        return lax.ppermute(value, "seq", [(i, i ^ 1) for i in range(4)])

    def swap_x(value):
        return lax.ppermute(value, "seq", [(i, i ^ 2) for i in range(4)])

    def to_core(value, to_owner):
        pairs = []
        for sh in range(n_shard):
            for se in range(4):
                sends = (sh // top == se % 2) != to_owner
                pairs.append((sh * 4 + se, (sh ^ top) * 4 + se if sends else sh * 4 + (se ^ 1)))
        return lax.ppermute(value, ("shard", "seq"), pairs)

    def join(pieces):
        return jnp.concatenate(pieces) if len(pieces) > 1 else pieces[0]

    class Gather:
        def __init__(self, own_block, over):
            self.pieces, self.offsets, self.over = [own_block[None]], [[0]], list(over)

        def swap(self, value, rel, bit):
            got = swap(value, bit)
            self.pieces.append(got)
            self.offsets.append([r ^ bit for r in rel])
            return got

        def steps(self, count, *gate):
            for bit in [self.over.pop(0) for _ in range(count)]:
                held, rel = join(self.pieces), [r for o in self.offsets for r in o]
                self.pieces, self.offsets = [held], [rel]
                gate = (self.swap(after(held, *gate), rel, bit),)
            return gate[0]

        def part(self, index, *gate):
            return self.swap(after(self.pieces[index], *gate), self.offsets[index], self.over[0])

    def fold(value, got):
        return (value[: value.shape[0] // 2].astype(F32) + got.astype(F32)).astype(BF)

    def upper(value):
        return value[value.shape[0] // 2 :]

    def add_x(value):
        return (value.astype(F32) + swap_x(value).astype(F32)).astype(BF)

    def pick(value, flag, axis):
        return jnp.where(
            flag == 0,
            lax.index_in_dim(value, 0, axis, False),
            lax.index_in_dim(value, 1, axis, False),
        )

    def ordered(flag, own, other, axis):
        return jnp.where(
            flag == 0, jnp.concatenate([own, other], axis), jnp.concatenate([other, own], axis)
        )

    over_x = swap_x(tokens)
    over_core = swap_core(tokens)
    toks = [tokens, over_core, over_x]
    plan, ids_row = make_plan(segment_ids, place)

    own_a, own_b = prepare(
        place, qkv_weight, out_weight, (first_gain, first_bias, second_gain, second_bias)
    )
    up_half = lax.dynamic_slice_in_dim(up_weight, cb * ff_half, ff_half, 1)
    down_rows = down_weight.shape[0] // 2
    down_half = lax.dynamic_slice_in_dim(down_weight, xb * down_rows, down_rows, 0)
    middle = len(bits) - 2
    gather_a = Gather(own_a, bits[::-1])
    gather_b = Gather(own_b, bits[::-1])
    gather_up = Gather(up_half, bits[::-1])
    a1 = gather_a.steps(1)
    b1 = gather_b.steps(1, a1)
    a2 = gather_a.steps(middle, plan)
    a3 = gather_a.steps(1)
    b2 = gather_b.steps(middle, a2, up_half, down_half)
    d1 = to_core(after(down_half, b1), False)
    toks.append(swap_core(after(over_x, b2)))
    b2 = after(b2, a3)
    gather_b.pieces[1] = b2
    b3 = gather_b.steps(1)
    part_a = assemble(gather_a.pieces, gather_a.offsets, shard)
    vectors = vectors_of(part_a)

    saved, own_ctx, sends = [], [], []

    def head(j, weight, *gate):
        ctx_own, ctx_send, ctx_full, lse = attend(
            plan, toks, weight, after(ids_row, *gate)
        )
        own_ctx.append(ctx_own)
        sends.append(ctx_send)
        saved.append((ctx_full, lse))
        return ctx_own

    gather_down = Gather(jnp.where(owner, down_half, d1), bits[-2::-1])
    d2 = gather_down.steps(middle)
    u1 = gather_up.steps(1, gather_down.pieces[0])
    ctx = head(0, part_a[:, :TRIO], b2, vectors, gather_down.pieces[0])
    b3, d2, u1 = after(b3, ctx), after(d2, ctx), after(u1, ctx)
    gather_b.pieces[1], gather_down.pieces[1], gather_up.pieces[1] = b3, d2, u1
    d3 = gather_down.steps(1)
    u2 = gather_up.steps(middle)
    part_b = assemble(gather_b.pieces, gather_b.offsets, shard)
    far_a = swap_x(after(part_a, ctx))
    far_b = swap_x(part_b[:, : 2 * TRIO])
    ctx = head(1, part_b[:, :TRIO], gather_down.pieces[0], gather_up.pieces[0])
    d3, u2 = after(d3, ctx), after(u2, ctx)
    gather_down.pieces[1], gather_up.pieces[1] = d3, u2
    held_up = join(gather_up.pieces)
    gather_up.offsets = [[r for o in gather_up.offsets for r in o]]
    gather_up.pieces = [held_up]
    u3 = gather_up.part(0)
    held = join(gather_down.pieces)
    ctx = head(2, part_b[:, TRIO : 2 * TRIO], held_up, held)
    sends[2], held, far_a, far_b = lax.optimization_barrier((sends[2], held, far_a, far_b))
    others = [swap_x(value) for value in sends]
    rel = [2 * r for o in gather_down.offsets for r in o]
    held_far = swap_x(held)
    head_weights = [part_a[:, :TRIO], part_b[:, :TRIO], part_b[:, TRIO : 2 * TRIO]]
    far_weights = [far_a, far_b[:, :TRIO], far_b[:, TRIO:]]
    mixer = part_b[:, 2 * TRIO :].reshape(2, half_width, half_width)
    mixer = ordered(cb, pick(mixer, cb, 0), swap_core(pick(mixer, 1 - cb, 0)), 1)
    mixer = jnp.where(xb == 0, mixer, jnp.concatenate([mixer[quarter:], mixer[:quarter]]))
    context = jnp.concatenate(own_ctx + others)

    mixed = after(dot(context, mixer, 0, 0), u3)
    recv0, recv1 = [
        swap_core(mixed[at : at + rows // 2].astype(BF)) for at in (rows, rows + rows // 2)
    ]
    low0, low1, normed_one, inverse_one = first_norm(
        tokens, mixed, [recv0, recv1], vectors
    )
    widen = assemble(gather_up.pieces, gather_up.offsets, shard)
    act_low, act_t, slope, low_t = feed_up([low0, low1, swap_core(low0), swap_core(low1)], widen)
    held_far = after(held_far, act_low)
    narrow = assemble([held, held_far], [rel, [r + 1 for r in rel]], low_shard * 2 + xb)
    mlp_own, mlp_send = feed_down(act_low, narrow)
    result, grad_two, grad_mlp, late = second_norm(
        normed_one, mlp_own, swap_core(mlp_send), vectors, out_grad
    )

    grad_mlp = [grad_mlp, swap_core(grad_mlp)]
    narrow_grad = weight_grad(low_shard, act_t, grad_mlp, n_shard // 2, False)
    n1 = swap(upper(narrow_grad), bits[-2])
    first_own, send0, send1, grad_pre = feed_back(
        after(grad_mlp[0], narrow_grad), grad_mlp[1], slope, widen, narrow
    )
    widen_grad = weight_grad(shard, low_t, [grad_pre], n_shard)
    w1 = swap(upper(widen_grad), bits[0])
    recv0, recv1, _ = lax.optimization_barrier((swap_core(send0), swap_core(send1), widen_grad))
    grad_one, attn0, attn1, sums = first_back(
        grad_two, first_own, [recv0, recv1], normed_one, inverse_one, vectors, late
    )
    attn = [attn0, attn1, swap_core(attn0), swap_core(attn1)]
    g_own, g_send = mix_back(mixer, attn)
    mixer_own, mixer_send = mix_grad(place, after(context, g_send), attn)
    g_recv = swap_x(g_send)
    mixer_grad = mix_place(place, mixer_own, swap_core(mixer_send), n_shard)

    def head_back(j, before, *gate):
        at = j * HEAD_DIM
        return attend_back(
            plan, place, toks, head_weights[j], after(ids_row, *gate),
            g_own[at : at + HEAD_DIM], g_recv[at : at + HEAD_DIM], *saved[j],
            sums if j == 2 else None, before, n_shard,
        )

    keeps, sends = [None] * 3, [None] * 3
    keeps[0], sends[0], early = head_back(0, mixer_grad)
    fars = [swap_x(sends[0])]
    narrow_grad = fold(narrow_grad, after(n1, early))
    for bit in bits[-3:0:-1]:
        narrow_grad = fold(narrow_grad, swap(upper(narrow_grad), bit))
    n2 = swap(upper(narrow_grad), bits[0])
    widen_grad = fold(widen_grad, after(w1, narrow_grad))
    for bit in bits[1:-2]:
        widen_grad = fold(widen_grad, swap(upper(widen_grad), bit))
    w2 = swap(upper(widen_grad), bits[-2])
    keeps[1], sends[1], part = head_back(1, None, narrow_grad, widen_grad)
    fars.append(swap_x(sends[1]))
    narrow_grad = fold(narrow_grad, after(n2, part))[0]
    n3 = to_core(narrow_grad, True)
    widen_grad = fold(widen_grad, after(w2, narrow_grad, fars[0]))
    w3 = swap(upper(widen_grad), bits[-1])
    early = after(early, narrow_grad, widen_grad)
    e1 = swap(upper(early), bits[0])
    keeps[2], sends[2], late = head_back(2, part, narrow_grad, widen_grad)
    fars.append(swap_x(sends[2]))
    widen_grad = fold(widen_grad, after(w3, late, fars[1]))[0]
    early = fold(early, after(e1, widen_grad))
    e2 = swap(upper(early), bits[1])
    late = after(late, widen_grad, early)
    l1 = swap(upper(late), bits[0])
    w4 = swap_x(widen_grad)
    late = fold(late, after(l1, fars[2]))
    l2 = swap(upper(late), bits[1])
    fars[2] = after(fars[2], late)
    back_own, back_core = input_back(keeps + fars, head_weights + far_weights, rows)
    back_near = swap_core(back_core)
    late = fold(late, after(l2, w4, back_core))
    for bit in bits[2:-1]:
        late = fold(late, swap(upper(late), bit))
    l3 = swap(upper(late), bits[-1])
    early = fold(early, after(e2, late))
    for bit in bits[2:-1]:
        early = fold(early, swap(upper(early), bit))
    e3 = swap(upper(early), bits[-1])
    narrow_grad = (narrow_grad.astype(F32) + after(n3, early).astype(F32)).astype(BF)
    halves = narrow_grad.reshape(2, -1, width)
    narrow_half = swap_core(pick(halves, 1 - cb, 0))
    narrow_half = jnp.where(owner, pick(halves, cb, 0), narrow_half)
    n4 = swap_x(narrow_half)
    widen_grad = (widen_grad.astype(F32) + after(w4, late).astype(F32)).astype(BF)
    widen_other = swap_core(widen_grad)
    input_grad = grad_one + back_own + after(back_near, late).astype(F32)
    early = fold(early, after(e3, narrow_half))[0]
    late = fold(late, after(l3, early))[0]
    mine = jnp.concatenate([early, late], 1)
    theirs = swap_x(mine)
    narrow_half = (narrow_half.astype(F32) + after(n4, mine).astype(F32)).astype(BF)
    narrow_other = swap_core(narrow_half)
    widen_grad = ordered(cb, widen_grad, widen_other, 1)
    narrow_grad = ordered(cb, narrow_half, narrow_other, 0)
    narrow_grad, widen_grad = narrow_grad.astype(F32), widen_grad.astype(F32)
    theirs = after(theirs, narrow_grad, widen_grad, input_grad)
    mixer_grad = (mine[:, :half_width].astype(F32) + theirs[:, :half_width].astype(F32)).astype(BF)
    chip = jnp.concatenate([mixer_grad, mine[:, half_width:], theirs[:, half_width:]], 1)
    other = swap_core(chip)
    mixer_grad = ordered(cb, mixer_grad, other[:, :half_width], 1)
    qkv_grad, sums = place_qkv(place, chip, other, half_width, width)
    return (
        result,
        input_grad,
        qkv_grad,
        mixer_grad.astype(F32),
        widen_grad,
        narrow_grad,
        sums[:, 0],
        sums[:, 1],
        sums[:, 2],
        sums[:, 3],
    )


def solution(mesh):
    placed = (
        P(("shard", "seq"), None),
        P("shard", None),
        P("shard", None),
        P("shard", None),
        P("shard", None),
        P("shard", None),
        P("shard"),
        P("shard"),
        P("shard"),
        P("shard"),
        P(("shard", "seq"), None),
    )
    return jax.shard_map(
        partial(shards, mesh.shape["shard"]),
        mesh=mesh,
        in_specs=placed,
        out_specs=(
            P(("shard", "seq"), None),
            P(("shard", "seq"), None),
            P("shard", None),
            P("shard", None),
            P("shard", None),
            P("shard", None),
            P("shard"),
            P("shard"),
            P("shard"),
            P("shard"),
        ),
        check_vma=False,
    )
```

```python
from functools import partial

import jax
import jax.numpy as jnp
from jax import lax
from jax.experimental import pallas as pl
from jax.experimental.pallas import tpu as pltpu
from jax.sharding import PartitionSpec as P

HEADS = 12
HEAD_DIM = 64
TRIO = 3 * HEAD_DIM
GROUPS = 16
EPSILON = 1e-12
FAR = -(2.0**30)
SCALE = HEAD_DIM**-0.5
TILE = 256
UNROLL = 2
BF = jnp.bfloat16
F32 = jnp.float32
VMEM = pl.BlockSpec(memory_space=pltpu.VMEM)
SMEM = pl.BlockSpec(memory_space=pltpu.SMEM)
FREE = pl.CostEstimate(flops=1, bytes_accessed=1, transcendentals=0)


def dot(a, b, ca, cb):
    return lax.dot_general(a, b, (((ca,), (cb,)), ((), ())), preferred_element_type=F32)


def shape(dims, kind):
    return jax.ShapeDtypeStruct(dims, kind)


def params(mebi):
    return pltpu.CompilerParams(vmem_limit_bytes=mebi << 20)


def assemble_kernel(offsets, info, *refs):
    out, sem = refs[-2:]
    copies = []
    for ref, rel in zip(refs[:-2], offsets):
        block = ref.shape[1]
        for i, r in enumerate(rel):
            at = pl.multiple_of((info[0] ^ r) * block, block)
            copies.append(
                pltpu.make_async_copy(ref.at[i], out.at[pl.ds(at, block), :], sem.at[len(copies)])
            )
    for copy in copies:
        copy.start()
    for copy in copies:
        copy.wait()


def assemble(pieces, offsets, me):
    block, cols = pieces[0].shape[1:]
    count = sum(len(r) for r in offsets)
    if block % 16:
        value = jnp.concatenate(pieces)
        order = [r for rel in offsets for r in rel]
        place = jnp.array([order.index(r) for r in range(count)], jnp.int32)
        return value[place[me ^ jnp.arange(count)]].reshape(count * block, cols)
    return pl.pallas_call(
        partial(assemble_kernel, offsets),
        out_shape=shape((count * block, cols), BF),
        in_specs=[SMEM] + [pl.BlockSpec(memory_space=pltpu.HBM)] * len(pieces),
        out_specs=VMEM,
        scratch_shapes=[pltpu.SemaphoreType.DMA((count,))],
        compiler_params=params(12),
        cost_estimate=FREE,
        name="assemble",
    )(me[None], *[pltpu.with_memory_space_constraint(p, pltpu.HBM) for p in pieces])


def prepare_kernel(info, qkv_far, out_far, *refs):
    vectors, (part_a, part_b, qkv, out_weight, rows, scratch, sem) = refs[:4], refs[4:]
    block, width = out_weight.shape
    half, quarter = width // 2, width // 4
    copies = [
        pltpu.make_async_copy(qkv_far, qkv, sem.at[0]),
        pltpu.make_async_copy(out_far, out_weight, sem.at[1]),
    ] + [pltpu.make_async_copy(v, rows.at[i], sem.at[2 + i]) for i, v in enumerate(vectors)]
    for copy in copies:
        copy.start()
    scratch[...] = jnp.zeros_like(scratch)
    for copy in copies:
        copy.wait()
    for i in range(4):
        scratch[i : i + 1, :block] = rows[i].astype(F32)
    part_a[:, TRIO:] = scratch[...].T[:block, : 256 - TRIO].astype(BF)
    for x in range(2):
        for c in range(2):

            @pl.when(jnp.logical_and(info[0] == x, info[1] == c))
            def _():
                at = c * half + x * quarter
                trio = [qkv[:, i * width + at : i * width + at + quarter] for i in range(3)]
                for j in range(3):
                    piece = jnp.concatenate(
                        [t[:, j * HEAD_DIM : (j + 1) * HEAD_DIM] for t in trio], 1
                    )
                    if j == 0:
                        part_a[:, :TRIO] = piece
                    else:
                        part_b[:, (j - 1) * TRIO : j * TRIO] = piece
                part_b[:, 2 * TRIO :] = out_weight[:, c * half : (c + 1) * half]


def prepare(info, qkv, out_weight, vectors):
    block, width = out_weight.shape
    far = [qkv, out_weight] + [v[None] for v in vectors]
    return pl.pallas_call(
        prepare_kernel,
        out_shape=(shape((block, 256), BF), shape((block, 2 * TRIO + width // 2), BF)),
        in_specs=[SMEM] + [pl.BlockSpec(memory_space=pltpu.HBM)] * 6,
        out_specs=(VMEM, VMEM),
        scratch_shapes=[
            pltpu.VMEM(qkv.shape, BF),
            pltpu.VMEM(out_weight.shape, BF),
            pltpu.VMEM((4, 1, block), BF),
            pltpu.VMEM((128, 128), F32),
            pltpu.SemaphoreType.DMA((6,)),
        ],
        compiler_params=params(8),
        cost_estimate=FREE,
        name="prepare",
    )(info, *[pltpu.with_memory_space_constraint(v, pltpu.HBM) for v in far])


def vectors_kernel(part, out):
    out[...] = part[:, 128:].astype(F32).T[TRIO - 128 : TRIO - 120]


def vectors_of(part):
    return pl.pallas_call(
        vectors_kernel,
        out_shape=shape((8, part.shape[0]), F32),
        in_specs=[VMEM],
        out_specs=VMEM,
        compiler_params=params(8),
        cost_estimate=FREE,
        name="vectors",
    )(part)


def doc_rows(ids_ref, same, other):
    ids = ids_ref[...]
    rows = lax.broadcasted_iota(jnp.int32, (GROUPS, ids.shape[1]), 0)
    return jnp.where(rows == ids, same, other).astype(BF)


def plan_kernel(ids_s, ids_v, place, plan, row):
    total = ids_v.shape[1]
    tiles = total // TILE
    chunk = total // 4
    me = place[0] * 2 + place[1]
    entries = (plan.shape[0] - 1) // 2
    for i in range(2 * entries):
        plan[1 + i] = jnp.int32(tiles)
    first = [ids_s[0, i * TILE] for i in range(tiles)]
    last = [ids_s[0, i * TILE + TILE - 1] for i in range(tiles)]
    flip = me * (chunk // TILE)
    count = jnp.int32(0)
    for i in range(tiles):
        for j in range(tiles):
            meet = jnp.logical_and(first[i] <= last[j], first[j] <= last[i])

            @pl.when(meet)
            def _():
                plan[1 + 2 * UNROLL + count] = i ^ flip
                plan[1 + entries + 2 * UNROLL + count] = j ^ flip

            count = count + meet.astype(jnp.int32)
    plan[0] = (count + UNROLL - 1) // UNROLL
    for r in range(4):
        at = pl.multiple_of((me ^ r) * chunk, chunk)
        row[:, r * chunk : (r + 1) * chunk] = ids_v[:, pl.ds(at, chunk)]


def make_plan(ids, place):
    total = ids.shape[1]
    entries = (total // TILE) ** 2 + 4 * UNROLL
    return pl.pallas_call(
        plan_kernel,
        out_shape=(shape((1 + 2 * entries,), jnp.int32), shape((1, total), jnp.int32)),
        in_specs=[SMEM, VMEM, SMEM],
        out_specs=(SMEM, VMEM),
        compiler_params=params(8),
        cost_estimate=FREE,
        name="plan",
    )(ids, ids, place)


def tile_of(plan, entry):
    return pl.multiple_of(plan[1 + entry] * TILE, TILE)


def attend_kernel(
    plan, tok0, tok1, tok2, tok3, weight, ids_ref, ctx_own, ctx_send, ctx_full, lse,
    q_t, k_nat, v_t, s_ref, p_ref, fade, top, sums, acc,
):
    total = ids_ref.shape[1]
    half = total // 2
    entries = (plan.shape[0] - 1) // 2
    weight_t = weight[...].T
    keys = weight[:, HEAD_DIM : 2 * HEAD_DIM]
    for i, tok in enumerate((tok0, tok1, tok2, tok3)):
        rows = tok[...]
        at, end = i * rows.shape[0], (i + 1) * rows.shape[0]
        trio = dot(weight_t, rows, 1, 1).astype(BF)
        q_t[:HEAD_DIM, at:end] = trio[:HEAD_DIM] * SCALE
        v_t[:, at:end] = trio[2 * HEAD_DIM :]
        k_nat[at:end, :HEAD_DIM] = dot(rows, keys, 1, 0).astype(BF)
    q_t[HEAD_DIM : HEAD_DIM + GROUPS, :total] = doc_rows(ids_ref, 0.0, FAR)
    q_t[HEAD_DIM + GROUPS :, :total] = jnp.zeros((128 - HEAD_DIM - GROUPS, total), BF)
    docs = jnp.concatenate(
        [doc_rows(ids_ref, 1.0, 0.0), jnp.zeros((128 - HEAD_DIM - GROUPS, total), BF)], 0
    )
    k_nat[:total, HEAD_DIM:] = docs.T
    top[...] = jnp.full_like(top, -3e38)
    sums[...] = jnp.zeros_like(sums)
    acc[...] = jnp.zeros_like(acc)

    def step(j, carry):
        i = j * UNROLL
        for u in range(UNROLL):
            q, k = tile_of(plan, i + u), tile_of(plan, entries + i + u)
            acc[:, pl.ds(q, TILE)] = acc[:, pl.ds(q, TILE)] * fade[u] + dot(
                v_t[:, pl.ds(k, TILE)], p_ref[u], 1, 0
            )
        peaks = [jnp.max(s_ref[u], 0, keepdims=True) for u in range(UNROLL)]
        for u in range(UNROLL):
            q = tile_of(plan, i + UNROLL + u)
            old = top[:, pl.ds(q, TILE)]
            new = jnp.maximum(old, peaks[u])
            powers = jnp.exp(s_ref[u] - new)
            decay = jnp.exp(old - new)
            top[:, pl.ds(q, TILE)] = new
            sums[:, pl.ds(q, TILE)] = sums[:, pl.ds(q, TILE)] * decay + jnp.sum(
                powers, 0, keepdims=True
            )
            fade[u] = decay
            p_ref[u] = powers.astype(BF)
        for u in range(UNROLL):
            q = tile_of(plan, i + 2 * UNROLL + u)
            k = tile_of(plan, entries + i + 2 * UNROLL + u)
            s_ref[u] = dot(k_nat[pl.ds(k, TILE), :], q_t[:, pl.ds(q, TILE)], 1, 0)
        return carry

    lax.fori_loop(0, plan[0] + 2, step, 0)
    ctx_full[...] = acc[:, :total] / sums[:, :total]
    lse[...] = top[:, :total] + jnp.log(sums[:, :total])
    ctx_own[...] = ctx_full[:, :half].astype(BF)
    ctx_send[...] = ctx_full[:, half:].astype(BF)


def attend(plan, toks, weight, ids):
    total = ids.shape[1]
    half = total // 2
    padded = total + TILE
    return pl.pallas_call(
        attend_kernel,
        out_shape=(
            shape((HEAD_DIM, half), BF),
            shape((HEAD_DIM, half), BF),
            shape((HEAD_DIM, total), F32),
            shape((1, total), F32),
        ),
        in_specs=[SMEM] + [VMEM] * 6,
        out_specs=(VMEM,) * 4,
        scratch_shapes=[
            pltpu.VMEM((128, padded), BF),
            pltpu.VMEM((padded, 128), BF),
            pltpu.VMEM((HEAD_DIM, padded), BF),
            pltpu.VMEM((UNROLL, TILE, TILE), F32),
            pltpu.VMEM((UNROLL, TILE, TILE), BF),
            pltpu.VMEM((UNROLL, 1, TILE), F32),
            pltpu.VMEM((1, padded), F32),
            pltpu.VMEM((1, padded), F32),
            pltpu.VMEM((HEAD_DIM, padded), F32),
        ],
        compiler_params=params(20),
        cost_estimate=FREE,
        name="attend",
    )(plan, *toks, weight, ids)


def attend_back_kernel(
    order, plan, place, tok0, tok1, tok2, tok3, weight, ids_ref, g_own, g_recv, ctx_full, lse_in,
    sums, before, keep, send, grad_out,
    q_t, kvd, k_t, g_t, qg_nat, lse, row_term, s_ref, d_ref, p_ref, e_ref, acc, dq_t, w_grad, out,
):
    total = ids_ref.shape[1]
    half = total // 2
    entries = (plan.shape[0] - 1) // 2
    toks = (tok0, tok1, tok2, tok3)
    chunk = tok0.shape[0]
    weight_t = weight[:, : 2 * HEAD_DIM].T
    natural_w = weight[:, HEAD_DIM:]
    for at, grad in ((0, g_own), (half, g_recv)):
        g_t[HEAD_DIM:, at : at + half] = grad[...]
    g_t[:HEAD_DIM, :total] = jnp.zeros((HEAD_DIM, total), BF)
    for i, tok in enumerate(toks):
        at, end = i * chunk, (i + 1) * chunk
        rows = tok[...]
        pair = dot(weight_t, rows, 1, 1).astype(BF)
        q_t[:HEAD_DIM, at:end] = pair[:HEAD_DIM] * SCALE
        k_t[:, at:end] = pair[HEAD_DIM:]
        kvd[at:end, :128] = dot(rows, natural_w, 1, 0).astype(BF)
    qg_nat[:total, :] = jnp.concatenate([q_t[:HEAD_DIM, :total], g_t[HEAD_DIM:, :total]], 0).T
    q_t[HEAD_DIM:128, :total] = jnp.zeros((128 - HEAD_DIM, total), BF)
    q_t[128 : 128 + GROUPS, :total] = doc_rows(ids_ref, 0.0, FAR)
    q_t[128 + GROUPS :, :total] = jnp.zeros((128 - GROUPS, total), BF)
    kvd[:total, 128:] = jnp.concatenate(
        [doc_rows(ids_ref, 1.0, 0.0), jnp.zeros((128 - GROUPS, total), BF)], 0
    ).T
    acc[...] = jnp.zeros_like(acc)
    dq_t[...] = jnp.zeros_like(dq_t)
    lse[:, :total] = lse_in[...]
    row_term[:, :total] = jnp.sum(
        ctx_full[...] * g_t[HEAD_DIM:, :total].astype(F32), 0, keepdims=True
    )
    left = lax.broadcasted_iota(jnp.int32, (TILE, 128), 1) < HEAD_DIM

    def step(j, carry):
        i = j * UNROLL
        for u in range(UNROLL):
            q, k = tile_of(plan, i + u), tile_of(plan, entries + i + u)
            grad_scores, chance = e_ref[u], p_ref[u]
            natural = qg_nat[pl.ds(q, TILE), :]
            dq_t[:, pl.ds(q, TILE)] += dot(k_t[:, pl.ds(k, TILE)], grad_scores, 1, 0)
            acc[pl.ds(k, TILE), :] += jnp.where(
                left, dot(grad_scores, natural, 1, 0), dot(chance, natural, 1, 0)
            )
        for u in range(UNROLL):
            q = tile_of(plan, i + UNROLL + u)
            chance = jnp.exp(s_ref[u] - lse[:, pl.ds(q, TILE)])
            p_ref[u] = chance.astype(BF)
            e_ref[u] = (chance * (d_ref[u] - row_term[:, pl.ds(q, TILE)])).astype(BF)
        for u in range(UNROLL):
            q = tile_of(plan, i + 2 * UNROLL + u)
            rows = kvd[pl.ds(tile_of(plan, entries + i + 2 * UNROLL + u), TILE), :]
            s_ref[u] = dot(rows, q_t[:, pl.ds(q, TILE)], 1, 0)
            d_ref[u] = dot(rows[:, :128], g_t[:, pl.ds(q, TILE)], 1, 0)
        return carry

    lax.fori_loop(0, plan[0] + 2, step, 0)
    out[:HEAD_DIM, :] = (dq_t[:, :total] * SCALE).astype(BF)
    out[HEAD_DIM:, :] = acc[:total, :].T.astype(BF)
    keep[...] = out[:, :half]
    send[...] = out[:, half:]
    for i, tok in enumerate(toks):
        part = dot(out[:, i * chunk : (i + 1) * chunk], tok[...], 1, 0)
        w_grad[:TRIO, :] = part if i == 0 else w_grad[:TRIO, :] + part
    if sums is not None:
        w_grad[TRIO : TRIO + 8, :] = sums[...]
        w_grad[TRIO + 8 :, :] = jnp.zeros((256 - TRIO - 8, w_grad.shape[1]), F32)
    else:
        w_grad[TRIO:, :] = jnp.zeros((256 - TRIO, w_grad.shape[1]), F32)
    natural = w_grad[...].T
    block = grad_out.shape[1]
    for b in range(len(order)):
        to = order_of(order, place[2], b)
        value = natural[b * block : (b + 1) * block].astype(BF)
        if before is None:
            grad_out[to] = value
        else:
            ahead = before.shape[2]
            grad_out[to, :, :ahead] = before[to]
            grad_out[to, :, ahead:] = value


def order_of(order, me, b):
    rel = me ^ b
    bits = len(order).bit_length() - 1
    place = 0
    for i in range(bits):
        place = place | (((rel >> i) & 1) << (bits - 1 - i))
    return place


def attend_back(plan, place, toks, weight, ids, g_own, g_recv, ctx_full, lse, sums, before, n_shard):
    total = ids.shape[1]
    width = weight.shape[0]
    padded = total + TILE
    extra = [value for value in (sums, before) if value is not None]
    cols = 256 + (0 if before is None else before.shape[2])

    def kernel(*refs):
        refs = list(refs)
        if sums is None:
            refs.insert(12, None)
        if before is None:
            refs.insert(13, None)
        attend_back_kernel(range(n_shard), *refs)

    return pl.pallas_call(
        kernel,
        out_shape=(shape((TRIO, total // 2), BF),) * 2
        + (shape((n_shard, width // n_shard, cols), BF),),
        in_specs=[SMEM, SMEM] + [VMEM] * (10 + len(extra)),
        out_specs=(VMEM,) * 3,
        scratch_shapes=[
            pltpu.VMEM((256, padded), BF),
            pltpu.VMEM((padded, 256), BF),
            pltpu.VMEM((HEAD_DIM, padded), BF),
            pltpu.VMEM((128, padded), BF),
            pltpu.VMEM((padded, 128), BF),
            pltpu.VMEM((1, padded), F32),
            pltpu.VMEM((1, padded), F32),
            pltpu.VMEM((UNROLL, TILE, TILE), F32),
            pltpu.VMEM((UNROLL, TILE, TILE), F32),
            pltpu.VMEM((UNROLL, TILE, TILE), BF),
            pltpu.VMEM((UNROLL, TILE, TILE), BF),
            pltpu.VMEM((padded, 128), F32),
            pltpu.VMEM((HEAD_DIM, padded), F32),
            pltpu.VMEM((256, width), F32),
            pltpu.VMEM((TRIO, total), BF),
        ],
        compiler_params=params(24),
        cost_estimate=FREE,
        name="attend_back",
    )(plan, place, *toks, weight, ids, g_own, g_recv, ctx_full, lse, *extra)


def input_back_kernel(*refs):
    grads, weights, (own, send), (tall, wide) = refs[:6], refs[6:12], refs[12:14], refs[14:]
    rows = own.shape[0]
    step = 256
    for i, (grad, weight) in enumerate(zip(grads, weights)):
        tall[i * TRIO : (i + 1) * TRIO, :] = grad[...]
        wide[:, i * TRIO : (i + 1) * TRIO] = weight[:, :TRIO]

    def body(i, carry):
        at = pl.multiple_of(i * step, step)
        part = dot(tall[:, pl.ds(at, step)].T, wide[...], 1, 1)

        @pl.when(at < rows)
        def _():
            own[pl.ds(at, step), :] = part

        @pl.when(at >= rows)
        def _():
            send[pl.ds(pl.multiple_of(at - rows, step), step), :] = part.astype(BF)

        return carry

    lax.fori_loop(0, 2 * rows // step, body, 0)


def input_back(grads, weights, rows):
    width = weights[0].shape[0]
    return pl.pallas_call(
        input_back_kernel,
        out_shape=(shape((rows, width), F32), shape((rows, width), BF)),
        in_specs=[VMEM] * 12,
        out_specs=(VMEM,) * 2,
        scratch_shapes=[pltpu.VMEM((6 * TRIO, 2 * rows), BF), pltpu.VMEM((width, 6 * TRIO), BF)],
        compiler_params=params(24),
        cost_estimate=FREE,
        name="input_back",
    )(*grads, *weights)


def place_qkv_kernel(start, info, chip, other, out, sums_out):
    part = out.shape[1] // 3
    x, c = info[0] == 0, info[1] == 0
    values = [
        ref[:, start + dx * 768 : start + (dx + 1) * 768].astype(F32)
        for ref in (chip, other)
        for dx in range(2)
    ]
    tail = [v[:, 2 * 256 + TRIO : 2 * 256 + TRIO + 8] for v in values]
    sums_out[...] = tail[0] + tail[1] + tail[2] + tail[3]
    for sec in range(3):
        at = sec * HEAD_DIM
        near, near_x, far, far_x = [
            jnp.concatenate(
                [v[:, j * 256 + at : j * 256 + at + HEAD_DIM] for j in range(3)], 1
            )
            for v in values
        ]
        near, near_x = jnp.where(x, near, near_x), jnp.where(x, near_x, near)
        far, far_x = jnp.where(x, far, far_x), jnp.where(x, far_x, far)
        out[:, sec * part : (sec + 1) * part] = jnp.concatenate(
            [
                jnp.where(c, near, far),
                jnp.where(c, near_x, far_x),
                jnp.where(c, far, near),
                jnp.where(c, far_x, near_x),
            ],
            1,
        )


def place_qkv(info, chip, other, start, width):
    block = chip.shape[0]
    return pl.pallas_call(
        partial(place_qkv_kernel, start),
        out_shape=(shape((block, 3 * width), F32), shape((block, 8), F32)),
        in_specs=[SMEM] + [VMEM] * 2,
        out_specs=(VMEM, VMEM),
        compiler_params=params(8),
        cost_estimate=FREE,
        name="place_qkv",
    )(info, chip, other)


def gelu_both(u):
    root = 0.7978845608028654
    cube = 0.044715 * root
    square = u * u
    t = jnp.tanh(u * (root + cube * square))
    half = 0.5 * (1.0 + t)
    act = u * half
    slope = half + act * (1.0 - t) * (root + 3.0 * cube * square)
    return act, slope


def feed_up_kernel(low0, low1, low2, low3, up, act_out, act_t, slope_out, low_t, low):
    step = low0.shape[0]
    for p, piece in enumerate((low0, low1, low2, low3)):
        low[p * step : (p + 1) * step, :] = piece[...]

    def body(i, carry):
        at = pl.multiple_of(i * step, step)
        value = low[pl.ds(at, step), :]
        low_t[:, pl.ds(at, step)] = value.T
        act, slope = gelu_both(dot(value, up[...], 1, 0))
        act = act.astype(BF)
        act_out[pl.ds(at, step), :] = act
        act_t[:, pl.ds(at, step)] = act.T
        slope_out[pl.ds(at, step), :] = slope.astype(BF)
        return carry

    lax.fori_loop(0, 4, body, 0)


def feed_up(lows, up):
    rows, width = lows[0].shape
    hidden = up.shape[1]
    return pl.pallas_call(
        feed_up_kernel,
        out_shape=(
            shape((4 * rows, hidden), BF),
            shape((hidden, 4 * rows), BF),
            shape((4 * rows, hidden), BF),
            shape((width, 4 * rows), BF),
        ),
        in_specs=[VMEM] * 5,
        out_specs=(VMEM,) * 4,
        scratch_shapes=[pltpu.VMEM((4 * rows, width), BF)],
        compiler_params=params(32),
        cost_estimate=FREE,
        name="feed_up",
    )(*lows, up)


def feed_down_kernel(act, down, own, send):
    rows = own.shape[0]
    step = 256

    def body(i, carry):
        at = pl.multiple_of(i * step, step)
        part = dot(act[pl.ds(at, step), :], down[...], 1, 0)

        @pl.when(at < rows)
        def _():
            own[pl.ds(at, step), :] = part

        @pl.when(at >= rows)
        def _():
            send[pl.ds(pl.multiple_of(at - rows, step), step), :] = part.astype(BF)

        return carry

    lax.fori_loop(0, 2 * rows // step, body, 0)


def feed_down(act, down):
    rows, hidden = act.shape
    width = down.shape[1]
    return pl.pallas_call(
        feed_down_kernel,
        out_shape=(shape((rows // 2, width), F32), shape((rows // 2, width), BF)),
        in_specs=[VMEM] * 2,
        out_specs=(VMEM,) * 2,
        compiler_params=params(24),
        cost_estimate=FREE,
        name="feed_down",
    )(act, down)


def feed_back_kernel(
    grad_own, grad_other, slope, up, down, own, send0, send1, pre_out, grad, send
):
    rows = grad_own.shape[0]
    step = 256
    grad[:rows, :] = grad_own[...]
    grad[rows:, :] = grad_other[...]

    def body(i, carry):
        at = pl.multiple_of(i * step, step)
        pre = dot(grad[pl.ds(at, step), :], down[...], 1, 1)
        pre = (pre * slope[pl.ds(at, step), :].astype(F32)).astype(BF)
        pre_out[pl.ds(at, step), :] = pre
        part = dot(pre, up[...], 1, 1)

        @pl.when(at < rows)
        def _():
            own[pl.ds(at, step), :] = part

        @pl.when(at >= rows)
        def _():
            send[pl.ds(pl.multiple_of(at - rows, step), step), :] = part.astype(BF)

        return carry

    lax.fori_loop(0, 2 * rows // step, body, 0)
    send0[...] = send[: rows // 2, :]
    send1[...] = send[rows // 2 :, :]


def feed_back(grad_own, grad_other, slope, up, down):
    rows, width = grad_own.shape
    hidden = up.shape[1]
    return pl.pallas_call(
        feed_back_kernel,
        out_shape=(
            shape((rows, width), F32),
            shape((rows // 2, width), BF),
            shape((rows // 2, width), BF),
            shape((2 * rows, hidden), BF),
        ),
        in_specs=[VMEM] * 5,
        out_specs=(VMEM,) * 4,
        scratch_shapes=[pltpu.VMEM((2 * rows, width), BF), pltpu.VMEM((rows, width), BF)],
        compiler_params=params(32),
        cost_estimate=FREE,
        name="feed_back",
    )(grad_own, grad_other, slope, up, down)


def weight_grad_kernel(blocks, reverse, shard, left, right_own, right_other, out):
    rows, cols = left.shape[0], out.shape[2]
    half = left.shape[1] // 2
    step = 256
    block = out.shape[1]
    lone = right_other is None

    def body(i, carry):
        at = pl.multiple_of(i * step, step)
        if lone:
            value = dot(left[...], right_own[:, pl.ds(at, step)], 1, 0)
        else:
            value = dot(left[:, :half], right_own[:, pl.ds(at, step)], 1, 0) + dot(
                left[:, half:], right_other[:, pl.ds(at, step)], 1, 0
            )
        for b in range(blocks):
            to = order_of(range(blocks), shard[0], b) if reverse else shard[0] ^ b
            out[to, :, pl.ds(at, step)] = value[
                b * block : (b + 1) * block
            ].astype(BF)
        return carry

    lax.fori_loop(0, cols // step, body, 0)


def weight_grad(shard, left, rights, blocks, reverse=True):
    rows, cols = left.shape[0], rights[0].shape[1]

    def kernel(*refs):
        refs = list(refs)
        if len(rights) == 1:
            refs.insert(3, None)
        weight_grad_kernel(blocks, reverse, *refs)

    return pl.pallas_call(
        kernel,
        out_shape=shape((blocks, rows // blocks, cols), BF),
        in_specs=[SMEM, VMEM] + [VMEM] * len(rights),
        out_specs=VMEM,
        compiler_params=params(24),
        cost_estimate=FREE,
        name="weight_grad",
    )(shard[None], left, *rights)


def mix_back_kernel(mixer, grad0, grad1, grad2, grad3, *outs):
    rows = grad0.shape[0]
    for p, grad in enumerate((grad0, grad1, grad2, grad3)):
        value = dot(mixer[...], grad[...], 1, 1).astype(BF)
        for j, out in enumerate(outs):
            out[:, p * rows : (p + 1) * rows] = value[j * HEAD_DIM : (j + 1) * HEAD_DIM]


def mix_back(mixer, grads):
    rows = grads[0].shape[0] * 4
    return pl.pallas_call(
        mix_back_kernel,
        out_shape=(shape((HEAD_DIM, rows), BF),) * 6,
        in_specs=[VMEM] * 5,
        out_specs=(VMEM,) * 6,
        compiler_params=params(16),
        cost_estimate=FREE,
        name="mix_back",
    )(mixer, *grads)


def mix_grad_kernel(info, context, grad0, grad1, grad2, grad3, own, send):
    rows = grad0.shape[0]
    half_width = own.shape[1]
    for out, half in ((own, info[1]), (send, 1 - info[1])):
        at = pl.multiple_of(half * half_width, half_width)
        total = None
        for p, grad in enumerate((grad0, grad1, grad2, grad3)):
            part = dot(
                context[:, p * rows : (p + 1) * rows], grad[:, pl.ds(at, half_width)], 1, 0
            )
            total = part if total is None else total + part
        out[...] = total.astype(BF)


def mix_grad(info, context, grads):
    half_width = context.shape[0]
    return pl.pallas_call(
        mix_grad_kernel,
        out_shape=(shape((half_width, half_width), BF),) * 2,
        in_specs=[SMEM] + [VMEM] * 5,
        out_specs=(VMEM,) * 2,
        compiler_params=params(16),
        cost_estimate=FREE,
        name="mix_grad",
    )(info, context, *grads)


def mix_place_kernel(blocks, info, own, recv, behind, out, scratch):
    half_width = own.shape[1]
    quarter = half_width // 2
    x, c, shard = info[0], info[1], info[2]
    for ref, dc in ((own, 0), (recv, 1)):
        for dx in range(2):
            at = pl.multiple_of((c ^ dc) * half_width + (x ^ dx) * quarter, quarter)
            scratch[pl.ds(at, quarter), :] = ref[dx * quarter : (dx + 1) * quarter, :].astype(F32)
    block = out.shape[1]
    for b in range(blocks):
        to = order_of(range(blocks), shard, b)
        out[to, :, :half_width] = scratch[b * block : (b + 1) * block, :].astype(BF)
    out[:, :, half_width:] = behind[...]


def mix_place(info, own, recv, behind):
    half_width = own.shape[1]
    blocks, block, cols = behind.shape
    return pl.pallas_call(
        partial(mix_place_kernel, blocks),
        out_shape=shape((blocks, block, half_width + cols), BF),
        in_specs=[SMEM] + [VMEM] * 3,
        out_specs=VMEM,
        scratch_shapes=[pltpu.VMEM((2 * half_width, half_width), F32)],
        compiler_params=params(8),
        cost_estimate=FREE,
        name="mix_place",
    )(info, own, recv, behind)


def row_tiles(rows, step, body):
    lax.fori_loop(0, rows // step, lambda i, c: body(pl.ds(pl.multiple_of(i * step, step), step), c), 0)


def mean_of(value):
    return jnp.mean(value, -1, keepdims=True)


def first_norm_kernel(
    tokens, mixed, recv0, recv1, vectors, low0, low1, normed_out, inverse_out, recv, low
):
    gain, bias = vectors[0:1, :], vectors[1:2, :]
    half = recv0.shape[0]
    recv[:half, :] = recv0[...]
    recv[half:, :] = recv1[...]

    def body(at, carry):
        hidden = tokens[at, :].astype(F32) + mixed[at, :] + recv[at, :].astype(F32)
        centred = hidden - mean_of(hidden)
        inverse = lax.rsqrt(mean_of(centred * centred) + EPSILON)
        normed = centred * inverse
        normed_out[at, :] = normed
        inverse_out[at, :] = inverse
        low[at, :] = (normed * gain + bias).astype(BF)
        return carry

    row_tiles(tokens.shape[0], 128, body)
    low0[...] = low[:half, :]
    low1[...] = low[half:, :]


def first_norm(tokens, mixed, recvs, vectors):
    rows, width = tokens.shape
    return pl.pallas_call(
        first_norm_kernel,
        grid=(1,),
        out_shape=(shape((rows // 2, width), BF),) * 2
        + (shape((rows, width), F32), shape((rows, 1), F32)),
        in_specs=[pl.BlockSpec((rows, width), lambda i: (0, 0))] * 2
        + [pl.BlockSpec((rows // 2, width), lambda i: (0, 0))] * 2
        + [pl.BlockSpec(vectors.shape, lambda i: (0, 0))],
        scratch_shapes=[pltpu.VMEM((rows, width), BF)] * 2,
        out_specs=(pl.BlockSpec((rows // 2, width), lambda i: (0, 0)),) * 2
        + (
            pl.BlockSpec((rows, width), lambda i: (0, 0)),
            pl.BlockSpec((rows, 1), lambda i: (0, 0)),
        ),
        compiler_params=params(24),
        cost_estimate=FREE,
        name="first_norm",
    )(tokens, mixed, *recvs, vectors)


def second_norm_kernel(normed_one, mlp, recv, vectors, grad, result, grad_two, grad_low, sums):
    gain_one, bias_one = vectors[0:1, :], vectors[1:2, :]
    gain, bias = vectors[2:3, :], vectors[3:4, :]
    sums[...] = jnp.zeros_like(sums)

    def body(at, carry):
        hidden = normed_one[at, :] * gain_one + bias_one + mlp[at, :] + recv[at, :].astype(F32)
        centred = hidden - mean_of(hidden)
        inverse = lax.rsqrt(mean_of(centred * centred) + EPSILON)
        normed = centred * inverse
        result[at, :] = (normed * gain + bias).astype(BF)
        grad_y = grad[at, :].astype(F32)
        grad_n = grad_y * gain
        value = inverse * (grad_n - mean_of(grad_n) - normed * mean_of(grad_n * normed))
        grad_two[at, :] = value
        grad_low[at, :] = value.astype(BF)
        sums[2:3, :] += jnp.sum(grad_y * normed, 0, keepdims=True)
        sums[3:4, :] += jnp.sum(grad_y, 0, keepdims=True)
        return carry

    row_tiles(grad.shape[0], 128, body)


def second_norm(normed_one, mlp, recv, vectors, grad):
    rows, width = grad.shape
    return pl.pallas_call(
        second_norm_kernel,
        out_shape=(
            shape((rows, width), BF),
            shape((rows, width), F32),
            shape((rows, width), BF),
            shape((8, width), F32),
        ),
        in_specs=[VMEM] * 5,
        out_specs=(VMEM,) * 4,
        compiler_params=params(24),
        cost_estimate=FREE,
        name="second_norm",
    )(normed_one, mlp, recv, vectors, grad)


def first_back_kernel(
    grad_two, own, recv0, recv1, normed_one, inverse_one, vectors, late,
    grad_one, low0, low1, sums, grad_low, recv,
):
    gain = vectors[0:1, :]
    half = low0.shape[0]
    recv[:half, :] = recv0[...]
    recv[half:, :] = recv1[...]
    sums[...] = late[...]

    def body(at, carry):
        normed = normed_one[at, :]
        grad_y = grad_two[at, :] + own[at, :] + recv[at, :].astype(F32)
        grad_n = grad_y * gain
        value = inverse_one[at, :] * (grad_n - mean_of(grad_n) - normed * mean_of(grad_n * normed))
        grad_one[at, :] = value
        grad_low[at, :] = value.astype(BF)
        sums[0:1, :] += jnp.sum(grad_y * normed, 0, keepdims=True)
        sums[1:2, :] += jnp.sum(grad_y, 0, keepdims=True)
        return carry

    row_tiles(grad_two.shape[0], 128, body)
    low0[...] = grad_low[:half, :]
    low1[...] = grad_low[half:, :]


def first_back(grad_two, own, recvs, normed_one, inverse_one, vectors, late):
    rows, width = grad_two.shape
    return pl.pallas_call(
        first_back_kernel,
        out_shape=(shape((rows, width), F32),)
        + (shape((rows // 2, width), BF),) * 2
        + (shape((8, width), F32),),
        in_specs=[VMEM] * 8,
        out_specs=(VMEM,) * 4,
        scratch_shapes=[pltpu.VMEM((rows, width), BF)] * 2,
        compiler_params=params(24),
        cost_estimate=FREE,
        name="first_back",
    )(grad_two, own, *recvs, normed_one, inverse_one, vectors, late)


def after(value, *earlier):
    return lax.optimization_barrier((value,) + earlier)[0]


def shards(
    n_shard,
    tokens,
    segment_ids,
    qkv_weight,
    out_weight,
    up_weight,
    down_weight,
    first_gain,
    first_bias,
    second_gain,
    second_bias,
    out_grad,
):
    rows, width = tokens.shape
    half_width = width // 2
    quarter = width // 4
    ff_half = up_weight.shape[1] // 2
    block = qkv_weight.shape[0]
    shard = lax.axis_index("shard").astype(jnp.int32)
    seq = lax.axis_index("seq").astype(jnp.int32)
    xb, cb = seq // 2, seq % 2
    bits = [1 << b for b in range(n_shard.bit_length() - 1)]
    top = bits[-1]
    owner = (shard // top) % 2 == cb
    low_shard = shard % top
    place = jnp.stack([xb, cb, shard])

    def swap(value, mask):
        return lax.ppermute(value, "shard", [(i, i ^ mask) for i in range(n_shard)])

    def swap_core(value):
        return lax.ppermute(value, "seq", [(i, i ^ 1) for i in range(4)])

    def swap_x(value):
        return lax.ppermute(value, "seq", [(i, i ^ 2) for i in range(4)])

    def to_core(value, to_owner):
        pairs = []
        for sh in range(n_shard):
            for se in range(4):
                sends = (sh // top == se % 2) != to_owner
                pairs.append((sh * 4 + se, (sh ^ top) * 4 + se if sends else sh * 4 + (se ^ 1)))
        return lax.ppermute(value, ("shard", "seq"), pairs)

    def join(pieces):
        return jnp.concatenate(pieces) if len(pieces) > 1 else pieces[0]

    class Gather:
        def __init__(self, own_block, over):
            self.pieces, self.offsets, self.over = [own_block[None]], [[0]], list(over)

        def swap(self, value, rel, bit):
            got = swap(value, bit)
            self.pieces.append(got)
            self.offsets.append([r ^ bit for r in rel])
            return got

        def steps(self, count, *gate):
            for bit in [self.over.pop(0) for _ in range(count)]:
                held, rel = join(self.pieces), [r for o in self.offsets for r in o]
                self.pieces, self.offsets = [held], [rel]
                gate = (self.swap(after(held, *gate), rel, bit),)
            return gate[0]

        def part(self, index, *gate):
            return self.swap(after(self.pieces[index], *gate), self.offsets[index], self.over[0])

    def fold(value, got):
        return (value[: value.shape[0] // 2].astype(F32) + got.astype(F32)).astype(BF)

    def upper(value):
        return value[value.shape[0] // 2 :]

    def add_x(value):
        return (value.astype(F32) + swap_x(value).astype(F32)).astype(BF)

    def pick(value, flag, axis):
        return jnp.where(
            flag == 0,
            lax.index_in_dim(value, 0, axis, False),
            lax.index_in_dim(value, 1, axis, False),
        )

    def ordered(flag, own, other, axis):
        return jnp.where(
            flag == 0, jnp.concatenate([own, other], axis), jnp.concatenate([other, own], axis)
        )

    over_x = swap_x(tokens)
    over_core = swap_core(tokens)
    toks = [tokens, over_core, over_x]
    plan, ids_row = make_plan(segment_ids, place)

    own_a, own_b = prepare(
        place, qkv_weight, out_weight, (first_gain, first_bias, second_gain, second_bias)
    )
    up_half = lax.dynamic_slice_in_dim(up_weight, cb * ff_half, ff_half, 1)
    down_rows = down_weight.shape[0] // 2
    down_half = lax.dynamic_slice_in_dim(down_weight, xb * down_rows, down_rows, 0)
    middle = len(bits) - 2
    gather_a = Gather(own_a, bits[::-1])
    gather_b = Gather(own_b, bits[::-1])
    gather_up = Gather(up_half, bits[::-1])
    a1 = gather_a.steps(1)
    b1 = gather_b.steps(1, a1)
    a2 = gather_a.steps(middle, plan)
    a3 = gather_a.steps(1)
    b2 = gather_b.steps(middle, a2, up_half, down_half)
    toks.append(swap_core(after(over_x, b2)))
    d1 = to_core(after(down_half, b1), False)
    b2 = after(b2, a3, d1)
    gather_b.pieces[1] = b2
    b3 = gather_b.steps(1)
    part_a = assemble(gather_a.pieces, gather_a.offsets, shard)
    vectors = vectors_of(part_a)

    saved, own_ctx, sends = [], [], []

    def head(j, weight, *gate):
        ctx_own, ctx_send, ctx_full, lse = attend(
            plan, toks, weight, after(ids_row, *gate)
        )
        own_ctx.append(ctx_own)
        sends.append(ctx_send)
        saved.append((ctx_full, lse))
        return ctx_own

    gather_down = Gather(jnp.where(owner, down_half, d1), bits[-2::-1])
    d2 = gather_down.steps(middle)
    u1 = gather_up.steps(1, gather_down.pieces[0])
    ctx = head(0, part_a[:, :TRIO], b2, vectors, gather_down.pieces[0])
    b3, d2, u1 = after(b3, ctx), after(d2, ctx), after(u1, ctx)
    gather_b.pieces[1], gather_down.pieces[1], gather_up.pieces[1] = b3, d2, u1
    d3 = gather_down.steps(1)
    u2 = gather_up.steps(middle)
    part_b = assemble(gather_b.pieces, gather_b.offsets, shard)
    far_a = swap_x(after(part_a, ctx))
    far_b = swap_x(part_b[:, : 2 * TRIO])
    ctx = head(1, part_b[:, :TRIO], gather_down.pieces[0], gather_up.pieces[0])
    d3, u2 = after(d3, ctx), after(u2, ctx)
    gather_down.pieces[1], gather_up.pieces[1] = d3, u2
    held_up = join(gather_up.pieces)
    gather_up.offsets = [[r for o in gather_up.offsets for r in o]]
    gather_up.pieces = [held_up]
    u3 = gather_up.part(0)
    held = join(gather_down.pieces)
    ctx = head(2, part_b[:, TRIO : 2 * TRIO], held_up, held)
    sends[2], held, far_a, far_b = lax.optimization_barrier((sends[2], held, far_a, far_b))
    others = [swap_x(value) for value in sends]
    rel = [2 * r for o in gather_down.offsets for r in o]
    held_far = swap_x(held)
    head_weights = [part_a[:, :TRIO], part_b[:, :TRIO], part_b[:, TRIO : 2 * TRIO]]
    far_weights = [far_a, far_b[:, :TRIO], far_b[:, TRIO:]]
    mixer = part_b[:, 2 * TRIO :].reshape(2, half_width, half_width)
    mixer = ordered(cb, pick(mixer, cb, 0), swap_core(pick(mixer, 1 - cb, 0)), 1)
    mixer = jnp.where(xb == 0, mixer, jnp.concatenate([mixer[quarter:], mixer[:quarter]]))
    context = jnp.concatenate(own_ctx + others)

    mixed = after(dot(context, mixer, 0, 0), u3)
    recv0, recv1 = [
        swap_core(mixed[at : at + rows // 2].astype(BF)) for at in (rows, rows + rows // 2)
    ]
    low0, low1, normed_one, inverse_one = first_norm(
        tokens, mixed, [recv0, recv1], vectors
    )
    widen = assemble(gather_up.pieces, gather_up.offsets, shard)
    act_low, act_t, slope, low_t = feed_up([low0, low1, swap_core(low0), swap_core(low1)], widen)
    held_far = after(held_far, act_low)
    narrow = assemble([held, held_far], [rel, [r + 1 for r in rel]], low_shard * 2 + xb)
    mlp_own, mlp_send = feed_down(act_low, narrow)
    result, grad_two, grad_mlp, late = second_norm(
        normed_one, mlp_own, swap_core(mlp_send), vectors, out_grad
    )

    grad_mlp = [grad_mlp, swap_core(grad_mlp)]
    narrow_grad = weight_grad(low_shard, act_t, grad_mlp, n_shard // 2, False)
    n1 = swap(upper(narrow_grad), bits[-2])
    first_own, send0, send1, grad_pre = feed_back(
        after(grad_mlp[0], narrow_grad), grad_mlp[1], slope, widen, narrow
    )
    widen_grad = weight_grad(shard, low_t, [grad_pre], n_shard)
    w1 = swap(upper(widen_grad), bits[0])
    recv0, recv1, _ = lax.optimization_barrier((swap_core(send0), swap_core(send1), widen_grad))
    grad_one, attn0, attn1, sums = first_back(
        grad_two, first_own, [recv0, recv1], normed_one, inverse_one, vectors, late
    )
    attn = [attn0, attn1, swap_core(attn0), swap_core(attn1)]
    gs = mix_back(mixer, attn)
    g_recv = [swap_x(g) for g in gs[3:]]
    mixer_own, mixer_send = mix_grad(place, after(context, *gs), attn)
    mixer_recv = swap_core(mixer_send)

    def head_back(j, before, *gate):
        return attend_back(
            plan, place, toks, head_weights[j], after(ids_row, *gate),
            gs[j], g_recv[j], *saved[j],
            sums if j == 2 else None, before, n_shard,
        )

    keeps, sends = [None] * 3, [None] * 3
    keeps[0], sends[0], part = head_back(0, None, mixer_own)
    fars = [swap_x(sends[0])]
    narrow_grad = fold(narrow_grad, after(n1, part, *g_recv[1:]))
    for bit in bits[-3:0:-1]:
        narrow_grad = fold(narrow_grad, swap(upper(narrow_grad), bit))
    n2 = swap(upper(narrow_grad), bits[0])
    early = mix_place(place, mixer_own, mixer_recv, after(part, narrow_grad))
    widen_grad = fold(widen_grad, after(w1, early))
    for bit in bits[1:-2]:
        widen_grad = fold(widen_grad, swap(upper(widen_grad), bit))
    w2 = swap(upper(widen_grad), bits[-2])
    keeps[1], sends[1], part = head_back(1, None, early, widen_grad)
    fars.append(swap_x(sends[1]))
    narrow_grad = fold(narrow_grad, after(n2, part))[0]
    n3 = to_core(narrow_grad, True)
    widen_grad = fold(widen_grad, after(w2, narrow_grad, fars[0]))
    w3 = swap(upper(widen_grad), bits[-1])
    early = after(early, narrow_grad, widen_grad)
    e1 = swap(upper(early), bits[0])
    keeps[2], sends[2], late = head_back(2, part, narrow_grad, widen_grad)
    fars.append(swap_x(sends[2]))
    widen_grad = fold(widen_grad, after(w3, late, fars[1]))[0]
    early = fold(early, after(e1, widen_grad))
    e2 = swap(upper(early), bits[1])
    late = after(late, widen_grad, early)
    l1 = swap(upper(late), bits[0])
    w4 = swap_x(widen_grad)
    late = fold(late, after(l1, fars[2]))
    l2 = swap(upper(late), bits[1])
    early = fold(early, after(e2, late))
    for bit in bits[2:-1]:
        early = fold(early, swap(upper(early), bit))
    e3 = swap(upper(early), bits[-1])
    fars[2] = after(fars[2], late)
    back_own, back_core = input_back(keeps + fars, head_weights + far_weights, rows)
    back_near = swap_core(back_core)
    early = fold(early, after(e3, back_core))[0]
    late = fold(late, after(l2, w4, early))
    for bit in bits[2:-1]:
        late = fold(late, swap(upper(late), bit))
    l3 = swap(upper(late), bits[-1])
    narrow_grad = (narrow_grad.astype(F32) + after(n3, late).astype(F32)).astype(BF)
    halves = narrow_grad.reshape(2, -1, width)
    narrow_half = swap_core(pick(halves, 1 - cb, 0))
    narrow_half = jnp.where(owner, pick(halves, cb, 0), narrow_half)
    n4 = swap_x(narrow_half)
    widen_grad = (widen_grad.astype(F32) + after(w4, late).astype(F32)).astype(BF)
    widen_other = swap_core(widen_grad)
    input_grad = grad_one + back_own + after(back_near, late).astype(F32)
    late = fold(late, after(l3, narrow_half))[0]
    mine = jnp.concatenate([early, late], 1)
    theirs = swap_x(mine)
    narrow_half = (narrow_half.astype(F32) + after(n4, mine).astype(F32)).astype(BF)
    narrow_other = swap_core(narrow_half)
    widen_grad = ordered(cb, widen_grad, widen_other, 1)
    narrow_grad = ordered(cb, narrow_half, narrow_other, 0)
    narrow_grad, widen_grad = narrow_grad.astype(F32), widen_grad.astype(F32)
    theirs = after(theirs, narrow_grad, widen_grad, input_grad)
    mixer_grad = (mine[:, :half_width].astype(F32) + theirs[:, :half_width].astype(F32)).astype(BF)
    chip = jnp.concatenate([mixer_grad, mine[:, half_width:], theirs[:, half_width:]], 1)
    other = swap_core(chip)
    mixer_grad = ordered(cb, mixer_grad, other[:, :half_width], 1)
    qkv_grad, sums = place_qkv(place, chip, other, half_width, width)
    return (
        result,
        input_grad,
        qkv_grad,
        mixer_grad.astype(F32),
        widen_grad,
        narrow_grad,
        sums[:, 0],
        sums[:, 1],
        sums[:, 2],
        sums[:, 3],
    )


def solution(mesh):
    placed = (
        P(("shard", "seq"), None),
        P("shard", None),
        P("shard", None),
        P("shard", None),
        P("shard", None),
        P("shard", None),
        P("shard"),
        P("shard"),
        P("shard"),
        P("shard"),
        P(("shard", "seq"), None),
    )
    return jax.shard_map(
        partial(shards, mesh.shape["shard"]),
        mesh=mesh,
        in_specs=placed,
        out_specs=(
            P(("shard", "seq"), None),
            P(("shard", "seq"), None),
            P("shard", None),
            P("shard", None),
            P("shard", None),
            P("shard", None),
            P("shard"),
            P("shard"),
            P("shard"),
            P("shard"),
        ),
        check_vma=False,
    )
```

```python
from functools import partial

import jax
import jax.numpy as jnp
from jax import lax
from jax.experimental import pallas as pl
from jax.experimental.pallas import tpu as pltpu
from jax.sharding import PartitionSpec as P

HEADS = 12
HEAD_DIM = 64
TRIO = 3 * HEAD_DIM
GROUPS = 16
EPSILON = 1e-12
FAR = -(2.0**30)
SCALE = HEAD_DIM**-0.5
TILE = 256
UNROLL = 2
BF = jnp.bfloat16
F32 = jnp.float32
VMEM = pl.BlockSpec(memory_space=pltpu.VMEM)
SMEM = pl.BlockSpec(memory_space=pltpu.SMEM)
FREE = pl.CostEstimate(flops=1, bytes_accessed=1, transcendentals=0)


def dot(a, b, ca, cb):
    return lax.dot_general(a, b, (((ca,), (cb,)), ((), ())), preferred_element_type=F32)


def shape(dims, kind):
    return jax.ShapeDtypeStruct(dims, kind)


def params(mebi):
    return pltpu.CompilerParams(vmem_limit_bytes=mebi << 20)


def assemble_kernel(offsets, info, *refs):
    out, sem = refs[-2:]
    copies = []
    for ref, rel in zip(refs[:-2], offsets):
        block = ref.shape[1]
        for i, r in enumerate(rel):
            at = pl.multiple_of((info[0] ^ r) * block, block)
            copies.append(
                pltpu.make_async_copy(ref.at[i], out.at[pl.ds(at, block), :], sem.at[len(copies)])
            )
    for copy in copies:
        copy.start()
    for copy in copies:
        copy.wait()


def assemble(pieces, offsets, me):
    block, cols = pieces[0].shape[1:]
    count = sum(len(r) for r in offsets)
    if block % 16:
        value = jnp.concatenate(pieces)
        order = [r for rel in offsets for r in rel]
        place = jnp.array([order.index(r) for r in range(count)], jnp.int32)
        return value[place[me ^ jnp.arange(count)]].reshape(count * block, cols)
    return pl.pallas_call(
        partial(assemble_kernel, offsets),
        out_shape=shape((count * block, cols), BF),
        in_specs=[SMEM] + [pl.BlockSpec(memory_space=pltpu.HBM)] * len(pieces),
        out_specs=VMEM,
        scratch_shapes=[pltpu.SemaphoreType.DMA((count,))],
        compiler_params=params(12),
        cost_estimate=FREE,
        name="assemble",
    )(me[None], *[pltpu.with_memory_space_constraint(p, pltpu.HBM) for p in pieces])


def prepare_kernel(info, qkv_far, out_far, *refs):
    vectors, (part_a, part_b, qkv, out_weight, rows, scratch, sem) = refs[:4], refs[4:]
    block, width = out_weight.shape
    half, quarter = width // 2, width // 4
    copies = [
        pltpu.make_async_copy(qkv_far, qkv, sem.at[0]),
        pltpu.make_async_copy(out_far, out_weight, sem.at[1]),
    ] + [pltpu.make_async_copy(v, rows.at[i], sem.at[2 + i]) for i, v in enumerate(vectors)]
    for copy in copies:
        copy.start()
    scratch[...] = jnp.zeros_like(scratch)
    for copy in copies:
        copy.wait()
    for i in range(4):
        scratch[i : i + 1, :block] = rows[i].astype(F32)
    part_a[:, TRIO:] = scratch[...].T[:block, : 256 - TRIO].astype(BF)
    for x in range(2):
        for c in range(2):

            @pl.when(jnp.logical_and(info[0] == x, info[1] == c))
            def _():
                at = c * half + x * quarter
                trio = [qkv[:, i * width + at : i * width + at + quarter] for i in range(3)]
                for j in range(3):
                    piece = jnp.concatenate(
                        [t[:, j * HEAD_DIM : (j + 1) * HEAD_DIM] for t in trio], 1
                    )
                    if j == 0:
                        part_a[:, :TRIO] = piece
                    else:
                        part_b[:, (j - 1) * TRIO : j * TRIO] = piece
                part_b[:, 2 * TRIO :] = out_weight[:, c * half : (c + 1) * half]


def prepare(info, qkv, out_weight, vectors):
    block, width = out_weight.shape
    far = [qkv, out_weight] + [v[None] for v in vectors]
    return pl.pallas_call(
        prepare_kernel,
        out_shape=(shape((block, 256), BF), shape((block, 2 * TRIO + width // 2), BF)),
        in_specs=[SMEM] + [pl.BlockSpec(memory_space=pltpu.HBM)] * 6,
        out_specs=(VMEM, VMEM),
        scratch_shapes=[
            pltpu.VMEM(qkv.shape, BF),
            pltpu.VMEM(out_weight.shape, BF),
            pltpu.VMEM((4, 1, block), BF),
            pltpu.VMEM((128, 128), F32),
            pltpu.SemaphoreType.DMA((6,)),
        ],
        compiler_params=params(8),
        cost_estimate=FREE,
        name="prepare",
    )(info, *[pltpu.with_memory_space_constraint(v, pltpu.HBM) for v in far])


def vectors_kernel(part, out):
    out[...] = part[:, 128:].astype(F32).T[TRIO - 128 : TRIO - 120]


def vectors_of(part):
    return pl.pallas_call(
        vectors_kernel,
        out_shape=shape((8, part.shape[0]), F32),
        in_specs=[VMEM],
        out_specs=VMEM,
        compiler_params=params(8),
        cost_estimate=FREE,
        name="vectors",
    )(part)


def doc_rows(ids_ref, same, other):
    ids = ids_ref[...]
    rows = lax.broadcasted_iota(jnp.int32, (GROUPS, ids.shape[1]), 0)
    return jnp.where(rows == ids, same, other).astype(BF)


def plan_kernel(ids_s, ids_v, place, plan, row):
    total = ids_v.shape[1]
    tiles = total // TILE
    chunk = total // 4
    me = place[0] * 2 + place[1]
    entries = (plan.shape[0] - 1) // 2
    for i in range(2 * entries):
        plan[1 + i] = jnp.int32(tiles)
    first = [ids_s[0, i * TILE] for i in range(tiles)]
    last = [ids_s[0, i * TILE + TILE - 1] for i in range(tiles)]
    flip = me * (chunk // TILE)
    count = jnp.int32(0)
    for i in range(tiles):
        for j in range(tiles):
            meet = jnp.logical_and(first[i] <= last[j], first[j] <= last[i])

            @pl.when(meet)
            def _():
                plan[1 + 2 * UNROLL + count] = i ^ flip
                plan[1 + entries + 2 * UNROLL + count] = j ^ flip

            count = count + meet.astype(jnp.int32)
    plan[0] = (count + UNROLL - 1) // UNROLL
    for r in range(4):
        at = pl.multiple_of((me ^ r) * chunk, chunk)
        row[:, r * chunk : (r + 1) * chunk] = ids_v[:, pl.ds(at, chunk)]


def make_plan(ids, place):
    total = ids.shape[1]
    entries = (total // TILE) ** 2 + 4 * UNROLL
    return pl.pallas_call(
        plan_kernel,
        out_shape=(shape((1 + 2 * entries,), jnp.int32), shape((1, total), jnp.int32)),
        in_specs=[SMEM, VMEM, SMEM],
        out_specs=(SMEM, VMEM),
        compiler_params=params(8),
        cost_estimate=FREE,
        name="plan",
    )(ids, ids, place)


def tile_of(plan, entry):
    return pl.multiple_of(plan[1 + entry] * TILE, TILE)


def attend_kernel(
    plan, tok0, tok1, tok2, tok3, weight, ids_ref, ctx_own, ctx_send, ctx_full, lse,
    q_t, k_nat, v_t, s_ref, p_ref, fade, top, sums, acc,
):
    total = ids_ref.shape[1]
    half = total // 2
    entries = (plan.shape[0] - 1) // 2
    weight_t = weight[...].T
    keys = weight[:, HEAD_DIM : 2 * HEAD_DIM]
    for i, tok in enumerate((tok0, tok1, tok2, tok3)):
        rows = tok[...]
        at, end = i * rows.shape[0], (i + 1) * rows.shape[0]
        trio = dot(weight_t, rows, 1, 1).astype(BF)
        q_t[:HEAD_DIM, at:end] = trio[:HEAD_DIM] * SCALE
        v_t[:, at:end] = trio[2 * HEAD_DIM :]
        k_nat[at:end, :HEAD_DIM] = dot(rows, keys, 1, 0).astype(BF)
    q_t[HEAD_DIM : HEAD_DIM + GROUPS, :total] = doc_rows(ids_ref, 0.0, FAR)
    q_t[HEAD_DIM + GROUPS :, :total] = jnp.zeros((128 - HEAD_DIM - GROUPS, total), BF)
    docs = jnp.concatenate(
        [doc_rows(ids_ref, 1.0, 0.0), jnp.zeros((128 - HEAD_DIM - GROUPS, total), BF)], 0
    )
    k_nat[:total, HEAD_DIM:] = docs.T
    top[...] = jnp.full_like(top, -3e38)
    sums[...] = jnp.zeros_like(sums)
    acc[...] = jnp.zeros_like(acc)

    def step(j, carry):
        i = j * UNROLL
        for u in range(UNROLL):
            q, k = tile_of(plan, i + u), tile_of(plan, entries + i + u)
            acc[:, pl.ds(q, TILE)] = acc[:, pl.ds(q, TILE)] * fade[u] + dot(
                v_t[:, pl.ds(k, TILE)], p_ref[u], 1, 0
            )
        peaks = [jnp.max(s_ref[u], 0, keepdims=True) for u in range(UNROLL)]
        for u in range(UNROLL):
            q = tile_of(plan, i + UNROLL + u)
            old = top[:, pl.ds(q, TILE)]
            new = jnp.maximum(old, peaks[u])
            powers = jnp.exp(s_ref[u] - new)
            decay = jnp.exp(old - new)
            top[:, pl.ds(q, TILE)] = new
            sums[:, pl.ds(q, TILE)] = sums[:, pl.ds(q, TILE)] * decay + jnp.sum(
                powers, 0, keepdims=True
            )
            fade[u] = decay
            p_ref[u] = powers.astype(BF)
        for u in range(UNROLL):
            q = tile_of(plan, i + 2 * UNROLL + u)
            k = tile_of(plan, entries + i + 2 * UNROLL + u)
            s_ref[u] = dot(k_nat[pl.ds(k, TILE), :], q_t[:, pl.ds(q, TILE)], 1, 0)
        return carry

    lax.fori_loop(0, plan[0] + 2, step, 0)
    ctx_full[...] = acc[:, :total] / sums[:, :total]
    lse[...] = top[:, :total] + jnp.log(sums[:, :total])
    ctx_own[...] = ctx_full[:, :half].astype(BF)
    ctx_send[...] = ctx_full[:, half:].astype(BF)


def attend(plan, toks, weight, ids):
    total = ids.shape[1]
    half = total // 2
    padded = total + TILE
    return pl.pallas_call(
        attend_kernel,
        out_shape=(
            shape((HEAD_DIM, half), BF),
            shape((HEAD_DIM, half), BF),
            shape((HEAD_DIM, total), F32),
            shape((1, total), F32),
        ),
        in_specs=[SMEM] + [VMEM] * 6,
        out_specs=(VMEM,) * 4,
        scratch_shapes=[
            pltpu.VMEM((128, padded), BF),
            pltpu.VMEM((padded, 128), BF),
            pltpu.VMEM((HEAD_DIM, padded), BF),
            pltpu.VMEM((UNROLL, TILE, TILE), F32),
            pltpu.VMEM((UNROLL, TILE, TILE), BF),
            pltpu.VMEM((UNROLL, 1, TILE), F32),
            pltpu.VMEM((1, padded), F32),
            pltpu.VMEM((1, padded), F32),
            pltpu.VMEM((HEAD_DIM, padded), F32),
        ],
        compiler_params=params(20),
        cost_estimate=FREE,
        name="attend",
    )(plan, *toks, weight, ids)


def attend_back_kernel(
    order, plan, place, tok0, tok1, tok2, tok3, weight, ids_ref, g_own, g_recv, ctx_full, lse_in,
    sums, before, keep, send, grad_out,
    q_t, kvd, k_t, g_t, qg_nat, lse, row_term, s_ref, d_ref, p_ref, e_ref, acc, dq_t, w_grad, out,
):
    total = ids_ref.shape[1]
    half = total // 2
    entries = (plan.shape[0] - 1) // 2
    toks = (tok0, tok1, tok2, tok3)
    chunk = tok0.shape[0]
    weight_t = weight[:, : 2 * HEAD_DIM].T
    natural_w = weight[:, HEAD_DIM:]
    for at, grad in ((0, g_own), (half, g_recv)):
        g_t[HEAD_DIM:, at : at + half] = grad[...]
    g_t[:HEAD_DIM, :total] = jnp.zeros((HEAD_DIM, total), BF)
    for i, tok in enumerate(toks):
        at, end = i * chunk, (i + 1) * chunk
        rows = tok[...]
        pair = dot(weight_t, rows, 1, 1).astype(BF)
        q_t[:HEAD_DIM, at:end] = pair[:HEAD_DIM] * SCALE
        k_t[:, at:end] = pair[HEAD_DIM:]
        kvd[at:end, :128] = dot(rows, natural_w, 1, 0).astype(BF)
    qg_nat[:total, :] = jnp.concatenate([q_t[:HEAD_DIM, :total], g_t[HEAD_DIM:, :total]], 0).T
    q_t[HEAD_DIM:128, :total] = jnp.zeros((128 - HEAD_DIM, total), BF)
    q_t[128 : 128 + GROUPS, :total] = doc_rows(ids_ref, 0.0, FAR)
    q_t[128 + GROUPS :, :total] = jnp.zeros((128 - GROUPS, total), BF)
    kvd[:total, 128:] = jnp.concatenate(
        [doc_rows(ids_ref, 1.0, 0.0), jnp.zeros((128 - GROUPS, total), BF)], 0
    ).T
    acc[...] = jnp.zeros_like(acc)
    dq_t[...] = jnp.zeros_like(dq_t)
    lse[:, :total] = lse_in[...]
    row_term[:, :total] = jnp.sum(
        ctx_full[...] * g_t[HEAD_DIM:, :total].astype(F32), 0, keepdims=True
    )
    left = lax.broadcasted_iota(jnp.int32, (TILE, 128), 1) < HEAD_DIM

    def step(j, carry):
        i = j * UNROLL
        for u in range(UNROLL):
            q, k = tile_of(plan, i + u), tile_of(plan, entries + i + u)
            grad_scores, chance = e_ref[u], p_ref[u]
            natural = qg_nat[pl.ds(q, TILE), :]
            dq_t[:, pl.ds(q, TILE)] += dot(k_t[:, pl.ds(k, TILE)], grad_scores, 1, 0)
            acc[pl.ds(k, TILE), :] += jnp.where(
                left, dot(grad_scores, natural, 1, 0), dot(chance, natural, 1, 0)
            )
        for u in range(UNROLL):
            q = tile_of(plan, i + UNROLL + u)
            chance = jnp.exp(s_ref[u] - lse[:, pl.ds(q, TILE)])
            p_ref[u] = chance.astype(BF)
            e_ref[u] = (chance * (d_ref[u] - row_term[:, pl.ds(q, TILE)])).astype(BF)
        for u in range(UNROLL):
            q = tile_of(plan, i + 2 * UNROLL + u)
            rows = kvd[pl.ds(tile_of(plan, entries + i + 2 * UNROLL + u), TILE), :]
            s_ref[u] = dot(rows, q_t[:, pl.ds(q, TILE)], 1, 0)
            d_ref[u] = dot(rows[:, :128], g_t[:, pl.ds(q, TILE)], 1, 0)
        return carry

    lax.fori_loop(0, plan[0] + 2, step, 0)
    out[:HEAD_DIM, :] = (dq_t[:, :total] * SCALE).astype(BF)
    out[HEAD_DIM:, :] = acc[:total, :].T.astype(BF)
    keep[...] = out[:, :half]
    send[...] = out[:, half:]
    for i, tok in enumerate(toks):
        part = dot(out[:, i * chunk : (i + 1) * chunk], tok[...], 1, 0)
        w_grad[:TRIO, :] = part if i == 0 else w_grad[:TRIO, :] + part
    if sums is not None:
        w_grad[TRIO : TRIO + 8, :] = sums[...]
        w_grad[TRIO + 8 :, :] = jnp.zeros((256 - TRIO - 8, w_grad.shape[1]), F32)
    else:
        w_grad[TRIO:, :] = jnp.zeros((256 - TRIO, w_grad.shape[1]), F32)
    natural = w_grad[...].T
    block = grad_out.shape[1]
    for b in range(len(order)):
        to = order_of(order, place[2], b)
        value = natural[b * block : (b + 1) * block].astype(BF)
        if before is None:
            grad_out[to] = value
        else:
            ahead = before.shape[2]
            grad_out[to, :, :ahead] = before[to]
            grad_out[to, :, ahead:] = value


def order_of(order, me, b):
    rel = me ^ b
    bits = len(order).bit_length() - 1
    place = 0
    for i in range(bits):
        place = place | (((rel >> i) & 1) << (bits - 1 - i))
    return place


def attend_back(plan, place, toks, weight, ids, g_own, g_recv, ctx_full, lse, sums, before, n_shard):
    total = ids.shape[1]
    width = weight.shape[0]
    padded = total + TILE
    extra = [value for value in (sums, before) if value is not None]
    cols = 256 + (0 if before is None else before.shape[2])

    def kernel(*refs):
        refs = list(refs)
        if sums is None:
            refs.insert(12, None)
        if before is None:
            refs.insert(13, None)
        attend_back_kernel(range(n_shard), *refs)

    return pl.pallas_call(
        kernel,
        out_shape=(shape((TRIO, total // 2), BF),) * 2
        + (shape((n_shard, width // n_shard, cols), BF),),
        in_specs=[SMEM, SMEM] + [VMEM] * (10 + len(extra)),
        out_specs=(VMEM,) * 3,
        scratch_shapes=[
            pltpu.VMEM((256, padded), BF),
            pltpu.VMEM((padded, 256), BF),
            pltpu.VMEM((HEAD_DIM, padded), BF),
            pltpu.VMEM((128, padded), BF),
            pltpu.VMEM((padded, 128), BF),
            pltpu.VMEM((1, padded), F32),
            pltpu.VMEM((1, padded), F32),
            pltpu.VMEM((UNROLL, TILE, TILE), F32),
            pltpu.VMEM((UNROLL, TILE, TILE), F32),
            pltpu.VMEM((UNROLL, TILE, TILE), BF),
            pltpu.VMEM((UNROLL, TILE, TILE), BF),
            pltpu.VMEM((padded, 128), F32),
            pltpu.VMEM((HEAD_DIM, padded), F32),
            pltpu.VMEM((256, width), F32),
            pltpu.VMEM((TRIO, total), BF),
        ],
        compiler_params=params(24),
        cost_estimate=FREE,
        name="attend_back",
    )(plan, place, *toks, weight, ids, g_own, g_recv, ctx_full, lse, *extra)


def input_back_kernel(*refs):
    grads, weights, (own, send), (tall, wide) = refs[:6], refs[6:12], refs[12:14], refs[14:]
    rows = own.shape[0]
    step = 256
    for i, (grad, weight) in enumerate(zip(grads, weights)):
        tall[i * TRIO : (i + 1) * TRIO, :] = grad[...]
        wide[:, i * TRIO : (i + 1) * TRIO] = weight[:, :TRIO]

    def body(i, carry):
        at = pl.multiple_of(i * step, step)
        part = dot(tall[:, pl.ds(at, step)].T, wide[...], 1, 1)

        @pl.when(at < rows)
        def _():
            own[pl.ds(at, step), :] = part

        @pl.when(at >= rows)
        def _():
            send[pl.ds(pl.multiple_of(at - rows, step), step), :] = part.astype(BF)

        return carry

    lax.fori_loop(0, 2 * rows // step, body, 0)


def input_back(grads, weights, rows):
    width = weights[0].shape[0]
    return pl.pallas_call(
        input_back_kernel,
        out_shape=(shape((rows, width), F32), shape((rows, width), BF)),
        in_specs=[VMEM] * 12,
        out_specs=(VMEM,) * 2,
        scratch_shapes=[pltpu.VMEM((6 * TRIO, 2 * rows), BF), pltpu.VMEM((width, 6 * TRIO), BF)],
        compiler_params=params(24),
        cost_estimate=FREE,
        name="input_back",
    )(*grads, *weights)


def place_qkv_kernel(start, info, chip, other, out, mixed_out, sums_out):
    part = out.shape[1] // 3
    x, c = info[0] == 0, info[1] == 0
    near, far = chip[:, :start].astype(F32), other[:, :start].astype(F32)
    mixed_out[:, :start] = jnp.where(c, near, far)
    mixed_out[:, start:] = jnp.where(c, far, near)
    values = [
        ref[:, start + dx * 768 : start + (dx + 1) * 768].astype(F32)
        for ref in (chip, other)
        for dx in range(2)
    ]
    tail = [v[:, 2 * 256 + TRIO : 2 * 256 + TRIO + 8] for v in values]
    sums_out[...] = tail[0] + tail[1] + tail[2] + tail[3]
    for sec in range(3):
        at = sec * HEAD_DIM
        near, near_x, far, far_x = [
            jnp.concatenate(
                [v[:, j * 256 + at : j * 256 + at + HEAD_DIM] for j in range(3)], 1
            )
            for v in values
        ]
        near, near_x = jnp.where(x, near, near_x), jnp.where(x, near_x, near)
        far, far_x = jnp.where(x, far, far_x), jnp.where(x, far_x, far)
        out[:, sec * part : (sec + 1) * part] = jnp.concatenate(
            [
                jnp.where(c, near, far),
                jnp.where(c, near_x, far_x),
                jnp.where(c, far, near),
                jnp.where(c, far_x, near_x),
            ],
            1,
        )


def place_qkv(info, chip, other, start, width):
    block = chip.shape[0]
    return pl.pallas_call(
        partial(place_qkv_kernel, start),
        out_shape=(
            shape((block, 3 * width), F32), shape((block, width), F32), shape((block, 8), F32)
        ),
        in_specs=[SMEM] + [VMEM] * 2,
        out_specs=(VMEM,) * 3,
        compiler_params=params(8),
        cost_estimate=FREE,
        name="place_qkv",
    )(info, chip, other)


def gelu_both(u):
    root = 0.7978845608028654
    cube = 0.044715 * root
    square = u * u
    t = jnp.tanh(u * (root + cube * square))
    half = 0.5 * (1.0 + t)
    act = u * half
    slope = half + act * (1.0 - t) * (root + 3.0 * cube * square)
    return act, slope


def feed_up_kernel(low0, low1, low2, low3, up, act_out, act_t, slope_out, low_t, low):
    step = low0.shape[0]
    for p, piece in enumerate((low0, low1, low2, low3)):
        low[p * step : (p + 1) * step, :] = piece[...]

    def body(i, carry):
        at = pl.multiple_of(i * step, step)
        value = low[pl.ds(at, step), :]
        low_t[:, pl.ds(at, step)] = value.T
        act, slope = gelu_both(dot(value, up[...], 1, 0))
        act = act.astype(BF)
        act_out[pl.ds(at, step), :] = act
        act_t[:, pl.ds(at, step)] = act.T
        slope_out[pl.ds(at, step), :] = slope.astype(BF)
        return carry

    lax.fori_loop(0, 4, body, 0)


def feed_up(lows, up):
    rows, width = lows[0].shape
    hidden = up.shape[1]
    return pl.pallas_call(
        feed_up_kernel,
        out_shape=(
            shape((4 * rows, hidden), BF),
            shape((hidden, 4 * rows), BF),
            shape((4 * rows, hidden), BF),
            shape((width, 4 * rows), BF),
        ),
        in_specs=[VMEM] * 5,
        out_specs=(VMEM,) * 4,
        scratch_shapes=[pltpu.VMEM((4 * rows, width), BF)],
        compiler_params=params(32),
        cost_estimate=FREE,
        name="feed_up",
    )(*lows, up)


def feed_down_kernel(act, down, own, send):
    rows = own.shape[0]
    step = 256

    def body(i, carry):
        at = pl.multiple_of(i * step, step)
        part = dot(act[pl.ds(at, step), :], down[...], 1, 0)

        @pl.when(at < rows)
        def _():
            own[pl.ds(at, step), :] = part

        @pl.when(at >= rows)
        def _():
            send[pl.ds(pl.multiple_of(at - rows, step), step), :] = part.astype(BF)

        return carry

    lax.fori_loop(0, 2 * rows // step, body, 0)


def feed_down(act, down):
    rows, hidden = act.shape
    width = down.shape[1]
    return pl.pallas_call(
        feed_down_kernel,
        out_shape=(shape((rows // 2, width), F32), shape((rows // 2, width), BF)),
        in_specs=[VMEM] * 2,
        out_specs=(VMEM,) * 2,
        compiler_params=params(24),
        cost_estimate=FREE,
        name="feed_down",
    )(act, down)


def feed_back_kernel(
    grad_own, grad_other, slope, up, down, own, send0, send1, pre_out, grad, send
):
    rows = grad_own.shape[0]
    step = 256
    grad[:rows, :] = grad_own[...]
    grad[rows:, :] = grad_other[...]

    def body(i, carry):
        at = pl.multiple_of(i * step, step)
        pre = dot(grad[pl.ds(at, step), :], down[...], 1, 1)
        pre = (pre * slope[pl.ds(at, step), :].astype(F32)).astype(BF)
        pre_out[pl.ds(at, step), :] = pre
        part = dot(pre, up[...], 1, 1)

        @pl.when(at < rows)
        def _():
            own[pl.ds(at, step), :] = part

        @pl.when(at >= rows)
        def _():
            send[pl.ds(pl.multiple_of(at - rows, step), step), :] = part.astype(BF)

        return carry

    lax.fori_loop(0, 2 * rows // step, body, 0)
    send0[...] = send[: rows // 2, :]
    send1[...] = send[rows // 2 :, :]


def feed_back(grad_own, grad_other, slope, up, down):
    rows, width = grad_own.shape
    hidden = up.shape[1]
    return pl.pallas_call(
        feed_back_kernel,
        out_shape=(
            shape((rows, width), F32),
            shape((rows // 2, width), BF),
            shape((rows // 2, width), BF),
            shape((2 * rows, hidden), BF),
        ),
        in_specs=[VMEM] * 5,
        out_specs=(VMEM,) * 4,
        scratch_shapes=[pltpu.VMEM((2 * rows, width), BF), pltpu.VMEM((rows, width), BF)],
        compiler_params=params(32),
        cost_estimate=FREE,
        name="feed_back",
    )(grad_own, grad_other, slope, up, down)


def weight_grad_kernel(blocks, reverse, shard, left, right_own, right_other, out):
    rows, cols = left.shape[0], out.shape[2]
    half = left.shape[1] // 2
    step = 256
    block = out.shape[1]
    lone = right_other is None

    def body(i, carry):
        at = pl.multiple_of(i * step, step)
        if lone:
            value = dot(left[...], right_own[:, pl.ds(at, step)], 1, 0)
        else:
            value = dot(left[:, :half], right_own[:, pl.ds(at, step)], 1, 0) + dot(
                left[:, half:], right_other[:, pl.ds(at, step)], 1, 0
            )
        for b in range(blocks):
            to = order_of(range(blocks), shard[0], b) if reverse else shard[0] ^ b
            out[to, :, pl.ds(at, step)] = value[
                b * block : (b + 1) * block
            ].astype(BF)
        return carry

    lax.fori_loop(0, cols // step, body, 0)


def weight_grad(shard, left, rights, blocks, reverse=True):
    rows, cols = left.shape[0], rights[0].shape[1]

    def kernel(*refs):
        refs = list(refs)
        if len(rights) == 1:
            refs.insert(3, None)
        weight_grad_kernel(blocks, reverse, *refs)

    return pl.pallas_call(
        kernel,
        out_shape=shape((blocks, rows // blocks, cols), BF),
        in_specs=[SMEM, VMEM] + [VMEM] * len(rights),
        out_specs=VMEM,
        compiler_params=params(24),
        cost_estimate=FREE,
        name="weight_grad",
    )(shard[None], left, *rights)


def mix_back_kernel(mixer, grad0, grad1, grad2, grad3, *outs):
    rows = grad0.shape[0]
    for p, grad in enumerate((grad0, grad1, grad2, grad3)):
        value = dot(mixer[...], grad[...], 1, 1).astype(BF)
        for j, out in enumerate(outs):
            out[:, p * rows : (p + 1) * rows] = value[j * HEAD_DIM : (j + 1) * HEAD_DIM]


def mix_back(mixer, grads):
    rows = grads[0].shape[0] * 4
    return pl.pallas_call(
        mix_back_kernel,
        out_shape=(shape((HEAD_DIM, rows), BF),) * 6,
        in_specs=[VMEM] * 5,
        out_specs=(VMEM,) * 6,
        compiler_params=params(16),
        cost_estimate=FREE,
        name="mix_back",
    )(mixer, *grads)


def mix_grad_kernel(info, context, grad0, grad1, grad2, grad3, own, send):
    rows = grad0.shape[0]
    half_width = own.shape[1]
    for out, half in ((own, info[1]), (send, 1 - info[1])):
        at = pl.multiple_of(half * half_width, half_width)
        total = None
        for p, grad in enumerate((grad0, grad1, grad2, grad3)):
            part = dot(
                context[:, p * rows : (p + 1) * rows], grad[:, pl.ds(at, half_width)], 1, 0
            )
            total = part if total is None else total + part
        out[...] = total.astype(BF)


def mix_grad(info, context, grads):
    half_width = context.shape[0]
    return pl.pallas_call(
        mix_grad_kernel,
        out_shape=(shape((half_width, half_width), BF),) * 2,
        in_specs=[SMEM] + [VMEM] * 5,
        out_specs=(VMEM,) * 2,
        compiler_params=params(16),
        cost_estimate=FREE,
        name="mix_grad",
    )(info, context, *grads)


def mix_place_kernel(blocks, info, own, recv, behind, out, scratch):
    half_width = own.shape[1]
    quarter = half_width // 2
    x, c, shard = info[0], info[1], info[2]
    for ref, dc in ((own, 0), (recv, 1)):
        for dx in range(2):
            at = pl.multiple_of((c ^ dc) * half_width + (x ^ dx) * quarter, quarter)
            scratch[pl.ds(at, quarter), :] = ref[dx * quarter : (dx + 1) * quarter, :].astype(F32)
    block = out.shape[1]
    for b in range(blocks):
        to = order_of(range(blocks), shard, b)
        out[to, :, :half_width] = scratch[b * block : (b + 1) * block, :].astype(BF)
    out[:, :, half_width:] = behind[...]


def mix_place(info, own, recv, behind):
    half_width = own.shape[1]
    blocks, block, cols = behind.shape
    return pl.pallas_call(
        partial(mix_place_kernel, blocks),
        out_shape=shape((blocks, block, half_width + cols), BF),
        in_specs=[SMEM] + [VMEM] * 3,
        out_specs=VMEM,
        scratch_shapes=[pltpu.VMEM((2 * half_width, half_width), F32)],
        compiler_params=params(8),
        cost_estimate=FREE,
        name="mix_place",
    )(info, own, recv, behind)


def row_tiles(rows, step, body):
    lax.fori_loop(0, rows // step, lambda i, c: body(pl.ds(pl.multiple_of(i * step, step), step), c), 0)


def mean_of(value):
    return jnp.mean(value, -1, keepdims=True)


def first_norm_kernel(
    tokens, mixed, recv0, recv1, vectors, low0, low1, normed_out, inverse_out, recv, low
):
    gain, bias = vectors[0:1, :], vectors[1:2, :]
    half = recv0.shape[0]
    recv[:half, :] = recv0[...]
    recv[half:, :] = recv1[...]

    def body(at, carry):
        hidden = tokens[at, :].astype(F32) + mixed[at, :] + recv[at, :].astype(F32)
        centred = hidden - mean_of(hidden)
        inverse = lax.rsqrt(mean_of(centred * centred) + EPSILON)
        normed = centred * inverse
        normed_out[at, :] = normed
        inverse_out[at, :] = inverse
        low[at, :] = (normed * gain + bias).astype(BF)
        return carry

    row_tiles(tokens.shape[0], 128, body)
    low0[...] = low[:half, :]
    low1[...] = low[half:, :]


def first_norm(tokens, mixed, recvs, vectors):
    rows, width = tokens.shape
    return pl.pallas_call(
        first_norm_kernel,
        grid=(1,),
        out_shape=(shape((rows // 2, width), BF),) * 2
        + (pltpu.HBM((rows, width), F32), pltpu.HBM((rows, 1), F32)),
        in_specs=[pl.BlockSpec((rows, width), lambda i: (0, 0))] * 2
        + [pl.BlockSpec((rows // 2, width), lambda i: (0, 0))] * 2
        + [pl.BlockSpec(vectors.shape, lambda i: (0, 0))],
        scratch_shapes=[pltpu.VMEM((rows, width), BF)] * 2,
        out_specs=(pl.BlockSpec((rows // 2, width), lambda i: (0, 0)),) * 2
        + (
            pl.BlockSpec((rows, width), lambda i: (0, 0)),
            pl.BlockSpec((rows, 1), lambda i: (0, 0)),
        ),
        compiler_params=params(24),
        cost_estimate=FREE,
        name="first_norm",
    )(tokens, mixed, *recvs, vectors)


def second_norm_kernel(normed_one, mlp, recv, vectors, grad, result, grad_two, grad_low, sums):
    gain_one, bias_one = vectors[0:1, :], vectors[1:2, :]
    gain, bias = vectors[2:3, :], vectors[3:4, :]
    sums[...] = jnp.zeros_like(sums)

    def body(at, carry):
        hidden = normed_one[at, :] * gain_one + bias_one + mlp[at, :] + recv[at, :].astype(F32)
        centred = hidden - mean_of(hidden)
        inverse = lax.rsqrt(mean_of(centred * centred) + EPSILON)
        normed = centred * inverse
        result[at, :] = (normed * gain + bias).astype(BF)
        grad_y = grad[at, :].astype(F32)
        grad_n = grad_y * gain
        value = inverse * (grad_n - mean_of(grad_n) - normed * mean_of(grad_n * normed))
        grad_two[at, :] = value
        grad_low[at, :] = value.astype(BF)
        sums[2:3, :] += jnp.sum(grad_y * normed, 0, keepdims=True)
        sums[3:4, :] += jnp.sum(grad_y, 0, keepdims=True)
        return carry

    row_tiles(grad.shape[0], 128, body)


def second_norm(normed_one, mlp, recv, vectors, grad):
    rows, width = grad.shape
    return pl.pallas_call(
        second_norm_kernel,
        out_shape=(
            shape((rows, width), BF),
            shape((rows, width), F32),
            shape((rows, width), BF),
            shape((8, width), F32),
        ),
        in_specs=[VMEM] * 5,
        out_specs=(VMEM,) * 4,
        compiler_params=params(24),
        cost_estimate=FREE,
        name="second_norm",
    )(normed_one, mlp, recv, vectors, grad)


def first_back_kernel(
    grad_two, own, recv0, recv1, normed_one, inverse_one, vectors, late,
    grad_one, low0, low1, sums, grad_low, recv,
):
    gain = vectors[0:1, :]
    half = low0.shape[0]
    recv[:half, :] = recv0[...]
    recv[half:, :] = recv1[...]
    sums[...] = late[...]

    def body(at, carry):
        normed = normed_one[at, :]
        grad_y = grad_two[at, :] + own[at, :] + recv[at, :].astype(F32)
        grad_n = grad_y * gain
        value = inverse_one[at, :] * (grad_n - mean_of(grad_n) - normed * mean_of(grad_n * normed))
        grad_one[at, :] = value
        grad_low[at, :] = value.astype(BF)
        sums[0:1, :] += jnp.sum(grad_y * normed, 0, keepdims=True)
        sums[1:2, :] += jnp.sum(grad_y, 0, keepdims=True)
        return carry

    row_tiles(grad_two.shape[0], 128, body)
    low0[...] = grad_low[:half, :]
    low1[...] = grad_low[half:, :]


def first_back(grad_two, own, recvs, normed_one, inverse_one, vectors, late):
    rows, width = grad_two.shape
    return pl.pallas_call(
        first_back_kernel,
        out_shape=(shape((rows, width), F32),)
        + (shape((rows // 2, width), BF),) * 2
        + (shape((8, width), F32),),
        in_specs=[VMEM] * 8,
        out_specs=(VMEM,) * 4,
        scratch_shapes=[pltpu.VMEM((rows, width), BF)] * 2,
        compiler_params=params(24),
        cost_estimate=FREE,
        name="first_back",
    )(grad_two, own, *recvs, normed_one, inverse_one, vectors, late)


def after(value, *earlier):
    return lax.optimization_barrier((value,) + earlier)[0]


def shards(
    n_shard,
    tokens,
    segment_ids,
    qkv_weight,
    out_weight,
    up_weight,
    down_weight,
    first_gain,
    first_bias,
    second_gain,
    second_bias,
    out_grad,
):
    rows, width = tokens.shape
    half_width = width // 2
    quarter = width // 4
    ff_half = up_weight.shape[1] // 2
    block = qkv_weight.shape[0]
    shard = lax.axis_index("shard").astype(jnp.int32)
    seq = lax.axis_index("seq").astype(jnp.int32)
    xb, cb = seq // 2, seq % 2
    bits = [1 << b for b in range(n_shard.bit_length() - 1)]
    top = bits[-1]
    owner = (shard // top) % 2 == cb
    low_shard = shard % top
    place = jnp.stack([xb, cb, shard])

    def swap(value, mask):
        return lax.ppermute(value, "shard", [(i, i ^ mask) for i in range(n_shard)])

    def swap_core(value):
        return lax.ppermute(value, "seq", [(i, i ^ 1) for i in range(4)])

    def swap_x(value):
        return lax.ppermute(value, "seq", [(i, i ^ 2) for i in range(4)])

    def to_core(value, to_owner):
        pairs = []
        for sh in range(n_shard):
            for se in range(4):
                sends = (sh // top == se % 2) != to_owner
                pairs.append((sh * 4 + se, (sh ^ top) * 4 + se if sends else sh * 4 + (se ^ 1)))
        return lax.ppermute(value, ("shard", "seq"), pairs)

    def join(pieces):
        return jnp.concatenate(pieces) if len(pieces) > 1 else pieces[0]

    class Gather:
        def __init__(self, own_block, over):
            self.pieces, self.offsets, self.over = [own_block[None]], [[0]], list(over)

        def swap(self, value, rel, bit):
            got = swap(value, bit)
            self.pieces.append(got)
            self.offsets.append([r ^ bit for r in rel])
            return got

        def steps(self, count, *gate):
            for bit in [self.over.pop(0) for _ in range(count)]:
                held, rel = join(self.pieces), [r for o in self.offsets for r in o]
                self.pieces, self.offsets = [held], [rel]
                gate = (self.swap(after(held, *gate), rel, bit),)
            return gate[0]

        def part(self, index, *gate):
            return self.swap(after(self.pieces[index], *gate), self.offsets[index], self.over[0])

    def fold(value, got):
        return (value[: value.shape[0] // 2].astype(F32) + got.astype(F32)).astype(BF)

    def upper(value):
        return value[value.shape[0] // 2 :]

    def add_x(value):
        return (value.astype(F32) + swap_x(value).astype(F32)).astype(BF)

    def pick(value, flag, axis):
        return jnp.where(
            flag == 0,
            lax.index_in_dim(value, 0, axis, False),
            lax.index_in_dim(value, 1, axis, False),
        )

    def ordered(flag, own, other, axis):
        return jnp.where(
            flag == 0, jnp.concatenate([own, other], axis), jnp.concatenate([other, own], axis)
        )

    over_x = swap_x(tokens)
    over_core = swap_core(tokens)
    toks = [tokens, over_core, over_x]
    plan, ids_row = make_plan(segment_ids, place)

    own_a, own_b = prepare(
        place, qkv_weight, out_weight, (first_gain, first_bias, second_gain, second_bias)
    )
    up_half = lax.dynamic_slice_in_dim(up_weight, cb * ff_half, ff_half, 1)
    down_rows = down_weight.shape[0] // 2
    down_half = lax.dynamic_slice_in_dim(down_weight, xb * down_rows, down_rows, 0)
    middle = len(bits) - 2
    gather_a = Gather(own_a, bits[::-1])
    gather_b = Gather(own_b, bits[::-1])
    gather_up = Gather(up_half, bits[::-1])
    a1 = gather_a.steps(1)
    b1 = gather_b.steps(1, a1)
    a2 = gather_a.steps(middle, plan)
    a3 = gather_a.steps(1)
    b2 = gather_b.steps(middle, a2, up_half, down_half)
    toks.append(swap_core(after(over_x, b2)))
    d1 = to_core(after(down_half, b1), False)
    b2 = after(b2, a3, d1)
    gather_b.pieces[1] = b2
    b3 = gather_b.steps(1)
    part_a = assemble(gather_a.pieces, gather_a.offsets, shard)
    vectors = vectors_of(part_a)

    saved, own_ctx, sends = [], [], []

    def head(j, weight, *gate):
        ctx_own, ctx_send, ctx_full, lse = attend(
            plan, toks, weight, after(ids_row, *gate)
        )
        own_ctx.append(ctx_own)
        sends.append(ctx_send)
        saved.append((ctx_full, lse))
        return ctx_own

    gather_down = Gather(jnp.where(owner, down_half, d1), bits[-2::-1])
    d2 = gather_down.steps(middle)
    u1 = gather_up.steps(1, gather_down.pieces[0])
    ctx = head(0, part_a[:, :TRIO], b2, vectors, gather_down.pieces[0])
    b3, d2, u1 = after(b3, ctx), after(d2, ctx), after(u1, ctx)
    gather_b.pieces[1], gather_down.pieces[1], gather_up.pieces[1] = b3, d2, u1
    d3 = gather_down.steps(1)
    u2 = gather_up.steps(middle)
    part_b = assemble(gather_b.pieces, gather_b.offsets, shard)
    far_a = swap_x(after(part_a, ctx))
    far_b = swap_x(part_b[:, : 2 * TRIO])
    ctx = head(1, part_b[:, :TRIO], gather_down.pieces[0], gather_up.pieces[0])
    d3, u2 = after(d3, ctx), after(u2, ctx)
    gather_down.pieces[1], gather_up.pieces[1] = d3, u2
    held_up = join(gather_up.pieces)
    gather_up.offsets = [[r for o in gather_up.offsets for r in o]]
    gather_up.pieces = [held_up]
    u3 = gather_up.part(0)
    held = join(gather_down.pieces)
    ctx = head(2, part_b[:, TRIO : 2 * TRIO], held_up, held)
    sends[2], held, far_a, far_b = lax.optimization_barrier((sends[2], held, far_a, far_b))
    others = [swap_x(value) for value in sends]
    rel = [2 * r for o in gather_down.offsets for r in o]
    held_far = swap_x(held)
    head_weights = [part_a[:, :TRIO], part_b[:, :TRIO], part_b[:, TRIO : 2 * TRIO]]
    far_weights = [far_a, far_b[:, :TRIO], far_b[:, TRIO:]]
    mixer = part_b[:, 2 * TRIO :].reshape(2, half_width, half_width)
    mixer = ordered(cb, pick(mixer, cb, 0), swap_core(pick(mixer, 1 - cb, 0)), 1)
    mixer = jnp.where(xb == 0, mixer, jnp.concatenate([mixer[quarter:], mixer[:quarter]]))
    context = jnp.concatenate(own_ctx + others)

    mixed = after(dot(context, mixer, 0, 0), u3)
    recv0, recv1 = [
        swap_core(mixed[at : at + rows // 2].astype(BF)) for at in (rows, rows + rows // 2)
    ]
    low0, low1, normed_one, inverse_one = first_norm(
        tokens, mixed, [recv0, recv1], vectors
    )
    widen = assemble(gather_up.pieces, gather_up.offsets, shard)
    act_low, act_t, slope, low_t = feed_up([low0, low1, swap_core(low0), swap_core(low1)], widen)
    held_far = after(held_far, act_low)
    narrow = assemble([held, held_far], [rel, [r + 1 for r in rel]], low_shard * 2 + xb)
    mlp_own, mlp_send = feed_down(act_low, narrow)
    result, grad_two, grad_mlp, late = second_norm(
        normed_one, mlp_own, swap_core(mlp_send), vectors, out_grad
    )

    grad_mlp = [grad_mlp, swap_core(grad_mlp)]
    narrow_grad = weight_grad(low_shard, act_t, grad_mlp, n_shard // 2, False)
    n1 = swap(upper(narrow_grad), bits[-2])
    first_own, send0, send1, grad_pre = feed_back(
        after(grad_mlp[0], narrow_grad), grad_mlp[1], slope, widen, narrow
    )
    widen_grad = weight_grad(shard, low_t, [grad_pre], n_shard)
    w1 = swap(upper(widen_grad), bits[0])
    recv0, recv1, _ = lax.optimization_barrier((swap_core(send0), swap_core(send1), widen_grad))
    grad_one, attn0, attn1, sums = first_back(
        grad_two, first_own, [recv0, recv1], normed_one, inverse_one, vectors, late
    )
    attn = [attn0, attn1, swap_core(attn0), swap_core(attn1)]
    gs = mix_back(mixer, attn)
    g_recv = [swap_x(g) for g in gs[3:]]
    mixer_own, mixer_send = mix_grad(place, after(context, *gs), attn)
    mixer_recv = swap_core(mixer_send)

    def head_back(j, before, *gate):
        return attend_back(
            plan, place, toks, head_weights[j], after(ids_row, *gate),
            gs[j], g_recv[j], *saved[j],
            sums if j == 2 else None, before, n_shard,
        )

    keeps, sends = [None] * 3, [None] * 3
    keeps[0], sends[0], part = head_back(0, None, mixer_own)
    fars = [swap_x(sends[0])]
    narrow_grad = fold(narrow_grad, after(n1, part, *g_recv[1:]))
    for bit in bits[-3:0:-1]:
        narrow_grad = fold(narrow_grad, swap(upper(narrow_grad), bit))
    n2 = swap(upper(narrow_grad), bits[0])
    early = mix_place(place, mixer_own, mixer_recv, after(part, narrow_grad))
    widen_grad = fold(widen_grad, after(w1, early))
    for bit in bits[1:-2]:
        widen_grad = fold(widen_grad, swap(upper(widen_grad), bit))
    w2 = swap(upper(widen_grad), bits[-2])
    keeps[1], sends[1], part = head_back(1, None, early, widen_grad)
    fars.append(swap_x(sends[1]))
    narrow_grad = fold(narrow_grad, after(n2, part))[0]
    n3 = to_core(narrow_grad, True)
    widen_grad = fold(widen_grad, after(w2, narrow_grad, fars[0]))
    w3 = swap(upper(widen_grad), bits[-1])
    early = after(early, narrow_grad, widen_grad)
    e1 = swap(upper(early), bits[0])
    keeps[2], sends[2], late = head_back(2, part, narrow_grad, widen_grad)
    fars.append(swap_x(sends[2]))
    widen_grad = fold(widen_grad, after(w3, late, fars[1]))[0]
    early = fold(early, after(e1, widen_grad))
    e2 = swap(upper(early), bits[1])
    late = after(late, widen_grad, early)
    l1 = swap(upper(late), bits[0])
    w4 = swap_x(widen_grad)
    late = fold(late, after(l1, fars[2]))
    l2 = swap(upper(late), bits[1])
    early = fold(early, after(e2, late))
    for bit in bits[2:-1]:
        early = fold(early, swap(upper(early), bit))
    e3 = swap(upper(early), bits[-1])
    fars[2] = after(fars[2], late)
    back_own, back_core = input_back(keeps + fars, head_weights + far_weights, rows)
    back_near = swap_core(back_core)
    early = fold(early, after(e3, back_core))[0]
    late = fold(late, after(l2, w4, early))
    for bit in bits[2:-1]:
        late = fold(late, swap(upper(late), bit))
    l3 = swap(upper(late), bits[-1])
    narrow_grad = (narrow_grad.astype(F32) + after(n3, late).astype(F32)).astype(BF)
    halves = narrow_grad.reshape(2, -1, width)
    narrow_half = swap_core(pick(halves, 1 - cb, 0))
    narrow_half = jnp.where(owner, pick(halves, cb, 0), narrow_half)
    n4 = swap_x(narrow_half)
    widen_grad = (widen_grad.astype(F32) + after(w4, late).astype(F32)).astype(BF)
    widen_other = swap_core(widen_grad)
    input_grad = grad_one + back_own + after(back_near, late).astype(F32)
    late = fold(late, after(l3, narrow_half))[0]
    mine = jnp.concatenate([early, late], 1)
    theirs = swap_x(mine)
    narrow_half = (narrow_half.astype(F32) + after(n4, mine).astype(F32)).astype(BF)
    narrow_other = swap_core(narrow_half)
    widen_grad = ordered(cb, widen_grad, widen_other, 1)
    narrow_grad = ordered(cb, narrow_half, narrow_other, 0)
    narrow_grad, widen_grad = narrow_grad.astype(F32), widen_grad.astype(F32)
    theirs = after(theirs, narrow_grad, widen_grad, input_grad)
    mixer_grad = (mine[:, :half_width].astype(F32) + theirs[:, :half_width].astype(F32)).astype(BF)
    chip = jnp.concatenate([mixer_grad, mine[:, half_width:], theirs[:, half_width:]], 1)
    other = swap_core(chip)
    qkv_grad, mixer_grad, sums = place_qkv(place, chip, other, half_width, width)
    return (
        result,
        input_grad,
        qkv_grad,
        mixer_grad,
        widen_grad,
        narrow_grad,
        sums[:, 0],
        sums[:, 1],
        sums[:, 2],
        sums[:, 3],
    )


def solution(mesh):
    placed = (
        P(("shard", "seq"), None),
        P("shard", None),
        P("shard", None),
        P("shard", None),
        P("shard", None),
        P("shard", None),
        P("shard"),
        P("shard"),
        P("shard"),
        P("shard"),
        P(("shard", "seq"), None),
    )
    return jax.shard_map(
        partial(shards, mesh.shape["shard"]),
        mesh=mesh,
        in_specs=placed,
        out_specs=(
            P(("shard", "seq"), None),
            P(("shard", "seq"), None),
            P("shard", None),
            P("shard", None),
            P("shard", None),
            P("shard", None),
            P("shard"),
            P("shard"),
            P("shard"),
            P("shard"),
        ),
        check_vma=False,
    )
```

```python
from functools import partial

import jax
import jax.numpy as jnp
from jax import lax
from jax.experimental import pallas as pl
from jax.experimental.pallas import tpu as pltpu
from jax.sharding import PartitionSpec as P

HEADS = 12
HEAD_DIM = 64
TRIO = 3 * HEAD_DIM
GROUPS = 16
EPSILON = 1e-12
FAR = -(2.0**30)
SCALE = HEAD_DIM**-0.5
TILE = 256
UNROLL = 2
BF = jnp.bfloat16
F32 = jnp.float32
VMEM = pl.BlockSpec(memory_space=pltpu.VMEM)
SMEM = pl.BlockSpec(memory_space=pltpu.SMEM)
FREE = pl.CostEstimate(flops=1, bytes_accessed=1, transcendentals=0)


def dot(a, b, ca, cb):
    return lax.dot_general(a, b, (((ca,), (cb,)), ((), ())), preferred_element_type=F32)


def shape(dims, kind):
    return jax.ShapeDtypeStruct(dims, kind)


def params(mebi):
    return pltpu.CompilerParams(vmem_limit_bytes=mebi << 20)


def assemble_kernel(offsets, info, *refs):
    out, sem = refs[-2:]
    copies = []
    for ref, rel in zip(refs[:-2], offsets):
        block = ref.shape[1]
        for i, r in enumerate(rel):
            at = pl.multiple_of((info[0] ^ r) * block, block)
            copies.append(
                pltpu.make_async_copy(ref.at[i], out.at[pl.ds(at, block), :], sem.at[len(copies)])
            )
    for copy in copies:
        copy.start()
    for copy in copies:
        copy.wait()


def assemble(pieces, offsets, me):
    block, cols = pieces[0].shape[1:]
    count = sum(len(r) for r in offsets)
    if block % 16:
        value = jnp.concatenate(pieces)
        order = [r for rel in offsets for r in rel]
        place = jnp.array([order.index(r) for r in range(count)], jnp.int32)
        return value[place[me ^ jnp.arange(count)]].reshape(count * block, cols)
    return pl.pallas_call(
        partial(assemble_kernel, offsets),
        out_shape=shape((count * block, cols), BF),
        in_specs=[SMEM] + [pl.BlockSpec(memory_space=pltpu.HBM)] * len(pieces),
        out_specs=VMEM,
        scratch_shapes=[pltpu.SemaphoreType.DMA((count,))],
        compiler_params=params(12),
        cost_estimate=FREE,
        name="assemble",
    )(me[None], *[pltpu.with_memory_space_constraint(p, pltpu.HBM) for p in pieces])


def prepare_kernel(info, qkv_far, out_far, *refs):
    vectors, (part_a, part_b, qkv, out_weight, rows, scratch, sem) = refs[:4], refs[4:]
    block, width = out_weight.shape
    half, quarter = width // 2, width // 4
    copies = [
        pltpu.make_async_copy(qkv_far, qkv, sem.at[0]),
        pltpu.make_async_copy(out_far, out_weight, sem.at[1]),
    ] + [pltpu.make_async_copy(v, rows.at[i], sem.at[2 + i]) for i, v in enumerate(vectors)]
    for copy in copies:
        copy.start()
    scratch[...] = jnp.zeros_like(scratch)
    for copy in copies:
        copy.wait()
    for i in range(4):
        scratch[i : i + 1, :block] = rows[i].astype(F32)
    part_a[:, TRIO:] = scratch[...].T[:block, : 256 - TRIO].astype(BF)
    for x in range(2):
        for c in range(2):

            @pl.when(jnp.logical_and(info[0] == x, info[1] == c))
            def _():
                at = c * half + x * quarter
                trio = [qkv[:, i * width + at : i * width + at + quarter] for i in range(3)]
                for j in range(3):
                    piece = jnp.concatenate(
                        [t[:, j * HEAD_DIM : (j + 1) * HEAD_DIM] for t in trio], 1
                    )
                    if j == 0:
                        part_a[:, :TRIO] = piece
                    else:
                        part_b[:, (j - 1) * TRIO : j * TRIO] = piece
                part_b[:, 2 * TRIO :] = out_weight[:, c * half : (c + 1) * half]


def prepare(info, qkv, out_weight, vectors):
    block, width = out_weight.shape
    far = [qkv, out_weight] + [v[None] for v in vectors]
    return pl.pallas_call(
        prepare_kernel,
        out_shape=(shape((block, 256), BF), shape((block, 2 * TRIO + width // 2), BF)),
        in_specs=[SMEM] + [pl.BlockSpec(memory_space=pltpu.HBM)] * 6,
        out_specs=(VMEM, VMEM),
        scratch_shapes=[
            pltpu.VMEM(qkv.shape, BF),
            pltpu.VMEM(out_weight.shape, BF),
            pltpu.VMEM((4, 1, block), BF),
            pltpu.VMEM((128, 128), F32),
            pltpu.SemaphoreType.DMA((6,)),
        ],
        compiler_params=params(8),
        cost_estimate=FREE,
        name="prepare",
    )(info, *[pltpu.with_memory_space_constraint(v, pltpu.HBM) for v in far])


def vectors_kernel(part, out):
    out[...] = part[:, 128:].astype(F32).T[TRIO - 128 : TRIO - 120]


def vectors_of(part):
    return pl.pallas_call(
        vectors_kernel,
        out_shape=shape((8, part.shape[0]), F32),
        in_specs=[VMEM],
        out_specs=VMEM,
        compiler_params=params(8),
        cost_estimate=FREE,
        name="vectors",
    )(part)


def doc_rows(ids_ref, same, other):
    ids = ids_ref[...]
    rows = lax.broadcasted_iota(jnp.int32, (GROUPS, ids.shape[1]), 0)
    return jnp.where(rows == ids, same, other).astype(BF)


def plan_kernel(ids_s, ids_v, place, plan, row):
    total = ids_v.shape[1]
    tiles = total // TILE
    chunk = total // 4
    me = place[0] * 2 + place[1]
    entries = (plan.shape[0] - 1) // 2
    for i in range(2 * entries):
        plan[1 + i] = jnp.int32(tiles)
    first = [ids_s[0, i * TILE] for i in range(tiles)]
    last = [ids_s[0, i * TILE + TILE - 1] for i in range(tiles)]
    flip = me * (chunk // TILE)
    count = jnp.int32(0)
    for i in range(tiles):
        for j in range(tiles):
            meet = jnp.logical_and(first[i] <= last[j], first[j] <= last[i])

            @pl.when(meet)
            def _():
                plan[1 + 2 * UNROLL + count] = i ^ flip
                plan[1 + entries + 2 * UNROLL + count] = j ^ flip

            count = count + meet.astype(jnp.int32)
    plan[0] = (count + UNROLL - 1) // UNROLL
    for r in range(4):
        at = pl.multiple_of((me ^ r) * chunk, chunk)
        row[:, r * chunk : (r + 1) * chunk] = ids_v[:, pl.ds(at, chunk)]


def make_plan(ids, place):
    total = ids.shape[1]
    entries = (total // TILE) ** 2 + 4 * UNROLL
    return pl.pallas_call(
        plan_kernel,
        out_shape=(shape((1 + 2 * entries,), jnp.int32), shape((1, total), jnp.int32)),
        in_specs=[SMEM, VMEM, SMEM],
        out_specs=(SMEM, VMEM),
        compiler_params=params(8),
        cost_estimate=FREE,
        name="plan",
    )(ids, ids, place)


def tile_of(plan, entry):
    return pl.multiple_of(plan[1 + entry] * TILE, TILE)


def attend_kernel(
    plan, tok0, tok1, tok2, tok3, weight, ids_ref, ctx_own, ctx_send, ctx_full, lse,
    q_t, k_nat, v_t, s_ref, p_ref, fade, top, sums, acc,
):
    total = ids_ref.shape[1]
    half = total // 2
    entries = (plan.shape[0] - 1) // 2
    weight_t = weight[...].T
    keys = weight[:, HEAD_DIM : 2 * HEAD_DIM]
    for i, tok in enumerate((tok0, tok1, tok2, tok3)):
        rows = tok[...]
        at, end = i * rows.shape[0], (i + 1) * rows.shape[0]
        trio = dot(weight_t, rows, 1, 1).astype(BF)
        q_t[:HEAD_DIM, at:end] = trio[:HEAD_DIM] * SCALE
        v_t[:, at:end] = trio[2 * HEAD_DIM :]
        k_nat[at:end, :HEAD_DIM] = dot(rows, keys, 1, 0).astype(BF)
    q_t[HEAD_DIM : HEAD_DIM + GROUPS, :total] = doc_rows(ids_ref, 0.0, FAR)
    q_t[HEAD_DIM + GROUPS :, :total] = jnp.zeros((128 - HEAD_DIM - GROUPS, total), BF)
    docs = jnp.concatenate(
        [doc_rows(ids_ref, 1.0, 0.0), jnp.zeros((128 - HEAD_DIM - GROUPS, total), BF)], 0
    )
    k_nat[:total, HEAD_DIM:] = docs.T
    top[...] = jnp.full_like(top, -3e38)
    sums[...] = jnp.zeros_like(sums)
    acc[...] = jnp.zeros_like(acc)

    def step(j, carry):
        i = j * UNROLL
        for u in range(UNROLL):
            q, k = tile_of(plan, i + u), tile_of(plan, entries + i + u)
            acc[:, pl.ds(q, TILE)] = acc[:, pl.ds(q, TILE)] * fade[u] + dot(
                v_t[:, pl.ds(k, TILE)], p_ref[u], 1, 0
            )
        peaks = [jnp.max(s_ref[u], 0, keepdims=True) for u in range(UNROLL)]
        for u in range(UNROLL):
            q = tile_of(plan, i + UNROLL + u)
            old = top[:, pl.ds(q, TILE)]
            new = jnp.maximum(old, peaks[u])
            powers = jnp.exp(s_ref[u] - new)
            decay = jnp.exp(old - new)
            top[:, pl.ds(q, TILE)] = new
            sums[:, pl.ds(q, TILE)] = sums[:, pl.ds(q, TILE)] * decay + jnp.sum(
                powers, 0, keepdims=True
            )
            fade[u] = decay
            p_ref[u] = powers.astype(BF)
        for u in range(UNROLL):
            q = tile_of(plan, i + 2 * UNROLL + u)
            k = tile_of(plan, entries + i + 2 * UNROLL + u)
            s_ref[u] = dot(k_nat[pl.ds(k, TILE), :], q_t[:, pl.ds(q, TILE)], 1, 0)
        return carry

    lax.fori_loop(0, plan[0] + 2, step, 0)
    ctx_full[...] = acc[:, :total] / sums[:, :total]
    lse[...] = top[:, :total] + jnp.log(sums[:, :total])
    ctx_own[...] = ctx_full[:, :half].astype(BF)
    ctx_send[...] = ctx_full[:, half:].astype(BF)


def attend(plan, toks, weight, ids):
    total = ids.shape[1]
    half = total // 2
    padded = total + TILE
    return pl.pallas_call(
        attend_kernel,
        out_shape=(
            shape((HEAD_DIM, half), BF),
            shape((HEAD_DIM, half), BF),
            shape((HEAD_DIM, total), F32),
            shape((1, total), F32),
        ),
        in_specs=[SMEM] + [VMEM] * 6,
        out_specs=(VMEM,) * 4,
        scratch_shapes=[
            pltpu.VMEM((128, padded), BF),
            pltpu.VMEM((padded, 128), BF),
            pltpu.VMEM((HEAD_DIM, padded), BF),
            pltpu.VMEM((UNROLL, TILE, TILE), F32),
            pltpu.VMEM((UNROLL, TILE, TILE), BF),
            pltpu.VMEM((UNROLL, 1, TILE), F32),
            pltpu.VMEM((1, padded), F32),
            pltpu.VMEM((1, padded), F32),
            pltpu.VMEM((HEAD_DIM, padded), F32),
        ],
        compiler_params=params(20),
        cost_estimate=FREE,
        name="attend",
    )(plan, *toks, weight, ids)


def attend_back_kernel(
    order, plan, place, tok0, tok1, tok2, tok3, weight, ids_ref, g_own, g_recv, ctx_full, lse_in,
    sums, before, keep, send, grad_out,
    q_t, kvd, k_t, g_t, qg_nat, lse, row_term, s_ref, d_ref, p_ref, e_ref, acc, dq_t, w_grad, out,
):
    total = ids_ref.shape[1]
    half = total // 2
    entries = (plan.shape[0] - 1) // 2
    toks = (tok0, tok1, tok2, tok3)
    chunk = tok0.shape[0]
    weight_t = weight[:, : 2 * HEAD_DIM].T
    natural_w = weight[:, HEAD_DIM:]
    for at, grad in ((0, g_own), (half, g_recv)):
        g_t[HEAD_DIM:, at : at + half] = grad[...]
    g_t[:HEAD_DIM, :total] = jnp.zeros((HEAD_DIM, total), BF)
    for i, tok in enumerate(toks):
        at, end = i * chunk, (i + 1) * chunk
        rows = tok[...]
        pair = dot(weight_t, rows, 1, 1).astype(BF)
        q_t[:HEAD_DIM, at:end] = pair[:HEAD_DIM] * SCALE
        k_t[:, at:end] = pair[HEAD_DIM:]
        kvd[at:end, :128] = dot(rows, natural_w, 1, 0).astype(BF)
    qg_nat[:total, :] = jnp.concatenate([q_t[:HEAD_DIM, :total], g_t[HEAD_DIM:, :total]], 0).T
    q_t[HEAD_DIM:128, :total] = jnp.zeros((128 - HEAD_DIM, total), BF)
    q_t[128 : 128 + GROUPS, :total] = doc_rows(ids_ref, 0.0, FAR)
    q_t[128 + GROUPS :, :total] = jnp.zeros((128 - GROUPS, total), BF)
    kvd[:total, 128:] = jnp.concatenate(
        [doc_rows(ids_ref, 1.0, 0.0), jnp.zeros((128 - GROUPS, total), BF)], 0
    ).T
    acc[...] = jnp.zeros_like(acc)
    dq_t[...] = jnp.zeros_like(dq_t)
    lse[:, :total] = lse_in[...]
    row_term[:, :total] = jnp.sum(
        ctx_full[...] * g_t[HEAD_DIM:, :total].astype(F32), 0, keepdims=True
    )
    left = lax.broadcasted_iota(jnp.int32, (TILE, 128), 1) < HEAD_DIM

    def step(j, carry):
        i = j * UNROLL
        for u in range(UNROLL):
            q, k = tile_of(plan, i + u), tile_of(plan, entries + i + u)
            grad_scores, chance = e_ref[u], p_ref[u]
            natural = qg_nat[pl.ds(q, TILE), :]
            dq_t[:, pl.ds(q, TILE)] += dot(k_t[:, pl.ds(k, TILE)], grad_scores, 1, 0)
            acc[pl.ds(k, TILE), :] += jnp.where(
                left, dot(grad_scores, natural, 1, 0), dot(chance, natural, 1, 0)
            )
        for u in range(UNROLL):
            q = tile_of(plan, i + UNROLL + u)
            chance = jnp.exp(s_ref[u] - lse[:, pl.ds(q, TILE)])
            p_ref[u] = chance.astype(BF)
            e_ref[u] = (chance * (d_ref[u] - row_term[:, pl.ds(q, TILE)])).astype(BF)
        for u in range(UNROLL):
            q = tile_of(plan, i + 2 * UNROLL + u)
            rows = kvd[pl.ds(tile_of(plan, entries + i + 2 * UNROLL + u), TILE), :]
            s_ref[u] = dot(rows, q_t[:, pl.ds(q, TILE)], 1, 0)
            d_ref[u] = dot(rows[:, :128], g_t[:, pl.ds(q, TILE)], 1, 0)
        return carry

    lax.fori_loop(0, plan[0] + 2, step, 0)
    out[:HEAD_DIM, :] = (dq_t[:, :total] * SCALE).astype(BF)
    out[HEAD_DIM:, :] = acc[:total, :].T.astype(BF)
    keep[...] = out[:, :half]
    send[...] = out[:, half:]
    for i, tok in enumerate(toks):
        part = dot(out[:, i * chunk : (i + 1) * chunk], tok[...], 1, 0)
        w_grad[:TRIO, :] = part if i == 0 else w_grad[:TRIO, :] + part
    if sums is not None:
        w_grad[TRIO : TRIO + 8, :] = sums[...]
        w_grad[TRIO + 8 :, :] = jnp.zeros((256 - TRIO - 8, w_grad.shape[1]), F32)
    else:
        w_grad[TRIO:, :] = jnp.zeros((256 - TRIO, w_grad.shape[1]), F32)
    natural = w_grad[...].T
    block = grad_out.shape[1]
    for b in range(len(order)):
        to = order_of(order, place[2], b)
        value = natural[b * block : (b + 1) * block].astype(BF)
        if before is None:
            grad_out[to] = value
        else:
            ahead = before.shape[2]
            grad_out[to, :, :ahead] = before[to]
            grad_out[to, :, ahead:] = value


def order_of(order, me, b):
    rel = me ^ b
    bits = len(order).bit_length() - 1
    place = 0
    for i in range(bits):
        place = place | (((rel >> i) & 1) << (bits - 1 - i))
    return place


def attend_back(plan, place, toks, weight, ids, g_own, g_recv, ctx_full, lse, sums, before, n_shard):
    total = ids.shape[1]
    width = weight.shape[0]
    padded = total + TILE
    extra = [value for value in (sums, before) if value is not None]
    cols = 256 + (0 if before is None else before.shape[2])

    def kernel(*refs):
        refs = list(refs)
        if sums is None:
            refs.insert(12, None)
        if before is None:
            refs.insert(13, None)
        attend_back_kernel(range(n_shard), *refs)

    return pl.pallas_call(
        kernel,
        out_shape=(shape((TRIO, total // 2), BF),) * 2
        + (shape((n_shard, width // n_shard, cols), BF),),
        in_specs=[SMEM, SMEM] + [VMEM] * (10 + len(extra)),
        out_specs=(VMEM,) * 3,
        scratch_shapes=[
            pltpu.VMEM((256, padded), BF),
            pltpu.VMEM((padded, 256), BF),
            pltpu.VMEM((HEAD_DIM, padded), BF),
            pltpu.VMEM((128, padded), BF),
            pltpu.VMEM((padded, 128), BF),
            pltpu.VMEM((1, padded), F32),
            pltpu.VMEM((1, padded), F32),
            pltpu.VMEM((UNROLL, TILE, TILE), F32),
            pltpu.VMEM((UNROLL, TILE, TILE), F32),
            pltpu.VMEM((UNROLL, TILE, TILE), BF),
            pltpu.VMEM((UNROLL, TILE, TILE), BF),
            pltpu.VMEM((padded, 128), F32),
            pltpu.VMEM((HEAD_DIM, padded), F32),
            pltpu.VMEM((256, width), F32),
            pltpu.VMEM((TRIO, total), BF),
        ],
        compiler_params=params(24),
        cost_estimate=FREE,
        name="attend_back",
    )(plan, place, *toks, weight, ids, g_own, g_recv, ctx_full, lse, *extra)


def input_back_kernel(*refs):
    grads, weights, (own, send), (tall, wide) = refs[:6], refs[6:12], refs[12:14], refs[14:]
    rows = own.shape[0]
    step = 256
    for i, (grad, weight) in enumerate(zip(grads, weights)):
        tall[i * TRIO : (i + 1) * TRIO, :] = grad[...]
        wide[:, i * TRIO : (i + 1) * TRIO] = weight[:, :TRIO]

    def body(i, carry):
        at = pl.multiple_of(i * step, step)
        part = dot(tall[:, pl.ds(at, step)].T, wide[...], 1, 1)

        @pl.when(at < rows)
        def _():
            own[pl.ds(at, step), :] = part

        @pl.when(at >= rows)
        def _():
            send[pl.ds(pl.multiple_of(at - rows, step), step), :] = part.astype(BF)

        return carry

    lax.fori_loop(0, 2 * rows // step, body, 0)


def input_back(grads, weights, rows):
    width = weights[0].shape[0]
    return pl.pallas_call(
        input_back_kernel,
        out_shape=(shape((rows, width), F32), shape((rows, width), BF)),
        in_specs=[VMEM] * 12,
        out_specs=(VMEM,) * 2,
        scratch_shapes=[pltpu.VMEM((6 * TRIO, 2 * rows), BF), pltpu.VMEM((width, 6 * TRIO), BF)],
        compiler_params=params(24),
        cost_estimate=FREE,
        name="input_back",
    )(*grads, *weights)


def place_qkv_kernel(start, info, chip, other, out, mixed_out, sums_out):
    part = out.shape[1] // 3
    x, c = info[0] == 0, info[1] == 0
    near, far = chip[:, :start].astype(F32), other[:, :start].astype(F32)
    mixed_out[:, :start] = jnp.where(c, near, far)
    mixed_out[:, start:] = jnp.where(c, far, near)
    values = [
        ref[:, start + dx * 768 : start + (dx + 1) * 768].astype(F32)
        for ref in (chip, other)
        for dx in range(2)
    ]
    tail = [v[:, 2 * 256 + TRIO : 2 * 256 + TRIO + 8] for v in values]
    sums_out[...] = tail[0] + tail[1] + tail[2] + tail[3]
    for sec in range(3):
        at = sec * HEAD_DIM
        near, near_x, far, far_x = [
            jnp.concatenate(
                [v[:, j * 256 + at : j * 256 + at + HEAD_DIM] for j in range(3)], 1
            )
            for v in values
        ]
        near, near_x = jnp.where(x, near, near_x), jnp.where(x, near_x, near)
        far, far_x = jnp.where(x, far, far_x), jnp.where(x, far_x, far)
        out[:, sec * part : (sec + 1) * part] = jnp.concatenate(
            [
                jnp.where(c, near, far),
                jnp.where(c, near_x, far_x),
                jnp.where(c, far, near),
                jnp.where(c, far_x, near_x),
            ],
            1,
        )


def place_qkv(info, chip, other, start, width):
    block = chip.shape[0]
    return pl.pallas_call(
        partial(place_qkv_kernel, start),
        out_shape=(
            shape((block, 3 * width), F32), shape((block, width), F32), shape((block, 8), F32)
        ),
        in_specs=[SMEM] + [VMEM] * 2,
        out_specs=(VMEM,) * 3,
        compiler_params=params(8),
        cost_estimate=FREE,
        name="place_qkv",
    )(info, chip, other)


def gelu_both(u):
    root = 0.7978845608028654
    cube = 0.044715 * root
    square = u * u
    t = jnp.tanh(u * (root + cube * square))
    half = 0.5 * (1.0 + t)
    act = u * half
    slope = half + act * (1.0 - t) * (root + 3.0 * cube * square)
    return act, slope


def feed_up_kernel(low0, low1, low2, low3, up, act_out, act_t, slope_out, low_t, low):
    step = low0.shape[0]
    for p, piece in enumerate((low0, low1, low2, low3)):
        low[p * step : (p + 1) * step, :] = piece[...]

    def body(i, carry):
        at = pl.multiple_of(i * step, step)
        value = low[pl.ds(at, step), :]
        low_t[:, pl.ds(at, step)] = value.T
        act, slope = gelu_both(dot(value, up[...], 1, 0))
        act = act.astype(BF)
        act_out[pl.ds(at, step), :] = act
        act_t[:, pl.ds(at, step)] = act.T
        slope_out[pl.ds(at, step), :] = slope.astype(BF)
        return carry

    lax.fori_loop(0, 4, body, 0)


def feed_up(lows, up):
    rows, width = lows[0].shape
    hidden = up.shape[1]
    return pl.pallas_call(
        feed_up_kernel,
        out_shape=(
            shape((4 * rows, hidden), BF),
            shape((hidden, 4 * rows), BF),
            shape((4 * rows, hidden), BF),
            shape((width, 4 * rows), BF),
        ),
        in_specs=[VMEM] * 5,
        out_specs=(VMEM,) * 4,
        scratch_shapes=[pltpu.VMEM((4 * rows, width), BF)],
        compiler_params=params(32),
        cost_estimate=FREE,
        name="feed_up",
    )(*lows, up)


def feed_down_kernel(act, down, own, send):
    rows = own.shape[0]
    step = 256

    def body(i, carry):
        at = pl.multiple_of(i * step, step)
        part = dot(act[pl.ds(at, step), :], down[...], 1, 0)

        @pl.when(at < rows)
        def _():
            own[pl.ds(at, step), :] = part

        @pl.when(at >= rows)
        def _():
            send[pl.ds(pl.multiple_of(at - rows, step), step), :] = part.astype(BF)

        return carry

    lax.fori_loop(0, 2 * rows // step, body, 0)


def feed_down(act, down):
    rows, hidden = act.shape
    width = down.shape[1]
    return pl.pallas_call(
        feed_down_kernel,
        out_shape=(shape((rows // 2, width), F32), shape((rows // 2, width), BF)),
        in_specs=[VMEM] * 2,
        out_specs=(VMEM,) * 2,
        compiler_params=params(24),
        cost_estimate=FREE,
        name="feed_down",
    )(act, down)


def feed_back_kernel(
    grad_own, grad_other, slope, up, down, own, send0, send1, pre_out, grad, send
):
    rows = grad_own.shape[0]
    step = 256
    grad[:rows, :] = grad_own[...]
    grad[rows:, :] = grad_other[...]

    def body(i, carry):
        at = pl.multiple_of(i * step, step)
        pre = dot(grad[pl.ds(at, step), :], down[...], 1, 1)
        pre = (pre * slope[pl.ds(at, step), :].astype(F32)).astype(BF)
        pre_out[pl.ds(at, step), :] = pre
        part = dot(pre, up[...], 1, 1)

        @pl.when(at < rows)
        def _():
            own[pl.ds(at, step), :] = part

        @pl.when(at >= rows)
        def _():
            send[pl.ds(pl.multiple_of(at - rows, step), step), :] = part.astype(BF)

        return carry

    lax.fori_loop(0, 2 * rows // step, body, 0)
    send0[...] = send[: rows // 2, :]
    send1[...] = send[rows // 2 :, :]


def feed_back(grad_own, grad_other, slope, up, down):
    rows, width = grad_own.shape
    hidden = up.shape[1]
    return pl.pallas_call(
        feed_back_kernel,
        out_shape=(
            shape((rows, width), F32),
            shape((rows // 2, width), BF),
            shape((rows // 2, width), BF),
            shape((2 * rows, hidden), BF),
        ),
        in_specs=[VMEM] * 5,
        out_specs=(VMEM,) * 4,
        scratch_shapes=[pltpu.VMEM((2 * rows, width), BF), pltpu.VMEM((rows, width), BF)],
        compiler_params=params(32),
        cost_estimate=FREE,
        name="feed_back",
    )(grad_own, grad_other, slope, up, down)


def weight_grad_kernel(blocks, reverse, shard, left, right_own, right_other, out):
    rows, cols = left.shape[0], out.shape[2]
    half = left.shape[1] // 2
    step = 256
    block = out.shape[1]
    lone = right_other is None

    def body(i, carry):
        at = pl.multiple_of(i * step, step)
        if lone:
            value = dot(left[...], right_own[:, pl.ds(at, step)], 1, 0)
        else:
            value = dot(left[:, :half], right_own[:, pl.ds(at, step)], 1, 0) + dot(
                left[:, half:], right_other[:, pl.ds(at, step)], 1, 0
            )
        for b in range(blocks):
            to = order_of(range(blocks), shard[0], b) if reverse else shard[0] ^ b
            out[to, :, pl.ds(at, step)] = value[
                b * block : (b + 1) * block
            ].astype(BF)
        return carry

    lax.fori_loop(0, cols // step, body, 0)


def weight_grad(shard, left, rights, blocks, reverse=True):
    rows, cols = left.shape[0], rights[0].shape[1]

    def kernel(*refs):
        refs = list(refs)
        if len(rights) == 1:
            refs.insert(3, None)
        weight_grad_kernel(blocks, reverse, *refs)

    return pl.pallas_call(
        kernel,
        out_shape=shape((blocks, rows // blocks, cols), BF),
        in_specs=[SMEM, VMEM] + [VMEM] * len(rights),
        out_specs=VMEM,
        compiler_params=params(24),
        cost_estimate=FREE,
        name="weight_grad",
    )(shard[None], left, *rights)


def mix_back_kernel(mixer, grad0, grad1, grad2, grad3, *outs):
    rows = grad0.shape[0]
    for p, grad in enumerate((grad0, grad1, grad2, grad3)):
        value = dot(mixer[...], grad[...], 1, 1).astype(BF)
        for j, out in enumerate(outs):
            out[:, p * rows : (p + 1) * rows] = value[j * HEAD_DIM : (j + 1) * HEAD_DIM]


def mix_back(mixer, grads):
    rows = grads[0].shape[0] * 4
    return pl.pallas_call(
        mix_back_kernel,
        out_shape=(shape((HEAD_DIM, rows), BF),) * 6,
        in_specs=[VMEM] * 5,
        out_specs=(VMEM,) * 6,
        compiler_params=params(16),
        cost_estimate=FREE,
        name="mix_back",
    )(mixer, *grads)


def mix_grad_kernel(info, context, grad0, grad1, grad2, grad3, own, send):
    rows = grad0.shape[0]
    half_width = own.shape[1]
    for out, half in ((own, info[1]), (send, 1 - info[1])):
        at = pl.multiple_of(half * half_width, half_width)
        total = None
        for p, grad in enumerate((grad0, grad1, grad2, grad3)):
            part = dot(
                context[:, p * rows : (p + 1) * rows], grad[:, pl.ds(at, half_width)], 1, 0
            )
            total = part if total is None else total + part
        out[...] = total.astype(BF)


def mix_grad(info, context, grads):
    half_width = context.shape[0]
    return pl.pallas_call(
        mix_grad_kernel,
        out_shape=(shape((half_width, half_width), BF),) * 2,
        in_specs=[SMEM] + [VMEM] * 5,
        out_specs=(VMEM,) * 2,
        compiler_params=params(16),
        cost_estimate=FREE,
        name="mix_grad",
    )(info, context, *grads)


def mix_place_kernel(blocks, info, own, recv, behind, out, scratch):
    half_width = own.shape[1]
    quarter = half_width // 2
    x, c, shard = info[0], info[1], info[2]
    for ref, dc in ((own, 0), (recv, 1)):
        for dx in range(2):
            at = pl.multiple_of((c ^ dc) * half_width + (x ^ dx) * quarter, quarter)
            scratch[pl.ds(at, quarter), :] = ref[dx * quarter : (dx + 1) * quarter, :].astype(F32)
    block = out.shape[1]
    for b in range(blocks):
        to = order_of(range(blocks), shard, b)
        out[to, :, :half_width] = scratch[b * block : (b + 1) * block, :].astype(BF)
    out[:, :, half_width:] = behind[...]


def mix_place(info, own, recv, behind):
    half_width = own.shape[1]
    blocks, block, cols = behind.shape
    return pl.pallas_call(
        partial(mix_place_kernel, blocks),
        out_shape=shape((blocks, block, half_width + cols), BF),
        in_specs=[SMEM] + [VMEM] * 3,
        out_specs=VMEM,
        scratch_shapes=[pltpu.VMEM((2 * half_width, half_width), F32)],
        compiler_params=params(8),
        cost_estimate=FREE,
        name="mix_place",
    )(info, own, recv, behind)


def row_tiles(rows, step, body):
    lax.fori_loop(0, rows // step, lambda i, c: body(pl.ds(pl.multiple_of(i * step, step), step), c), 0)


def mean_of(value):
    return jnp.mean(value, -1, keepdims=True)


def first_norm_kernel(
    tokens, mixed, recv0, recv1, vectors, low0, low1, normed_out, inverse_out, recv, low
):
    gain, bias = vectors[0:1, :], vectors[1:2, :]
    half = recv0.shape[0]
    recv[:half, :] = recv0[...]
    recv[half:, :] = recv1[...]

    def body(at, carry):
        hidden = tokens[at, :].astype(F32) + mixed[at, :] + recv[at, :].astype(F32)
        centred = hidden - mean_of(hidden)
        inverse = lax.rsqrt(mean_of(centred * centred) + EPSILON)
        normed = centred * inverse
        normed_out[at, :] = normed
        inverse_out[at, :] = inverse
        low[at, :] = (normed * gain + bias).astype(BF)
        return carry

    row_tiles(tokens.shape[0], 128, body)
    low0[...] = low[:half, :]
    low1[...] = low[half:, :]


def first_norm(tokens, mixed, recvs, vectors):
    rows, width = tokens.shape
    return pl.pallas_call(
        first_norm_kernel,
        grid=(1,),
        out_shape=(shape((rows // 2, width), BF),) * 2
        + (pltpu.HBM((rows, width), F32), pltpu.HBM((rows, 1), F32)),
        in_specs=[pl.BlockSpec((rows, width), lambda i: (0, 0))] * 2
        + [pl.BlockSpec((rows // 2, width), lambda i: (0, 0))] * 2
        + [pl.BlockSpec(vectors.shape, lambda i: (0, 0))],
        scratch_shapes=[pltpu.VMEM((rows, width), BF)] * 2,
        out_specs=(pl.BlockSpec((rows // 2, width), lambda i: (0, 0)),) * 2
        + (
            pl.BlockSpec((rows, width), lambda i: (0, 0)),
            pl.BlockSpec((rows, 1), lambda i: (0, 0)),
        ),
        compiler_params=params(24),
        cost_estimate=FREE,
        name="first_norm",
    )(tokens, mixed, *recvs, vectors)


def second_norm_kernel(normed_one, mlp, recv, vectors, grad, result, grad_two, grad_low, sums):
    gain_one, bias_one = vectors[0:1, :], vectors[1:2, :]
    gain, bias = vectors[2:3, :], vectors[3:4, :]
    sums[...] = jnp.zeros_like(sums)

    def body(at, carry):
        hidden = normed_one[at, :] * gain_one + bias_one + mlp[at, :] + recv[at, :].astype(F32)
        centred = hidden - mean_of(hidden)
        inverse = lax.rsqrt(mean_of(centred * centred) + EPSILON)
        normed = centred * inverse
        result[at, :] = (normed * gain + bias).astype(BF)
        grad_y = grad[at, :].astype(F32)
        grad_n = grad_y * gain
        value = inverse * (grad_n - mean_of(grad_n) - normed * mean_of(grad_n * normed))
        grad_two[at, :] = value
        grad_low[at, :] = value.astype(BF)
        sums[2:3, :] += jnp.sum(grad_y * normed, 0, keepdims=True)
        sums[3:4, :] += jnp.sum(grad_y, 0, keepdims=True)
        return carry

    row_tiles(grad.shape[0], 128, body)


def second_norm(normed_one, mlp, recv, vectors, grad):
    rows, width = grad.shape
    return pl.pallas_call(
        second_norm_kernel,
        out_shape=(
            shape((rows, width), BF),
            shape((rows, width), F32),
            shape((rows, width), BF),
            shape((8, width), F32),
        ),
        in_specs=[VMEM] * 5,
        out_specs=(VMEM,) * 4,
        compiler_params=params(24),
        cost_estimate=FREE,
        name="second_norm",
    )(normed_one, mlp, recv, vectors, grad)


def first_back_kernel(
    grad_two, own, recv0, recv1, normed_one, inverse_one, vectors, late,
    grad_one, low0, low1, sums, grad_low, recv,
):
    gain = vectors[0:1, :]
    half = low0.shape[0]
    recv[:half, :] = recv0[...]
    recv[half:, :] = recv1[...]
    sums[...] = late[...]

    def body(at, carry):
        normed = normed_one[at, :]
        grad_y = grad_two[at, :] + own[at, :] + recv[at, :].astype(F32)
        grad_n = grad_y * gain
        value = inverse_one[at, :] * (grad_n - mean_of(grad_n) - normed * mean_of(grad_n * normed))
        grad_one[at, :] = value
        grad_low[at, :] = value.astype(BF)
        sums[0:1, :] += jnp.sum(grad_y * normed, 0, keepdims=True)
        sums[1:2, :] += jnp.sum(grad_y, 0, keepdims=True)
        return carry

    row_tiles(grad_two.shape[0], 128, body)
    low0[...] = grad_low[:half, :]
    low1[...] = grad_low[half:, :]


def first_back(grad_two, own, recvs, normed_one, inverse_one, vectors, late):
    rows, width = grad_two.shape
    return pl.pallas_call(
        first_back_kernel,
        out_shape=(shape((rows, width), F32),)
        + (shape((rows // 2, width), BF),) * 2
        + (shape((8, width), F32),),
        in_specs=[VMEM] * 8,
        out_specs=(VMEM,) * 4,
        scratch_shapes=[pltpu.VMEM((rows, width), BF)] * 2,
        compiler_params=params(24),
        cost_estimate=FREE,
        name="first_back",
    )(grad_two, own, *recvs, normed_one, inverse_one, vectors, late)


def after(value, *earlier):
    return lax.optimization_barrier((value,) + earlier)[0]


def shards(
    n_shard,
    tokens,
    segment_ids,
    qkv_weight,
    out_weight,
    up_weight,
    down_weight,
    first_gain,
    first_bias,
    second_gain,
    second_bias,
    out_grad,
):
    rows, width = tokens.shape
    half_width = width // 2
    quarter = width // 4
    ff_half = up_weight.shape[1] // 2
    block = qkv_weight.shape[0]
    shard = lax.axis_index("shard").astype(jnp.int32)
    seq = lax.axis_index("seq").astype(jnp.int32)
    xb, cb = seq // 2, seq % 2
    bits = [1 << b for b in range(n_shard.bit_length() - 1)]
    top = bits[-1]
    owner = (shard // top) % 2 == cb
    low_shard = shard % top
    place = jnp.stack([xb, cb, shard])

    def swap(value, mask):
        return lax.ppermute(value, "shard", [(i, i ^ mask) for i in range(n_shard)])

    def swap_core(value):
        return lax.ppermute(value, "seq", [(i, i ^ 1) for i in range(4)])

    def swap_x(value):
        return lax.ppermute(value, "seq", [(i, i ^ 2) for i in range(4)])

    def to_core(value, to_owner):
        pairs = []
        for sh in range(n_shard):
            for se in range(4):
                sends = (sh // top == se % 2) != to_owner
                pairs.append((sh * 4 + se, (sh ^ top) * 4 + se if sends else sh * 4 + (se ^ 1)))
        return lax.ppermute(value, ("shard", "seq"), pairs)

    def join(pieces):
        return jnp.concatenate(pieces) if len(pieces) > 1 else pieces[0]

    class Gather:
        def __init__(self, own_block, over):
            self.pieces, self.offsets, self.over = [own_block[None]], [[0]], list(over)

        def swap(self, value, rel, bit):
            got = swap(value, bit)
            self.pieces.append(got)
            self.offsets.append([r ^ bit for r in rel])
            return got

        def steps(self, count, *gate):
            for bit in [self.over.pop(0) for _ in range(count)]:
                held, rel = join(self.pieces), [r for o in self.offsets for r in o]
                self.pieces, self.offsets = [held], [rel]
                gate = (self.swap(after(held, *gate), rel, bit),)
            return gate[0]

        def part(self, index, *gate):
            return self.swap(after(self.pieces[index], *gate), self.offsets[index], self.over[0])

    def fold(value, got):
        return (value[: value.shape[0] // 2].astype(F32) + got.astype(F32)).astype(BF)

    def upper(value):
        return value[value.shape[0] // 2 :]

    def add_x(value):
        return (value.astype(F32) + swap_x(value).astype(F32)).astype(BF)

    def pick(value, flag, axis):
        return jnp.where(
            flag == 0,
            lax.index_in_dim(value, 0, axis, False),
            lax.index_in_dim(value, 1, axis, False),
        )

    def ordered(flag, own, other, axis):
        return jnp.where(
            flag == 0, jnp.concatenate([own, other], axis), jnp.concatenate([other, own], axis)
        )

    over_x = swap_x(tokens)
    over_core = swap_core(tokens)
    toks = [tokens, over_core, over_x]
    plan, ids_row = make_plan(segment_ids, place)

    own_a, own_b = prepare(
        place, qkv_weight, out_weight, (first_gain, first_bias, second_gain, second_bias)
    )
    up_half = lax.dynamic_slice_in_dim(up_weight, cb * ff_half, ff_half, 1)
    down_rows = down_weight.shape[0] // 2
    down_half = lax.dynamic_slice_in_dim(down_weight, xb * down_rows, down_rows, 0)
    middle = len(bits) - 2
    gather_a = Gather(own_a, bits[::-1])
    gather_b = Gather(own_b, bits[::-1])
    gather_up = Gather(up_half, bits[::-1])
    a1 = gather_a.steps(1)
    b1 = gather_b.steps(1, a1)
    a2 = gather_a.steps(middle, plan)
    a3 = gather_a.steps(1)
    b2 = gather_b.steps(middle, a2, up_half, down_half)
    toks.append(swap_core(after(over_x, b2)))
    d1 = to_core(after(down_half, b1), False)
    b2 = after(b2, a3, d1)
    gather_b.pieces[1] = b2
    b3 = gather_b.steps(1)
    part_a = assemble(gather_a.pieces, gather_a.offsets, shard)
    vectors = vectors_of(part_a)

    saved, own_ctx, sends = [], [], []

    def head(j, weight, *gate):
        ctx_own, ctx_send, ctx_full, lse = attend(
            plan, toks, weight, after(ids_row, *gate)
        )
        own_ctx.append(ctx_own)
        sends.append(ctx_send)
        saved.append((ctx_full, lse))
        return ctx_own

    gather_down = Gather(jnp.where(owner, down_half, d1), bits[-2::-1])
    d2 = gather_down.steps(middle)
    u1 = gather_up.steps(1, gather_down.pieces[0])
    ctx = head(0, part_a[:, :TRIO], b2, vectors, gather_down.pieces[0])
    b3, d2, u1 = after(b3, ctx), after(d2, ctx), after(u1, ctx)
    gather_b.pieces[1], gather_down.pieces[1], gather_up.pieces[1] = b3, d2, u1
    u2 = gather_up.steps(middle)
    gather_down.pieces[1] = after(d2, gather_up.pieces[0])
    d3 = gather_down.steps(1)
    part_b = assemble(gather_b.pieces, gather_b.offsets, shard)
    far_a = swap_x(after(part_a, ctx))
    far_b = swap_x(part_b[:, : 2 * TRIO])
    ctx = head(1, part_b[:, :TRIO], gather_down.pieces[0], gather_up.pieces[0])
    d3, u2 = after(d3, ctx), after(u2, ctx)
    gather_down.pieces[1], gather_up.pieces[1] = d3, u2
    held_up = join(gather_up.pieces)
    gather_up.offsets = [[r for o in gather_up.offsets for r in o]]
    gather_up.pieces = [held_up]
    u3 = gather_up.part(0)
    held = join(gather_down.pieces)
    ctx = head(2, part_b[:, TRIO : 2 * TRIO], held_up, held)
    sends[2], held, far_a, far_b = lax.optimization_barrier((sends[2], held, far_a, far_b))
    others = [swap_x(value) for value in sends]
    rel = [2 * r for o in gather_down.offsets for r in o]
    held_far = swap_x(held)
    head_weights = [part_a[:, :TRIO], part_b[:, :TRIO], part_b[:, TRIO : 2 * TRIO]]
    far_weights = [far_a, far_b[:, :TRIO], far_b[:, TRIO:]]
    mixer = part_b[:, 2 * TRIO :].reshape(2, half_width, half_width)
    mixer = ordered(cb, pick(mixer, cb, 0), swap_core(pick(mixer, 1 - cb, 0)), 1)
    mixer = jnp.where(xb == 0, mixer, jnp.concatenate([mixer[quarter:], mixer[:quarter]]))
    context = jnp.concatenate(own_ctx + others)

    mixed = after(dot(context, mixer, 0, 0), u3)
    recv0, recv1 = [
        swap_core(mixed[at : at + rows // 2].astype(BF)) for at in (rows, rows + rows // 2)
    ]
    low0, low1, normed_one, inverse_one = first_norm(
        tokens, mixed, [recv0, recv1], vectors
    )
    widen = assemble(gather_up.pieces, gather_up.offsets, shard)
    act_low, act_t, slope, low_t = feed_up([low0, low1, swap_core(low0), swap_core(low1)], widen)
    held_far = after(held_far, act_low)
    narrow = assemble([held, held_far], [rel, [r + 1 for r in rel]], low_shard * 2 + xb)
    mlp_own, mlp_send = feed_down(act_low, narrow)
    result, grad_two, grad_mlp, late = second_norm(
        normed_one, mlp_own, swap_core(mlp_send), vectors, out_grad
    )

    grad_mlp = [grad_mlp, swap_core(grad_mlp)]
    narrow_grad = weight_grad(low_shard, act_t, grad_mlp, n_shard // 2, False)
    n1 = swap(upper(narrow_grad), bits[-2])
    first_own, send0, send1, grad_pre = feed_back(
        after(grad_mlp[0], narrow_grad), grad_mlp[1], slope, widen, narrow
    )
    widen_grad = weight_grad(shard, low_t, [grad_pre], n_shard)
    w1 = swap(upper(widen_grad), bits[0])
    recv0, recv1, _ = lax.optimization_barrier((swap_core(send0), swap_core(send1), widen_grad))
    grad_one, attn0, attn1, sums = first_back(
        grad_two, first_own, [recv0, recv1], normed_one, inverse_one, vectors, late
    )
    attn = [attn0, attn1, swap_core(attn0), swap_core(attn1)]
    gs = mix_back(mixer, attn)
    g_recv = [swap_x(g) for g in gs[3:]]
    mixer_own, mixer_send = mix_grad(place, after(context, *gs), attn)
    mixer_recv = swap_core(mixer_send)

    def head_back(j, before, *gate):
        return attend_back(
            plan, place, toks, head_weights[j], after(ids_row, *gate),
            gs[j], g_recv[j], *saved[j],
            sums if j == 2 else None, before, n_shard,
        )

    keeps, sends = [None] * 3, [None] * 3
    keeps[0], sends[0], part = head_back(0, None, mixer_own)
    fars = [swap_x(sends[0])]
    narrow_grad = fold(narrow_grad, after(n1, part, *g_recv[1:]))
    for bit in bits[-3:0:-1]:
        narrow_grad = fold(narrow_grad, swap(upper(narrow_grad), bit))
    n2 = swap(upper(narrow_grad), bits[0])
    early = mix_place(place, mixer_own, mixer_recv, after(part, narrow_grad))
    widen_grad = fold(widen_grad, after(w1, early))
    for bit in bits[1:-2]:
        widen_grad = fold(widen_grad, swap(upper(widen_grad), bit))
    w2 = swap(upper(widen_grad), bits[-2])
    keeps[1], sends[1], part = head_back(1, None, early, widen_grad)
    fars.append(swap_x(sends[1]))
    narrow_grad = fold(narrow_grad, after(n2, part))[0]
    n3 = to_core(narrow_grad, True)
    widen_grad = fold(widen_grad, after(w2, narrow_grad, fars[0]))
    w3 = swap(upper(widen_grad), bits[-1])
    early = after(early, narrow_grad, widen_grad)
    e1 = swap(upper(early), bits[0])
    keeps[2], sends[2], late = head_back(2, part, narrow_grad, widen_grad)
    fars.append(swap_x(sends[2]))
    widen_grad = fold(widen_grad, after(w3, late, fars[1]))[0]
    early = fold(early, after(e1, widen_grad))
    e2 = swap(upper(early), bits[1])
    late = after(late, widen_grad, early)
    l1 = swap(upper(late), bits[0])
    w4 = swap_x(widen_grad)
    late = fold(late, after(l1, fars[2]))
    l2 = swap(upper(late), bits[1])
    early = fold(early, after(e2, late))
    for bit in bits[2:-1]:
        early = fold(early, swap(upper(early), bit))
    e3 = swap(upper(early), bits[-1])
    fars[2] = after(fars[2], late)
    back_own, back_core = input_back(keeps + fars, head_weights + far_weights, rows)
    back_near = swap_core(back_core)
    early = fold(early, after(e3, back_core))[0]
    late = fold(late, after(l2, w4, early))
    for bit in bits[2:-1]:
        late = fold(late, swap(upper(late), bit))
    l3 = swap(upper(late), bits[-1])
    narrow_grad = (narrow_grad.astype(F32) + after(n3, late).astype(F32)).astype(BF)
    halves = narrow_grad.reshape(2, -1, width)
    narrow_half = swap_core(pick(halves, 1 - cb, 0))
    narrow_half = jnp.where(owner, pick(halves, cb, 0), narrow_half)
    n4 = swap_x(narrow_half)
    widen_grad = (widen_grad.astype(F32) + after(w4, late).astype(F32)).astype(BF)
    widen_other = swap_core(widen_grad)
    input_grad = grad_one + back_own + after(back_near, late).astype(F32)
    late = fold(late, after(l3, narrow_half))[0]
    mine = jnp.concatenate([early, late], 1)
    theirs = swap_x(mine)
    narrow_half = (narrow_half.astype(F32) + after(n4, mine).astype(F32)).astype(BF)
    narrow_other = swap_core(narrow_half)
    widen_grad = ordered(cb, widen_grad, widen_other, 1)
    narrow_grad = ordered(cb, narrow_half, narrow_other, 0)
    narrow_grad, widen_grad = narrow_grad.astype(F32), widen_grad.astype(F32)
    theirs = after(theirs, narrow_grad, widen_grad, input_grad)
    mixer_grad = (mine[:, :half_width].astype(F32) + theirs[:, :half_width].astype(F32)).astype(BF)
    chip = jnp.concatenate([mixer_grad, mine[:, half_width:], theirs[:, half_width:]], 1)
    other = swap_core(chip)
    qkv_grad, mixer_grad, sums = place_qkv(place, chip, other, half_width, width)
    return (
        result,
        input_grad,
        qkv_grad,
        mixer_grad,
        widen_grad,
        narrow_grad,
        sums[:, 0],
        sums[:, 1],
        sums[:, 2],
        sums[:, 3],
    )


def solution(mesh):
    placed = (
        P(("shard", "seq"), None),
        P("shard", None),
        P("shard", None),
        P("shard", None),
        P("shard", None),
        P("shard", None),
        P("shard"),
        P("shard"),
        P("shard"),
        P("shard"),
        P(("shard", "seq"), None),
    )
    return jax.shard_map(
        partial(shards, mesh.shape["shard"]),
        mesh=mesh,
        in_specs=placed,
        out_specs=(
            P(("shard", "seq"), None),
            P(("shard", "seq"), None),
            P("shard", None),
            P("shard", None),
            P("shard", None),
            P("shard", None),
            P("shard"),
            P("shard"),
            P("shard"),
            P("shard"),
        ),
        check_vma=False,
    )
```
